32 devices in a mesh: parts: 1, tile: 16 (over z, y, core), face: 2 (over x), sub: 1.
Axes of the slice: x: 2, y: 2, z: 4, core: 2. Of those that a mesh axis runs over, the one named last changes fastest.
Arguments:
- fields: bfloat16 [96, 4, 32, 96], P('sub', 'face', 'tile', 'parts'), may hold values from -6 to 6
- upstream: bfloat16 [96, 4, 32, 96], P('sub', 'face', 'tile', 'parts'), may hold values from -6 to 6
- kernel_one: bfloat16 [3, 3, 96, 96], replicated, may hold values from -0.21875 to 0.21875
- kernel_two: bfloat16 [3, 3, 96, 96], replicated, may hold values from -0.21875 to 0.21875
Outputs:
- result: bfloat16 [96, 4, 32, 96], P('sub', 'face', 'tile', 'parts')
- fields_grad: bfloat16 [96, 4, 32, 96], P('sub', 'face', 'tile', 'parts')
- kernel_one_grad: float32 [3, 3, 96, 96], P('parts', None, None, 'sub')
- kernel_two_grad: float32 [3, 3, 96, 96], P('parts', None, None, 'sub')
The draws below stay inside these ranges and needn't reach their ends.
All inputs are finite; a program needn't handle non-finite values.
Results may differ from the reference program's by a relative error of at most 0.0049.
Values may be sent and summed in bfloat16 or wider, within the bound.
A program may use at most 128 MiB of HBM per device.

```python
import jax
import jax.numpy as jnp
from jax import lax

C = 96
SIDE = 32


def level_of(key, shape, shards, smallest, largest):
    def one(dim, shards_of):
        steps = jax.random.uniform(jax.random.fold_in(jax.random.fold_in(key, 6), dim), (shards_of,), jnp.float32, smallest / len(shards), largest / len(shards))
        return jnp.repeat(jnp.exp(steps), shape[dim] // shards_of).reshape((-1,) + (1,) * (len(shape) - dim - 1))

    gain = one(*shards[0])
    for cut in shards[1:]:
        gain = gain * one(*cut)
    return gain


def scatter_about(own_key, dims, scale, reach, shards=(), kind=jnp.bfloat16):
    entries = jax.random.normal(own_key, dims, jnp.float32) * scale
    if len(shards) > 0:
        entries = level_of(own_key, dims, shards, -0.22, 0.18) * entries
    return jnp.clip(entries, min=-reach, max=reach).astype(kind)


def setup_inputs(seed: int = 0, part: int = 0) -> dict:
    key_list = jax.random.split(jax.random.key(seed), 5)
    own_keys = jax.random.split(jax.random.fold_in(key_list[4], part), 5)
    fields = scatter_about(own_keys[0], (C, 4, SIDE, 3 * SIDE), 1.0, 6.0, ((1, 2), (2, 16)))
    upstream = scatter_about(own_keys[1], (C, 4, SIDE, 3 * SIDE), 1.0, 6.0, ((1, 2), (2, 16)))
    kernel_one = scatter_about(key_list[2], (3, 3, C, C), (9 * C) ** -0.5, 0.21875)
    kernel_two = scatter_about(key_list[3], (3, 3, C, C), (9 * C) ** -0.5, 0.21875)
    return {"fields": fields, "upstream": upstream, "kernel_one": kernel_one, "kernel_two": kernel_two}


def activate(values):
    return jax.nn.gelu(values, approximate=True)

def sphere_pad(field):
    side = field.shape[2]
    before = jnp.roll(field, 1, axis=1)
    after = jnp.roll(field, -1, axis=1)
    top_line = after[:, :, 0, 0:side]
    bottom_line = before[:, :, side - 1, 2 * side:3 * side]
    left_line = jnp.concatenate([before[:, :, 0:side, 0], before[:, :, side - 1, 0:2 * side]], axis=2)
    right_line = jnp.concatenate([after[:, :, 0, side:3 * side], after[:, :, 0:side, 3 * side - 1]], axis=2)
    corner = jnp.zeros(field.shape[0:2] + (1,), field.dtype)
    top_row = jnp.concatenate([corner, top_line, corner], axis=2)
    bottom_row = jnp.concatenate([corner, bottom_line, corner], axis=2)
    middle = jnp.concatenate([left_line[:, :, None, :], field, right_line[:, :, None, :]], axis=2)
    return jnp.concatenate([top_row[:, :, :, None], middle, bottom_row[:, :, :, None]], axis=3)

def sphere_fold(gradient):
    side = gradient.shape[2] - 2
    height = 3 * side
    interior = gradient[:, :, 1:side + 1, 1:height + 1]
    grad_top = gradient[:, :, 1:side + 1, 0]
    grad_bottom = gradient[:, :, 1:side + 1, height + 1]
    grad_left = gradient[:, :, 0, 1:height + 1]
    grad_right = gradient[:, :, side + 1, 1:height + 1]
    to_after = jnp.zeros_like(interior)
    to_after = to_after.at[:, :, 0, 0:side].add(grad_top)
    to_after = to_after.at[:, :, 0, side:height].add(grad_right[:, :, 0:2 * side])
    to_after = to_after.at[:, :, 0:side, height - 1].add(grad_right[:, :, 2 * side:height])
    to_before = jnp.zeros_like(interior)
    to_before = to_before.at[:, :, side - 1, 2 * side:height].add(grad_bottom)
    to_before = to_before.at[:, :, 0:side, 0].add(grad_left[:, :, 0:side])
    to_before = to_before.at[:, :, side - 1, 0:2 * side].add(grad_left[:, :, side:height])
    return interior + jnp.roll(to_after, 1, axis=1) + jnp.roll(to_before, -1, axis=1)

def convolve(padded, kernel):
    return lax.conv_general_dilated(padded.astype(jnp.float32), kernel.astype(jnp.float32), (1, 1), 'VALID', dimension_numbers=('CNHW', 'HWIO', 'CNHW'), precision=lax.Precision.HIGHEST, preferred_element_type=jnp.float32)

def spread(cotangent, kernel):
    flipped = jnp.flip(kernel, (0, 1)).transpose(0, 1, 3, 2)
    return lax.conv_general_dilated(cotangent.astype(jnp.float32), flipped.astype(jnp.float32), (1, 1), ((2, 2), (2, 2)), dimension_numbers=('CNHW', 'HWIO', 'CNHW'), precision=lax.Precision.HIGHEST, preferred_element_type=jnp.float32)

def weight_terms(padded, cotangent):
    columns = cotangent.shape[2]
    height = cotangent.shape[3]
    flat_cot = cotangent.astype(jnp.float32).reshape(cotangent.shape[0], -1)
    tap_rows = []
    for col_tap in range(3):
        row_list = []
        for row_tap in range(3):
            tap_cells = padded[:, :, col_tap:col_tap + columns, row_tap:row_tap + height]
            tap_cells = tap_cells.astype(jnp.float32).reshape(padded.shape[0], -1)
            row_list.append(lax.dot_general(tap_cells, flat_cot, (((1,), (1,)), ((), ())), precision=lax.Precision.HIGHEST, preferred_element_type=jnp.float32))
        tap_rows.append(jnp.stack(row_list))
    return jnp.stack(tap_rows)

def reference(fields, upstream, kernel_one, kernel_two):
    face_side = fields.shape[2]
    cell_scale = 1.0 / (face_side * jnp.sqrt(jnp.float32(12.0)))
    padded_one = sphere_pad(fields)
    pre_one = convolve(padded_one, kernel_one)
    hidden = activate(pre_one).astype(jnp.bfloat16)
    padded_two = sphere_pad(hidden)
    result = convolve(padded_two, kernel_two).astype(jnp.bfloat16)
    hidden_grad = sphere_fold(spread(upstream, kernel_two))
    unused, pullback = jax.vjp(activate, pre_one)
    pre_grad = pullback(hidden_grad)[0].astype(jnp.bfloat16)
    fields_grad = sphere_fold(spread(pre_grad, kernel_one)).astype(jnp.bfloat16)
    kernel_one_grad = weight_terms(padded_one, pre_grad) * cell_scale
    kernel_two_grad = weight_terms(padded_two, upstream) * cell_scale
    return (result, fields_grad, kernel_one_grad, kernel_two_grad)
```

```python
import functools

import jax
import jax.numpy as jnp
from jax import lax
from jax.experimental import pallas as pl
from jax.experimental.pallas import tpu as pltpu
from jax.sharding import PartitionSpec as P

MESH = pl.DeviceIdType.MESH
F32 = jnp.float32
BF16 = jnp.bfloat16


def gelu_parts(v):
    root = 0.7978845608028654
    cube = 0.044715 * (v * v * v)
    th = jnp.tanh(root * (v + cube))
    value = v * (0.5 * (1.0 + th))
    slope = 0.5 * (1.0 + th) + 0.5 * v * (1.0 - th * th) * root * (1.0 + 0.134145 * (v * v))
    return value, slope


def product(a, b, da, db):
    return lax.dot_general(a, b, (((da,), (db,)), ((), ())), preferred_element_type=F32)


def body(n_t, n_f, scale, groups, fields_h, upstream_h, k1_h, k2_h, res_o, fg_o, w1_o, w2_o,
         raw, x, k1, k2, y, rows, lh, rh, ap, bm, aps, tr, dr, tl, dl, al, pad, xb, xf1, xf2,
         acc, sbuf, rlow, rfull, obuf,
         col_s, col_r, line_s, a_r, b_r, t_s, d_s, row_r, w_s, w_r, in_s):
    _, G, J, H, C = x.shape
    S = H // 3
    E = J + 2
    t = lax.axis_index("tile")
    f = lax.axis_index("face")
    fn = lax.rem(f + 1, n_f)
    fp = lax.rem(f + n_f - 1, n_f)
    first = t == 0
    last = t == n_t - 1
    inner_left = jnp.logical_not(first)
    inner_right = jnp.logical_not(last)

    def where_to(tile, face):
        return {"tile": tile, "face": face}

    def remote(src, dst, s, r, dev):
        return pltpu.make_async_remote_copy(
            src_ref=src, dst_ref=dst, send_sem=s, recv_sem=r, device_id=dev, device_id_type=MESH)

    def settle(ref, sem):
        pltpu.make_async_copy(ref, ref, sem).wait()

    def copies(p, src):
        c0, cl = src.at[:, :, 0], src.at[:, :, J - 1]
        right = lambda: remote(cl, lh.at[p], col_s.at[p, 0], col_r.at[p, 0], where_to(jnp.minimum(t + 1, n_t - 1), f))
        left = lambda: remote(c0, rh.at[p], col_s.at[p, 1], col_r.at[p, 1], where_to(jnp.maximum(t - 1, 0), f))
        seam = []
        if G > 1:
            seam.append((first, lambda: remote(src.at[:, 1:G, 0], rh.at[p, :, 0:G - 1], col_s.at[p, 2], col_r.at[p, 2], where_to(n_t - 1, f))))
            seam.append((last, lambda: remote(src.at[:, 0:G - 1, J - 1], lh.at[p, :, 1:G], col_s.at[p, 2], col_r.at[p, 2], where_to(0, f))))
        seam.append((first, lambda: remote(src.at[:, 0:1, 0], rh.at[p, :, G - 1:G], col_s.at[p, 3], col_r.at[p, 3], where_to(n_t - 1, fp))))
        seam.append((last, lambda: remote(src.at[:, G - 1:G, J - 1], lh.at[p, :, 0:1], col_s.at[p, 3], col_r.at[p, 3], where_to(0, fn))))
        a_own = lambda d: remote(aps.at[p, d, :, 1:G], ap.at[p, :, 0:G - 1], line_s.at[p, 0], a_r.at[p, 0], where_to(d, f))
        a_oth = lambda d: remote(aps.at[p, d, :, 0:1], ap.at[p, :, G - 1:G], line_s.at[p, 1], a_r.at[p, 1], where_to(d, fp))
        b_own = lambda d: remote(aps.at[p, d, :, 0:G - 1], bm.at[p, :, 1:G], line_s.at[p, 0], b_r.at[p, 0], where_to(d, f))
        b_oth = lambda d: remote(aps.at[p, d, :, G - 1:G], bm.at[p, :, 0:1], line_s.at[p, 1], b_r.at[p, 1], where_to(d, fn))
        t_own = lambda d: remote(rows.at[p, 0, :, 0:G - 1], tr.at[p, d, :, 1:G], t_s.at[p, 0], row_r.at[p, 0], where_to(0, f))
        t_oth = lambda d: remote(rows.at[p, 0, :, G - 1:G], tr.at[p, d, :, 0:1], t_s.at[p, 1], row_r.at[p, 1], where_to(0, fn))
        d_own = lambda d: remote(rows.at[p, 1, :, 1:G], dr.at[p, d, :, 0:G - 1], d_s.at[p, 0], row_r.at[p, 0], where_to(n_t - 1, f))
        d_oth = lambda d: remote(rows.at[p, 1, :, 0:1], dr.at[p, d, :, G - 1:G], d_s.at[p, 1], row_r.at[p, 1], where_to(n_t - 1, fp))
        return right, left, seam, a_own, a_oth, b_own, b_oth, t_own, t_oth, d_own, d_oth

    def stage(p, kind, src):
        for q in range(G):
            for j in range(J):
                rows[p, 0, kind, q, j:j + 1, :] = src[kind, q, j, 0:16].astype(F32)[0:1]
                rows[p, 1, kind, q, j:j + 1, :] = src[kind, q, j, H - 16:H].astype(F32)[15:16]
        more = 16 * kind

        @pl.when(first)
        def _():
            for q in range(G):
                al[kind, q, 16:16 + S + more, :] = src[kind, q, 0, 0:S + more].astype(F32)
            for d in range(n_t):
                aps[p, d, kind] = al[kind, :, 15 + d * J:15 + d * J + E, :]

        @pl.when(last)
        def _():
            for q in range(G):
                al[kind, q, 16 - more:16 + S, :] = src[kind, q, J - 1, 2 * S - more:H].astype(F32)
            for d in range(n_t):
                aps[p, d, kind] = al[kind, :, 15 + d * J:15 + d * J + E, :]

    def start(p, src):
        right, left, seam, a_own, a_oth, b_own, b_oth, t_own, t_oth, d_own, d_oth = copies(p, src)
        t_oth(t).start()
        d_oth(t).start()
        if G > 1:
            @pl.when(inner_left)
            def _():
                t_own(t).start()

            @pl.when(inner_right)
            def _():
                d_own(t).start()
        for cond, make in seam:
            @pl.when(cond)
            def _(make=make):
                make().start()

        @pl.when(first)
        def _():
            @pl.loop(0, n_t)
            def _(d):
                a_oth(n_t - 1 - d).start()
            if G > 1:
                @pl.loop(1, n_t)
                def _(d):
                    a_own(n_t - d).start()
                ap[p, :, 0:G - 1] = aps[p, 0, :, 1:G]
                tr[p, 0, :, 1:G] = rows[p, 0, :, 0:G - 1]

        @pl.when(last)
        def _():
            @pl.loop(0, n_t)
            def _(d):
                b_oth(d).start()
            if G > 1:
                @pl.loop(0, n_t - 1)
                def _(d):
                    b_own(d).start()
                bm[p, :, 1:G] = aps[p, n_t - 1, :, 0:G - 1]
                dr[p, n_t - 1, :, 0:G - 1] = rows[p, 1, :, 1:G]

        @pl.when(inner_right)
        def _():
            right().start()

        @pl.when(inner_left)
        def _():
            left().start()

    def await_arrivals(p, src):
        right, left, seam, a_own, a_oth, b_own, b_oth, t_own, t_oth, d_own, d_oth = copies(p, src)

        @pl.when(inner_left)
        def _():
            right().wait_recv()
            if G > 1:
                a_own(0).wait_recv()

        @pl.when(inner_right)
        def _():
            left().wait_recv()
            if G > 1:
                b_own(0).wait_recv()

        for cond, make in seam:
            @pl.when(last if cond is first else first)
            def _(make=make):
                make().wait_recv()

        a_oth(0).wait_recv()
        b_oth(0).wait_recv()

        @pl.when(first)
        def _():
            if G > 1:
                settle(tr.at[p, 1:n_t, :, 1:G], row_r.at[p, 0])
            settle(tr.at[p, :, :, 0:1], row_r.at[p, 1])
            for d in range(n_t):
                tl[:, :, 8 + d * J:8 + (d + 1) * J, :] = tr[p, d]

        @pl.when(last)
        def _():
            if G > 1:
                settle(dr.at[p, 0:n_t - 1, :, 0:G - 1], row_r.at[p, 0])
            settle(dr.at[p, :, :, G - 1:G], row_r.at[p, 1])
            for d in range(n_t):
                dl[:, :, 8 + d * J:8 + (d + 1) * J, :] = dr[p, d]

    def await_sends(p, src):
        right, left, seam, a_own, a_oth, b_own, b_oth, t_own, t_oth, d_own, d_oth = copies(p, src)

        @pl.when(inner_right)
        def _():
            right().wait_send()
            if G > 1:
                d_own(t).wait_send()

        @pl.when(inner_left)
        def _():
            left().wait_send()
            if G > 1:
                t_own(t).wait_send()

        for cond, make in seam:
            @pl.when(cond)
            def _(make=make):
                make().wait_send()
        t_oth(t).wait_send()
        d_oth(t).wait_send()

        @pl.when(jnp.logical_or(first, last))
        def _():
            if G > 1:
                settle(aps.at[p, 1:n_t, :, 1:G], line_s.at[p, 0])
            settle(aps.at[p, :, :, 0:1], line_s.at[p, 1])

    def fill_columns(src):
        for q in range(G):
            for j in range(J):
                pad[q, 1 + j, 8:8 + H, :] = src[q, j].astype(F32)

    def forward_taps(p, src, out):
        fill_columns(src)
        for q in range(G):
            @pl.when(inner_left)
            def _():
                pad[q, 0, 8:8 + H, :] = lh[p, 0, q].astype(F32)

            @pl.when(first)
            def _():
                pad[q, 0, 8:8 + S, :] = tl[0, q, 8:8 + S, :]
                pad[q, 0, 8 + S:8 + H, :] = lh[p, 0, q, 0:2 * S].astype(F32)

            @pl.when(inner_right)
            def _():
                pad[q, J + 1, 8:8 + H, :] = rh[p, 0, q].astype(F32)

            @pl.when(last)
            def _():
                pad[q, J + 1, 8:8 + 2 * S, :] = rh[p, 0, q, S:H].astype(F32)
                pad[q, J + 1, 8 + 2 * S:8 + H, :] = dl[0, q, 8:8 + S, :]
            for j in range(E):
                pad[q, j, 7:8, :] = ap[p, 0, q, j:j + 1]
                pad[q, j, 8 + H:9 + H, :] = bm[p, 0, q, j:j + 1]
        for a in range(3):
            for b in range(3):
                for q in range(G):
                    for j in range(J):
                        m = (q * J + j) * H
                        out[3 * a + b, m:m + H, :] = pad[q, j + a, 7 + b:7 + b + H, :].astype(BF16)

    def backward_taps(p, src, out):
        fill_columns(src)
        for q in range(G):
            @pl.when(inner_left)
            def _():
                pad[q, 0, 8:8 + H, :] = lh[p, 1, q].astype(F32)

            @pl.when(first)
            def _():
                pad[q, 0, :, :] = jnp.zeros((H + 16, C), F32)

            @pl.when(inner_right)
            def _():
                pad[q, J + 1, 8:8 + H, :] = rh[p, 1, q].astype(F32)

            @pl.when(last)
            def _():
                pad[q, J + 1, :, :] = jnp.zeros((H + 16, C), F32)
            for j in range(E):
                pad[q, j, 7:8, :] = jnp.zeros((1, C), F32)
                pad[q, j, 8 + H:9 + H, :] = jnp.zeros((1, C), F32)
        for a in range(3):
            for b in range(3):
                for q in range(G):
                    for j in range(J):
                        m = (q * J + j) * H
                        out[3 * a + b, m:m + H, :] = pad[q, j - a + 2, 9 - b:9 - b + H, :]
        for q in range(G):
            top = ap[p, 1, q]
            low = bm[p, 1, q]
            for b in range(3):
                for j in range(J):
                    m = (q * J + j) * H
                    out[b, m:m + 1, :] += top[j + 2 - b:j + 3 - b]
                    out[6 + b, m + H - 1:m + H, :] += low[j + 2 - b:j + 3 - b]

        @pl.when(last)
        def _():
            for q in range(G):
                m = (q * J + J - 1) * H
                pad[q, J + 1, 8:8 + H, :] = rh[p, 1, q].astype(F32)
                for e in range(3):
                    out[e, m:m + 2 * S, :] += pad[q, J + 1, 8 + S + 1 - e:8 + H + 1 - e, :]
                    out[3 * e + 2, m + 2 * S:m + H, :] += dl[1, q, 9 - e:9 - e + S, :]

        @pl.when(first)
        def _():
            for q in range(G):
                m = q * J * H
                pad[q, 0, 8:8 + H, :] = lh[p, 1, q].astype(F32)
                for e in range(3):
                    out[3 * e, m:m + S, :] += tl[1, q, 9 - e:9 - e + S, :]
                    out[6 + e, m + S:m + H, :] += pad[q, 0, 9 - e:9 - e + 2 * S, :]

    def apply(taps, k, dim):
        total = product(taps[0].astype(BF16), k[0, 0], 1, dim)
        for n in range(1, 9):
            total = total + product(taps[n].astype(BF16), k[n // 3, n % 3], 1, dim)
        return total

    def flat(src):
        return jnp.concatenate([src[q, j] for q in range(G) for j in range(J)], axis=0)

    def unflat(value, dst):
        for q in range(G):
            for j in range(J):
                m = (q * J + j) * H
                dst[q, j] = value[m:m + H]

    def channel_major(value, dst):
        for q in range(G):
            for j in range(J):
                m = (q * J + j) * H
                dst[:, q, j, :] = value[m:m + H].T.astype(BF16)

    per = C // 16
    blocks = acc.shape[1]

    def weight_terms(taps, cot, w):
        for n in range(9):
            term = product(taps[n], cot, 0, 0) * scale
            acc[w, n * per:(n + 1) * per] = term.reshape(per, 16, C)

    class Sum:
        def __init__(self, w, out):
            self.out, self.at, self.over = out, 0, False
            self.w, self.lo, self.length, self.done = w, 0, blocks, []
            self.used = [0, 0]
            self.sem = 0

        def members(self, bits):
            mine, place = [], 0
            for axis, s in bits:
                mine.append(lax.rem((t if axis == "tile" else f) // s, 2))
            found = []
            for k in range(1, 2 ** len(bits)):
                tile, face, digit = t, f, 0
                for pos, (axis, s) in enumerate(bits):
                    bit = mine[pos]
                    if (k >> pos) & 1:
                        if axis == "tile":
                            tile = tile + (1 - 2 * bit) * s
                        else:
                            face = face + (1 - 2 * bit) * s
                        bit = 1 - bit
                    digit = digit + bit * (1 << pos)
                found.append((digit, where_to(tile, face)))
            own = 0
            for pos, bit in enumerate(mine):
                own = own + bit * (1 << pos)
            return own, found

        def begin(self, n):
            bits, full = groups[n]
            own, found = self.members(bits)
            part = self.length // (len(found) + 1)
            w = self.w
            inbox = rfull if full else rlow
            at = self.used[full]
            self.flying = (inbox, at, part, len(found))
            for digit, dev in found:
                give = self.lo + digit * part
                if full:
                    out = acc.at[w, pl.ds(give, part)]
                else:
                    sbuf[w, pl.ds(give, part)] = acc[w, pl.ds(give, part)].astype(BF16)
                    out = sbuf.at[w, pl.ds(give, part)]
                at = self.used[full]
                self.used[full] += part
                remote(out, inbox.at[w, at:at + part], w_s.at[w, self.sem], w_r.at[w, self.sem], dev).start()
            keep = self.lo + own * part
            self.done.append((keep, part, found))
            self.lo, self.length = keep, part

        def end(self):
            inbox, at, part, count = self.flying
            whole = inbox.at[self.w, at:at + count * part]
            settle(whole, w_s.at[self.w, self.sem])
            settle(whole, w_r.at[self.w, self.sem])
            self.sem += 1
            total = acc[self.w, pl.ds(self.lo, self.length)]
            for n in range(count):
                total = total + inbox[self.w, at + n * part:at + (n + 1) * part].astype(F32)
            acc[self.w, pl.ds(self.lo, self.length)] = total

        def round(self):
            obuf[self.w, pl.ds(self.lo, self.length)] = acc[self.w, pl.ds(self.lo, self.length)].astype(BF16)

        def give(self, n):
            keep, part, found = self.done[n]
            self.flying = (part, len(found))
            for digit, dev in found:
                remote(obuf.at[self.w, pl.ds(keep, part)], obuf.at[self.w, pl.ds(keep, part)],
                       w_s.at[self.w, self.sem], w_r.at[self.w, self.sem], dev).start()

        def given(self):
            part, count = self.flying
            whole = obuf.at[self.w, 0:count * part]
            settle(whole, w_s.at[self.w, self.sem])
            settle(whole, w_r.at[self.w, self.sem])
            self.sem += 1

        def advance(self):
            at, count = self.at, len(groups)
            self.at += 1
            if at < count:
                if at > 0:
                    self.end()
                self.begin(at)
            elif at == count:
                self.end()
                self.round()
                self.give(count - 1)
            elif at < 2 * count:
                self.given()
                self.give(2 * count - 1 - at)
            elif at == 2 * count:
                self.given()
                for n in range(9):
                    self.out[n // 3, n % 3] = obuf[self.w, n * per:(n + 1) * per].reshape(C, C).astype(F32)
                self.over = True

    barrier = pltpu.get_barrier_semaphore()
    loads = [pltpu.make_async_copy(src, dst, in_s.at[n]) for n, (src, dst) in enumerate(
        ((fields_h, raw.at[0]), (upstream_h, raw.at[1]), (k1_h, k1), (k2_h, k2)))]
    for load in loads:
        load.start()

    @pl.loop(0, n_f)
    def _(df):
        @pl.loop(0, n_t)
        def _(dt):
            @pl.when(jnp.logical_or(df != f, dt != t))
            def _():
                pl.semaphore_signal(barrier, inc=1, device_id=where_to(dt, df), device_id_type=MESH)
    hidden, pre_grad = y.at[0], y.at[1]
    al[...] = jnp.zeros_like(al)
    tl[...] = jnp.zeros_like(tl)
    dl[...] = jnp.zeros_like(dl)
    for kind in range(2):
        loads[kind].wait()
        for q in range(G):
            for j in range(J):
                x[kind, q, j] = raw[kind, :, q, j, :].astype(F32).T.astype(BF16)
        stage(0, kind, x)
    if blocks > 9 * per:
        for w in range(2):
            acc[w, 9 * per:blocks] = jnp.zeros((blocks - 9 * per, 16, C), F32)
    pl.semaphore_wait(barrier, n_t * n_f - 1)

    start(0, x)
    loads[2].wait()
    loads[3].wait()
    await_arrivals(0, x)
    forward_taps(0, x.at[0], xf1)
    value, slope = gelu_parts(apply(xf1, k1, 0))
    unflat(value.astype(BF16), hidden)
    stage(1, 0, y)
    backward_taps(0, x.at[1], xb)
    cot = (apply(xb, k2, 1) * slope).astype(BF16)
    unflat(cot, pre_grad)
    stage(1, 1, y)
    start(1, y)
    one, two = Sum(0, w1_o), Sum(1, w2_o)
    cells = flat(hidden)
    for n in range(9):
        term = product(cells, xb[n].astype(BF16), 0, 0) * scale
        acc[1, n * per:(n + 1) * per] = term.reshape(per, 16, C)
    two.advance()
    weight_terms(xf1, cot, 0)
    one.advance()
    two.advance()
    one.advance()
    await_arrivals(1, y)
    forward_taps(1, hidden, xf2)
    channel_major(apply(xf2, k2, 0), res_o)
    two.advance()
    one.advance()
    backward_taps(1, pre_grad, xb)
    channel_major(apply(xb, k1, 1), fg_o)
    while not (one.over and two.over):
        one.advance()
        two.advance()
    await_sends(0, x)
    await_sends(1, y)


def deliver(*refs):
    sources, targets, sems = refs[0:4], refs[4:8], refs[8]
    moves = [pltpu.make_async_copy(a, b, sems.at[n]) for n, (a, b) in enumerate(zip(sources, targets))]
    for move in moves:
        move.start()
    for move in moves:
        move.wait()


def plan(n_t, n_f):
    tile_bits = [1 << i for i in range(n_t.bit_length() - 1)]
    face_bits = [1 << i for i in range(n_f.bit_length() - 1)]
    groups = [([("tile", tile_bits[0])], 1)]
    middle = [("face", s) for s in face_bits] + [("tile", s) for s in tile_bits[1:2]]
    rest = [("tile", s) for s in tile_bits[2:]]
    while middle:
        groups.append((middle[:2], 0))
        middle = middle[2:]
    while rest:
        groups.append((rest[:2], 0))
        rest = rest[2:]
    return groups


def run(fields, upstream, k1, k2, n_t, n_f):
    C, G, J, H = fields.shape
    S = H // 3
    E = J + 2
    M = G * J * H
    ranks = n_t * n_f
    blocks = -(-(9 * (C // 16)) // ranks) * ranks
    scale = 1.0 / (S * 12.0 ** 0.5)
    groups = plan(n_t, n_f)
    length, room = blocks, [1, 1]
    for bits, full in groups:
        others = 2 ** len(bits) - 1
        length //= others + 1
        room[full] += length * others
    dma = pltpu.SemaphoreType.DMA
    vmem = pl.BlockSpec(memory_space=pltpu.VMEM)
    hbm = pl.BlockSpec(memory_space=pltpu.HBM)
    held = [pltpu.with_memory_space_constraint(a, pltpu.HBM) for a in (fields, upstream, k1, k2)]
    return pl.pallas_call(
        functools.partial(body, n_t, n_f, scale, groups),
        out_shape=(
            jax.ShapeDtypeStruct((C, G, J, H), BF16),
            jax.ShapeDtypeStruct((C, G, J, H), BF16),
            jax.ShapeDtypeStruct((3, 3, C, C), F32),
            jax.ShapeDtypeStruct((3, 3, C, C), F32),
        ),
        in_specs=[hbm] * 4,
        out_specs=[vmem] * 4,
        scratch_shapes=[
            pltpu.VMEM((2, C, G, J, H), BF16),
            pltpu.VMEM((2, G, J, H, C), BF16),
            pltpu.VMEM(k1.shape, BF16),
            pltpu.VMEM(k2.shape, BF16),
            pltpu.VMEM((2, G, J, H, C), BF16),
            pltpu.VMEM((2, 2, 2, G, J, C), F32),
            pltpu.VMEM((2, 2, G, H, C), BF16),
            pltpu.VMEM((2, 2, G, H, C), BF16),
            pltpu.VMEM((2, 2, G, E, C), F32),
            pltpu.VMEM((2, 2, G, E, C), F32),
            pltpu.VMEM((2, n_t, 2, G, E, C), F32),
            pltpu.VMEM((2, n_t, 2, G, J, C), F32),
            pltpu.VMEM((2, n_t, 2, G, J, C), F32),
            pltpu.VMEM((2, G, S + 16, C), F32),
            pltpu.VMEM((2, G, S + 16, C), F32),
            pltpu.VMEM((2, G, S + 32, C), F32),
            pltpu.VMEM((G, J + 2, H + 16, C), F32),
            pltpu.VMEM((9, M, C), F32),
            pltpu.VMEM((9, M, C), BF16),
            pltpu.VMEM((9, M, C), BF16),
            pltpu.VMEM((2, blocks, 16, C), F32),
            pltpu.VMEM((2, blocks, 16, C), BF16),
            pltpu.VMEM((2, room[0], 16, C), BF16),
            pltpu.VMEM((2, room[1], 16, C), F32),
            pltpu.VMEM((2, blocks, 16, C), BF16),
            dma((2, 4)), dma((2, 4)),
            dma((2, 2)), dma((2, 2)), dma((2, 2)),
            dma((2, 2)), dma((2, 2)), dma((2, 2)),
            dma((2, 2 * len(groups))), dma((2, 2 * len(groups))), dma((4,)),
        ],
        compiler_params=pltpu.CompilerParams(
            collective_id=0, has_side_effects=True, vmem_limit_bytes=24 * 1024 * 1024),
    )(*held)


def send_out(made):
    vmem = pl.BlockSpec(memory_space=pltpu.VMEM)
    hbm = pl.BlockSpec(memory_space=pltpu.HBM)
    return pl.pallas_call(
        deliver,
        out_shape=[jax.ShapeDtypeStruct(a.shape, a.dtype) for a in made],
        in_specs=[vmem] * 4,
        out_specs=[hbm] * 4,
        scratch_shapes=[pltpu.SemaphoreType.DMA((4,))],
    )(*[pltpu.with_memory_space_constraint(a, pltpu.VMEM) for a in made])


def on_device(n_sub, n_t, n_f, fields, upstream, k1, k2):
    own = fields.shape[0]
    if n_sub > 1:
        fields = lax.all_gather(fields, "sub", axis=0, tiled=True)
        upstream = lax.all_gather(upstream, "sub", axis=0, tiled=True)
    made = run(fields, upstream, k1, k2, n_t, n_f)
    if n_sub > 1:
        at = lax.axis_index("sub") * own
        res, fgrad, w1, w2 = made
        return (
            lax.dynamic_slice_in_dim(res, at, own, 0),
            lax.dynamic_slice_in_dim(fgrad, at, own, 0),
            lax.dynamic_slice_in_dim(w1, at, own, 3),
            lax.dynamic_slice_in_dim(w2, at, own, 3),
        )
    return tuple(send_out(made))


def solution(mesh):
    placed = (P("sub", "face", "tile", "parts"), P("sub", "face", "tile", "parts"), P(), P())
    sizes = mesh.shape
    return jax.shard_map(
        functools.partial(on_device, sizes["sub"], sizes["tile"], sizes["face"]),
        mesh=mesh,
        in_specs=placed,
        out_specs=(
            P("sub", "face", "tile", "parts"),
            P("sub", "face", "tile", "parts"),
            P("parts", None, None, "sub"),
            P("parts", None, None, "sub"),
        ),
        check_vma=False,
    )
```

```python
import functools

import jax
import jax.numpy as jnp
from jax import lax
from jax.experimental import pallas as pl
from jax.experimental.pallas import tpu as pltpu
from jax.sharding import PartitionSpec as P

MESH = pl.DeviceIdType.MESH
F32 = jnp.float32
BF16 = jnp.bfloat16
LANES = 128


def gelu_parts(v):
    root = 0.7978845608028654
    cube = 0.044715 * (v * v * v)
    th = jnp.tanh(root * (v + cube))
    value = v * (0.5 * (1.0 + th))
    slope = 0.5 * (1.0 + th) + 0.5 * v * (1.0 - th * th) * root * (1.0 + 0.134145 * (v * v))
    return value, slope


def product(a, b, da, db):
    return lax.dot_general(a, b, (((da,), (db,)), ((), ())), preferred_element_type=F32)


def body(n_t, n_f, scale, groups, fields_h, upstream_h, k1_h, k2_h, res_o, fg_o, w1_o, w2_o,
         raw, x, k1, k2, y, rows, lh, rh, ap, bm, aps, tr, dr, tl, dl, al, pad, xb, xf1, xf2,
         acc, sbuf, rlow, rfull, obuf,
         col_s, col_r, line_s, a_r, b_r, t_s, d_s, row_r, w_s, w_r, in_s):
    _, G, J, H, C = x.shape
    S = H // 3
    E = J + 2
    t = lax.axis_index("tile")
    f = lax.axis_index("face")
    fn = lax.rem(f + 1, n_f)
    fp = lax.rem(f + n_f - 1, n_f)
    first = t == 0
    last = t == n_t - 1
    inner_left = jnp.logical_not(first)
    inner_right = jnp.logical_not(last)

    def where_to(tile, face):
        return {"tile": tile, "face": face}

    def remote(src, dst, s, r, dev):
        return pltpu.make_async_remote_copy(
            src_ref=src, dst_ref=dst, send_sem=s, recv_sem=r, device_id=dev, device_id_type=MESH)

    def settle(ref, sem):
        pltpu.make_async_copy(ref, ref, sem).wait()

    def copies(p, src):
        c0, cl = src.at[:, :, 0], src.at[:, :, J - 1]
        right = lambda: remote(cl, lh.at[p], col_s.at[p, 0], col_r.at[p, 0], where_to(jnp.minimum(t + 1, n_t - 1), f))
        left = lambda: remote(c0, rh.at[p], col_s.at[p, 1], col_r.at[p, 1], where_to(jnp.maximum(t - 1, 0), f))
        seam = []
        if G > 1:
            seam.append((first, lambda: remote(src.at[:, 1:G, 0], rh.at[p, :, 0:G - 1], col_s.at[p, 2], col_r.at[p, 2], where_to(n_t - 1, f))))
            seam.append((last, lambda: remote(src.at[:, 0:G - 1, J - 1], lh.at[p, :, 1:G], col_s.at[p, 2], col_r.at[p, 2], where_to(0, f))))
        seam.append((first, lambda: remote(src.at[:, 0:1, 0], rh.at[p, :, G - 1:G], col_s.at[p, 3], col_r.at[p, 3], where_to(n_t - 1, fp))))
        seam.append((last, lambda: remote(src.at[:, G - 1:G, J - 1], lh.at[p, :, 0:1], col_s.at[p, 3], col_r.at[p, 3], where_to(0, fn))))
        a_own = lambda d: remote(aps.at[p, d, :, 1:G], ap.at[p, :, 0:G - 1], line_s.at[p, 0], a_r.at[p, 0], where_to(d, f))
        a_oth = lambda d: remote(aps.at[p, d, :, 0:1], ap.at[p, :, G - 1:G], line_s.at[p, 1], a_r.at[p, 1], where_to(d, fp))
        b_own = lambda d: remote(aps.at[p, d, :, 0:G - 1], bm.at[p, :, 1:G], line_s.at[p, 0], b_r.at[p, 0], where_to(d, f))
        b_oth = lambda d: remote(aps.at[p, d, :, G - 1:G], bm.at[p, :, 0:1], line_s.at[p, 1], b_r.at[p, 1], where_to(d, fn))
        t_own = lambda d: remote(rows.at[p, 0, :, 0:G - 1], tr.at[p, d, :, 1:G], t_s.at[p, 0], row_r.at[p, 0], where_to(0, f))
        t_oth = lambda d: remote(rows.at[p, 0, :, G - 1:G], tr.at[p, d, :, 0:1], t_s.at[p, 1], row_r.at[p, 1], where_to(0, fn))
        d_own = lambda d: remote(rows.at[p, 1, :, 1:G], dr.at[p, d, :, 0:G - 1], d_s.at[p, 0], row_r.at[p, 0], where_to(n_t - 1, f))
        d_oth = lambda d: remote(rows.at[p, 1, :, 0:1], dr.at[p, d, :, G - 1:G], d_s.at[p, 1], row_r.at[p, 1], where_to(n_t - 1, fp))
        return right, left, seam, a_own, a_oth, b_own, b_oth, t_own, t_oth, d_own, d_oth

    def stage(p, kind, src):
        for q in range(G):
            for j in range(J):
                rows[p, 0, kind, q, j:j + 1, :] = src[kind, q, j, 0:16].astype(F32)[0:1]
                rows[p, 1, kind, q, j:j + 1, :] = src[kind, q, j, H - 16:H].astype(F32)[15:16]
        more = 16 * kind

        @pl.when(first)
        def _():
            for q in range(G):
                al[kind, q, 16:16 + S + more, :] = src[kind, q, 0, 0:S + more].astype(F32)
            for d in range(n_t):
                aps[p, d, kind] = al[kind, :, 15 + d * J:15 + d * J + E, :]

        @pl.when(last)
        def _():
            for q in range(G):
                al[kind, q, 16 - more:16 + S, :] = src[kind, q, J - 1, 2 * S - more:H].astype(F32)
            for d in range(n_t):
                aps[p, d, kind] = al[kind, :, 15 + d * J:15 + d * J + E, :]

    def start(p, src):
        right, left, seam, a_own, a_oth, b_own, b_oth, t_own, t_oth, d_own, d_oth = copies(p, src)
        t_oth(t).start()
        d_oth(t).start()
        if G > 1:
            @pl.when(inner_left)
            def _():
                t_own(t).start()

            @pl.when(inner_right)
            def _():
                d_own(t).start()
        for cond, make in seam:
            @pl.when(cond)
            def _(make=make):
                make().start()

        @pl.when(first)
        def _():
            @pl.loop(0, n_t)
            def _(d):
                a_oth(n_t - 1 - d).start()
            if G > 1:
                @pl.loop(1, n_t)
                def _(d):
                    a_own(n_t - d).start()
                ap[p, :, 0:G - 1] = aps[p, 0, :, 1:G]
                tr[p, 0, :, 1:G] = rows[p, 0, :, 0:G - 1]

        @pl.when(last)
        def _():
            @pl.loop(0, n_t)
            def _(d):
                b_oth(d).start()
            if G > 1:
                @pl.loop(0, n_t - 1)
                def _(d):
                    b_own(d).start()
                bm[p, :, 1:G] = aps[p, n_t - 1, :, 0:G - 1]
                dr[p, n_t - 1, :, 0:G - 1] = rows[p, 1, :, 1:G]

        @pl.when(inner_right)
        def _():
            right().start()

        @pl.when(inner_left)
        def _():
            left().start()

    def await_arrivals(p, src):
        right, left, seam, a_own, a_oth, b_own, b_oth, t_own, t_oth, d_own, d_oth = copies(p, src)

        @pl.when(inner_left)
        def _():
            right().wait_recv()
            if G > 1:
                a_own(0).wait_recv()

        @pl.when(inner_right)
        def _():
            left().wait_recv()
            if G > 1:
                b_own(0).wait_recv()

        for cond, make in seam:
            @pl.when(last if cond is first else first)
            def _(make=make):
                make().wait_recv()

        a_oth(0).wait_recv()
        b_oth(0).wait_recv()

        @pl.when(first)
        def _():
            if G > 1:
                settle(tr.at[p, 1:n_t, :, 1:G], row_r.at[p, 0])
            settle(tr.at[p, :, :, 0:1], row_r.at[p, 1])
            for d in range(n_t):
                tl[:, :, 8 + d * J:8 + (d + 1) * J, :] = tr[p, d]

        @pl.when(last)
        def _():
            if G > 1:
                settle(dr.at[p, 0:n_t - 1, :, 0:G - 1], row_r.at[p, 0])
            settle(dr.at[p, :, :, G - 1:G], row_r.at[p, 1])
            for d in range(n_t):
                dl[:, :, 8 + d * J:8 + (d + 1) * J, :] = dr[p, d]

    def await_sends(p, src):
        right, left, seam, a_own, a_oth, b_own, b_oth, t_own, t_oth, d_own, d_oth = copies(p, src)

        @pl.when(inner_right)
        def _():
            right().wait_send()
            if G > 1:
                d_own(t).wait_send()

        @pl.when(inner_left)
        def _():
            left().wait_send()
            if G > 1:
                t_own(t).wait_send()

        for cond, make in seam:
            @pl.when(cond)
            def _(make=make):
                make().wait_send()
        t_oth(t).wait_send()
        d_oth(t).wait_send()

        @pl.when(jnp.logical_or(first, last))
        def _():
            if G > 1:
                settle(aps.at[p, 1:n_t, :, 1:G], line_s.at[p, 0])
            settle(aps.at[p, :, :, 0:1], line_s.at[p, 1])

    def fill_columns(src):
        for q in range(G):
            for j in range(J):
                pad[q, 1 + j, 8:8 + H, :] = src[q, j].astype(F32)

    def forward_taps(p, src, out):
        fill_columns(src)
        for q in range(G):
            @pl.when(inner_left)
            def _():
                pad[q, 0, 8:8 + H, :] = lh[p, 0, q].astype(F32)

            @pl.when(first)
            def _():
                pad[q, 0, 8:8 + S, :] = tl[0, q, 8:8 + S, :]
                pad[q, 0, 8 + S:8 + H, :] = lh[p, 0, q, 0:2 * S].astype(F32)

            @pl.when(inner_right)
            def _():
                pad[q, J + 1, 8:8 + H, :] = rh[p, 0, q].astype(F32)

            @pl.when(last)
            def _():
                pad[q, J + 1, 8:8 + 2 * S, :] = rh[p, 0, q, S:H].astype(F32)
                pad[q, J + 1, 8 + 2 * S:8 + H, :] = dl[0, q, 8:8 + S, :]
            for j in range(E):
                pad[q, j, 7:8, :] = ap[p, 0, q, j:j + 1]
                pad[q, j, 8 + H:9 + H, :] = bm[p, 0, q, j:j + 1]
        for a in range(3):
            for b in range(3):
                for q in range(G):
                    for j in range(J):
                        m = (q * J + j) * H
                        out[3 * a + b, m:m + H, :] = pad[q, j + a, 7 + b:7 + b + H, :].astype(BF16)

    def backward_taps(p, src, out):
        fill_columns(src)
        for q in range(G):
            @pl.when(inner_left)
            def _():
                pad[q, 0, 8:8 + H, :] = lh[p, 1, q].astype(F32)

            @pl.when(first)
            def _():
                pad[q, 0, :, :] = jnp.zeros((H + 16, C), F32)

            @pl.when(inner_right)
            def _():
                pad[q, J + 1, 8:8 + H, :] = rh[p, 1, q].astype(F32)

            @pl.when(last)
            def _():
                pad[q, J + 1, :, :] = jnp.zeros((H + 16, C), F32)
            for j in range(E):
                pad[q, j, 7:8, :] = jnp.zeros((1, C), F32)
                pad[q, j, 8 + H:9 + H, :] = jnp.zeros((1, C), F32)
        for a in range(3):
            for b in range(3):
                for q in range(G):
                    for j in range(J):
                        m = (q * J + j) * H
                        out[3 * a + b, m:m + H, :] = pad[q, j - a + 2, 9 - b:9 - b + H, :]
        for q in range(G):
            top = ap[p, 1, q]
            low = bm[p, 1, q]
            for b in range(3):
                for j in range(J):
                    m = (q * J + j) * H
                    out[b, m:m + 1, :] += top[j + 2 - b:j + 3 - b]
                    out[6 + b, m + H - 1:m + H, :] += low[j + 2 - b:j + 3 - b]

        @pl.when(last)
        def _():
            for q in range(G):
                m = (q * J + J - 1) * H
                pad[q, J + 1, 8:8 + H, :] = rh[p, 1, q].astype(F32)
                for e in range(3):
                    out[e, m:m + 2 * S, :] += pad[q, J + 1, 8 + S + 1 - e:8 + H + 1 - e, :]
                    out[3 * e + 2, m + 2 * S:m + H, :] += dl[1, q, 9 - e:9 - e + S, :]

        @pl.when(first)
        def _():
            for q in range(G):
                m = q * J * H
                pad[q, 0, 8:8 + H, :] = lh[p, 1, q].astype(F32)
                for e in range(3):
                    out[3 * e, m:m + S, :] += tl[1, q, 9 - e:9 - e + S, :]
                    out[6 + e, m + S:m + H, :] += pad[q, 0, 9 - e:9 - e + 2 * S, :]

    def apply(taps, k, dim):
        total = product(taps[0].astype(BF16), k[0, 0], 1, dim)
        for n in range(1, 9):
            total = total + product(taps[n].astype(BF16), k[n // 3, n % 3], 1, dim)
        return total

    def flat(src):
        return jnp.concatenate([src[q, j] for q in range(G) for j in range(J)], axis=0)

    def unflat(value, dst):
        for q in range(G):
            for j in range(J):
                m = (q * J + j) * H
                dst[q, j] = value[m:m + H]

    def channel_major(value, dst):
        for q in range(G):
            for j in range(J):
                m = (q * J + j) * H
                dst[:, q, j, :] = value[m:m + H].T.astype(BF16)

    per = C // 16
    tiles = -(-9 * C // LANES)
    blocks = acc.shape[1]

    def pack(terms, w):
        spare = tiles * LANES - 9 * C
        wide = jnp.concatenate(terms + ([jnp.zeros((C, spare), F32)] if spare else []), axis=1)
        for n in range(tiles):
            acc[w, n * per:(n + 1) * per] = wide[:, n * LANES:(n + 1) * LANES].reshape(per, 16, LANES)

    def unpack(w, out):
        parts = [obuf[w, n * per:(n + 1) * per].astype(F32).reshape(C, LANES) for n in range(tiles)]
        wide = jnp.concatenate(parts, axis=1)
        for n in range(9):
            out[n // 3, n % 3] = wide[:, n * C:(n + 1) * C]

    class Sum:
        def __init__(self, w, out):
            self.out, self.at, self.over = out, 0, False
            self.w, self.lo, self.length, self.done = w, 0, blocks, []
            self.used = [0, 0]
            self.sem = 0

        def members(self, bits):
            mine = []
            for axis, s in bits:
                mine.append(lax.rem((t if axis == "tile" else f) // s, 2))
            found = []
            for k in range(1, 2 ** len(bits)):
                tile, face, digit = t, f, 0
                for pos, (axis, s) in enumerate(bits):
                    bit = mine[pos]
                    if (k >> pos) & 1:
                        if axis == "tile":
                            tile = tile + (1 - 2 * bit) * s
                        else:
                            face = face + (1 - 2 * bit) * s
                        bit = 1 - bit
                    digit = digit + bit * (1 << pos)
                found.append((digit, where_to(tile, face)))
            own = 0
            for pos, bit in enumerate(mine):
                own = own + bit * (1 << pos)
            return own, found

        def begin(self, n):
            bits, full, whole = groups[n]
            own, found = self.members(bits)
            w = self.w
            inbox = rfull if full else rlow
            at = self.used[full]
            part = self.length if whole else self.length // (len(found) + 1)
            self.flying = (inbox, at, part, len(found), whole)
            if whole:
                piece = pl.ds(self.lo, part)
                mine = pl.ds(at + own * part, part)
                sbuf[w, piece] = acc[w, piece].astype(BF16)
                for digit, dev in found:
                    remote(sbuf.at[w, piece], inbox.at[w, mine], w_s.at[w, self.sem], w_r.at[w, self.sem], dev).start()
                inbox[w, mine] = sbuf[w, piece]
                self.used[full] += part * (len(found) + 1)
                return
            for digit, dev in found:
                give = self.lo + digit * part
                if full:
                    out = acc.at[w, pl.ds(give, part)]
                else:
                    sbuf[w, pl.ds(give, part)] = acc[w, pl.ds(give, part)].astype(BF16)
                    out = sbuf.at[w, pl.ds(give, part)]
                at = self.used[full]
                self.used[full] += part
                remote(out, inbox.at[w, at:at + part], w_s.at[w, self.sem], w_r.at[w, self.sem], dev).start()
            keep = self.lo + own * part
            self.done.append((keep, part, found))
            self.lo, self.length = keep, part

        def end(self):
            inbox, at, part, count, whole = self.flying
            sent = inbox.at[self.w, at:at + count * part]
            settle(sent, w_s.at[self.w, self.sem])
            settle(sent, w_r.at[self.w, self.sem])
            self.sem += 1
            terms = [inbox[self.w, at + n * part:at + (n + 1) * part].astype(F32) for n in range(count + whole)]
            total = terms.pop(0) if whole else acc[self.w, pl.ds(self.lo, self.length)]
            for term in terms:
                total = total + term
            acc[self.w, pl.ds(self.lo, self.length)] = total

        def round(self):
            obuf[self.w, pl.ds(self.lo, self.length)] = acc[self.w, pl.ds(self.lo, self.length)].astype(BF16)

        def give(self):
            keep, part, found = self.done.pop()
            self.flying = (part, len(found))
            for digit, dev in found:
                remote(obuf.at[self.w, pl.ds(keep, part)], obuf.at[self.w, pl.ds(keep, part)],
                       w_s.at[self.w, self.sem], w_r.at[self.w, self.sem], dev).start()

        def given(self):
            part, count = self.flying
            whole = obuf.at[self.w, 0:count * part]
            settle(whole, w_s.at[self.w, self.sem])
            settle(whole, w_r.at[self.w, self.sem])
            self.sem += 1

        def advance(self):
            at, count = self.at, len(groups)
            self.at += 1
            if self.over:
                return
            if at < count:
                if at > 0:
                    self.end()
                self.begin(at)
                return
            if at == count:
                self.end()
                self.round()
            else:
                self.given()
            if self.done:
                self.give()
            else:
                unpack(self.w, self.out)
                self.over = True

    barrier = pltpu.get_barrier_semaphore()
    loads = [pltpu.make_async_copy(src, dst, in_s.at[n]) for n, (src, dst) in enumerate(
        ((fields_h, raw.at[0]), (upstream_h, raw.at[1]), (k1_h, k1), (k2_h, k2)))]
    for load in loads:
        load.start()

    @pl.loop(0, n_f)
    def _(df):
        @pl.loop(0, n_t)
        def _(dt):
            @pl.when(jnp.logical_or(df != f, dt != t))
            def _():
                pl.semaphore_signal(barrier, inc=1, device_id=where_to(dt, df), device_id_type=MESH)
    hidden, pre_grad = y.at[0], y.at[1]
    al[...] = jnp.zeros_like(al)
    tl[...] = jnp.zeros_like(tl)
    dl[...] = jnp.zeros_like(dl)
    for kind in range(2):
        loads[kind].wait()
        for q in range(G):
            for j in range(J):
                x[kind, q, j] = raw[kind, :, q, j, :].astype(F32).T.astype(BF16)
        stage(0, kind, x)
    if blocks > tiles * per:
        for w in range(2):
            acc[w, tiles * per:blocks] = jnp.zeros((blocks - tiles * per, 16, LANES), F32)
    pl.semaphore_wait(barrier, n_t * n_f - 1)

    start(0, x)
    loads[2].wait()
    loads[3].wait()
    await_arrivals(0, x)
    forward_taps(0, x.at[0], xf1)
    value, slope = gelu_parts(apply(xf1, k1, 0))
    unflat(value.astype(BF16), hidden)
    stage(1, 0, y)
    backward_taps(0, x.at[1], xb)
    cot = (apply(xb, k2, 1) * slope).astype(BF16)
    unflat(cot, pre_grad)
    stage(1, 1, y)
    start(1, y)
    one, two = Sum(0, w1_o), Sum(1, w2_o)
    cells = flat(hidden)
    pack([product(cells, xb[n].astype(BF16), 0, 0) * scale for n in range(9)], 1)
    two.advance()
    pack([product(xf1[n], cot, 0, 0) * scale for n in range(9)], 0)
    one.advance()
    two.advance()
    one.advance()
    two.advance()
    one.advance()
    await_arrivals(1, y)
    forward_taps(1, hidden, xf2)
    channel_major(apply(xf2, k2, 0), res_o)
    two.advance()
    one.advance()
    backward_taps(1, pre_grad, xb)
    channel_major(apply(xb, k1, 1), fg_o)
    while not (one.over and two.over):
        one.advance()
        two.advance()
    await_sends(0, x)
    await_sends(1, y)


def deliver(*refs):
    sources, targets, sems = refs[0:4], refs[4:8], refs[8]
    moves = [pltpu.make_async_copy(a, b, sems.at[n]) for n, (a, b) in enumerate(zip(sources, targets))]
    for move in moves:
        move.start()
    for move in moves:
        move.wait()


def plan(n_t, n_f):
    tile_bits = [("tile", 1 << i) for i in range(n_t.bit_length() - 1)]
    face_bits = [("face", 1 << i) for i in range(n_f.bit_length() - 1)]
    groups = [(tile_bits[:1], 1, 0)]
    middle, rest = face_bits + tile_bits[1:3], tile_bits[3:]
    while middle:
        groups.append((middle[:3], 0, 0))
        middle = middle[3:]
    while len(rest) > 2:
        groups.append((rest[:2], 0, 0))
        rest = rest[2:]
    if rest:
        groups.append((rest, 0, 1))
    return groups


def run(fields, upstream, k1, k2, n_t, n_f):
    C, G, J, H = fields.shape
    S = H // 3
    E = J + 2
    M = G * J * H
    scale = 1.0 / (S * 12.0 ** 0.5)
    groups = plan(n_t, n_f)
    cuts, stages = 1, 0
    for bits, full, whole in groups:
        cuts *= 1 if whole else 2 ** len(bits)
        stages += 1 if whole else 2
    blocks = -(-9 * C // LANES) * (C // 16)
    blocks = -(-blocks // cuts) * cuts
    length, room = blocks, [1, 1]
    for bits, full, whole in groups:
        members = 2 ** len(bits)
        if whole:
            room[full] += length * members
        else:
            length //= members
            room[full] += length * (members - 1)
    dma = pltpu.SemaphoreType.DMA
    vmem = pl.BlockSpec(memory_space=pltpu.VMEM)
    hbm = pl.BlockSpec(memory_space=pltpu.HBM)
    held = [pltpu.with_memory_space_constraint(a, pltpu.HBM) for a in (fields, upstream, k1, k2)]
    return pl.pallas_call(
        functools.partial(body, n_t, n_f, scale, groups),
        out_shape=(
            jax.ShapeDtypeStruct((C, G, J, H), BF16),
            jax.ShapeDtypeStruct((C, G, J, H), BF16),
            jax.ShapeDtypeStruct((3, 3, C, C), F32),
            jax.ShapeDtypeStruct((3, 3, C, C), F32),
        ),
        in_specs=[hbm] * 4,
        out_specs=[vmem] * 4,
        scratch_shapes=[
            pltpu.VMEM((2, C, G, J, H), BF16),
            pltpu.VMEM((2, G, J, H, C), BF16),
            pltpu.VMEM(k1.shape, BF16),
            pltpu.VMEM(k2.shape, BF16),
            pltpu.VMEM((2, G, J, H, C), BF16),
            pltpu.VMEM((2, 2, 2, G, J, C), F32),
            pltpu.VMEM((2, 2, G, H, C), BF16),
            pltpu.VMEM((2, 2, G, H, C), BF16),
            pltpu.VMEM((2, 2, G, E, C), F32),
            pltpu.VMEM((2, 2, G, E, C), F32),
            pltpu.VMEM((2, n_t, 2, G, E, C), F32),
            pltpu.VMEM((2, n_t, 2, G, J, C), F32),
            pltpu.VMEM((2, n_t, 2, G, J, C), F32),
            pltpu.VMEM((2, G, S + 16, C), F32),
            pltpu.VMEM((2, G, S + 16, C), F32),
            pltpu.VMEM((2, G, S + 32, C), F32),
            pltpu.VMEM((G, J + 2, H + 16, C), F32),
            pltpu.VMEM((9, M, C), F32),
            pltpu.VMEM((9, M, C), BF16),
            pltpu.VMEM((9, M, C), BF16),
            pltpu.VMEM((2, blocks, 16, LANES), F32),
            pltpu.VMEM((2, blocks, 16, LANES), BF16),
            pltpu.VMEM((2, room[0], 16, LANES), BF16),
            pltpu.VMEM((2, room[1], 16, LANES), F32),
            pltpu.VMEM((2, blocks, 16, LANES), BF16),
            dma((2, 4)), dma((2, 4)),
            dma((2, 2)), dma((2, 2)), dma((2, 2)),
            dma((2, 2)), dma((2, 2)), dma((2, 2)),
            dma((2, stages)), dma((2, stages)), dma((4,)),
        ],
        compiler_params=pltpu.CompilerParams(
            collective_id=0, has_side_effects=True, vmem_limit_bytes=24 * 1024 * 1024),
    )(*held)


def send_out(made):
    vmem = pl.BlockSpec(memory_space=pltpu.VMEM)
    hbm = pl.BlockSpec(memory_space=pltpu.HBM)
    return pl.pallas_call(
        deliver,
        out_shape=[jax.ShapeDtypeStruct(a.shape, a.dtype) for a in made],
        in_specs=[vmem] * 4,
        out_specs=[hbm] * 4,
        scratch_shapes=[pltpu.SemaphoreType.DMA((4,))],
    )(*[pltpu.with_memory_space_constraint(a, pltpu.VMEM) for a in made])


def on_device(n_sub, n_t, n_f, fields, upstream, k1, k2):
    own = fields.shape[0]
    if n_sub > 1:
        fields = lax.all_gather(fields, "sub", axis=0, tiled=True)
        upstream = lax.all_gather(upstream, "sub", axis=0, tiled=True)
    made = run(fields, upstream, k1, k2, n_t, n_f)
    if n_sub > 1:
        at = lax.axis_index("sub") * own
        res, fgrad, w1, w2 = made
        return (
            lax.dynamic_slice_in_dim(res, at, own, 0),
            lax.dynamic_slice_in_dim(fgrad, at, own, 0),
            lax.dynamic_slice_in_dim(w1, at, own, 3),
            lax.dynamic_slice_in_dim(w2, at, own, 3),
        )
    return tuple(send_out(made))


def solution(mesh):
    placed = (P("sub", "face", "tile", "parts"), P("sub", "face", "tile", "parts"), P(), P())
    sizes = mesh.shape
    return jax.shard_map(
        functools.partial(on_device, sizes["sub"], sizes["tile"], sizes["face"]),
        mesh=mesh,
        in_specs=placed,
        out_specs=(
            P("sub", "face", "tile", "parts"),
            P("sub", "face", "tile", "parts"),
            P("parts", None, None, "sub"),
            P("parts", None, None, "sub"),
        ),
        check_vma=False,
    )
```

```python
import functools

import jax
import jax.numpy as jnp
from jax import lax
from jax.experimental import pallas as pl
from jax.experimental.pallas import tpu as pltpu
from jax.sharding import PartitionSpec as P

MESH = pl.DeviceIdType.MESH
F32 = jnp.float32
BF16 = jnp.bfloat16
LANES = 128


def gelu_parts(v):
    root = 0.7978845608028654
    cube = 0.044715 * (v * v * v)
    th = jnp.tanh(root * (v + cube))
    value = v * (0.5 * (1.0 + th))
    slope = 0.5 * (1.0 + th) + 0.5 * v * (1.0 - th * th) * root * (1.0 + 0.134145 * (v * v))
    return value, slope


def product(a, b, da, db):
    return lax.dot_general(a, b, (((da,), (db,)), ((), ())), preferred_element_type=F32)


def body(n_t, n_f, scale, groups, fields_h, upstream_h, k1_h, k2_h, res_o, fg_o, w1_o, w2_o,
         raw, x, k1, k2, y, rows, lh, rh, ap, bm, aps, tr, dr, tl, dl, al, pad, xb, xf1, xf2, pre, back,
         acc, sbuf, rlow, rfull, obuf,
         col_s, col_r, line_s, a_r, b_r, t_s, d_s, row_r, w_s, w_r, in_s):
    _, G, J, H, C = x.shape
    S = H // 3
    E = J + 2
    t = lax.axis_index("tile")
    f = lax.axis_index("face")
    fn = lax.rem(f + 1, n_f)
    fp = lax.rem(f + n_f - 1, n_f)
    first = t == 0
    last = t == n_t - 1
    inner_left = jnp.logical_not(first)
    inner_right = jnp.logical_not(last)

    upper, lower = slice(S - 16, H), slice(0, 2 * S + 16)

    def where_to(tile, face):
        return {"tile": tile, "face": face}

    def remote(src, dst, s, r, dev):
        return pltpu.make_async_remote_copy(
            src_ref=src, dst_ref=dst, send_sem=s, recv_sem=r, device_id=dev, device_id_type=MESH)

    def settle(ref, sem):
        pltpu.make_async_copy(ref, ref, sem).wait()

    def copies(p, src):
        c0, cl = src.at[:, :, 0], src.at[:, :, J - 1]
        right = lambda: remote(cl, lh.at[p], col_s.at[p, 0], col_r.at[p, 0], where_to(jnp.minimum(t + 1, n_t - 1), f))
        left = lambda: remote(c0, rh.at[p], col_s.at[p, 1], col_r.at[p, 1], where_to(jnp.maximum(t - 1, 0), f))
        seam = []
        if G > 1:
            seam.append((first, lambda: remote(src.at[:, 1:G, 0, upper], rh.at[p, :, 0:G - 1, upper], col_s.at[p, 2], col_r.at[p, 2], where_to(n_t - 1, f))))
            seam.append((last, lambda: remote(src.at[:, 0:G - 1, J - 1, lower], lh.at[p, :, 1:G, lower], col_s.at[p, 2], col_r.at[p, 2], where_to(0, f))))
        seam.append((first, lambda: remote(src.at[:, 0:1, 0, upper], rh.at[p, :, G - 1:G, upper], col_s.at[p, 3], col_r.at[p, 3], where_to(n_t - 1, fp))))
        seam.append((last, lambda: remote(src.at[:, G - 1:G, J - 1, lower], lh.at[p, :, 0:1, lower], col_s.at[p, 3], col_r.at[p, 3], where_to(0, fn))))
        a_own = lambda d: remote(aps.at[p, d, :, 1:G], ap.at[p, :, 0:G - 1], line_s.at[p, 0], a_r.at[p, 0], where_to(d, f))
        a_oth = lambda d: remote(aps.at[p, d, :, 0:1], ap.at[p, :, G - 1:G], line_s.at[p, 1], a_r.at[p, 1], where_to(d, fp))
        b_own = lambda d: remote(aps.at[p, d, :, 0:G - 1], bm.at[p, :, 1:G], line_s.at[p, 0], b_r.at[p, 0], where_to(d, f))
        b_oth = lambda d: remote(aps.at[p, d, :, G - 1:G], bm.at[p, :, 0:1], line_s.at[p, 1], b_r.at[p, 1], where_to(d, fn))
        t_own = lambda d: remote(rows.at[p, 0, :, 0:G - 1], tr.at[p, d, :, 1:G], t_s.at[p, 0], row_r.at[p, 0], where_to(0, f))
        t_oth = lambda d: remote(rows.at[p, 0, :, G - 1:G], tr.at[p, d, :, 0:1], t_s.at[p, 1], row_r.at[p, 1], where_to(0, fn))
        d_own = lambda d: remote(rows.at[p, 1, :, 1:G], dr.at[p, d, :, 0:G - 1], d_s.at[p, 0], row_r.at[p, 0], where_to(n_t - 1, f))
        d_oth = lambda d: remote(rows.at[p, 1, :, 0:1], dr.at[p, d, :, G - 1:G], d_s.at[p, 1], row_r.at[p, 1], where_to(n_t - 1, fp))
        return right, left, seam, a_own, a_oth, b_own, b_oth, t_own, t_oth, d_own, d_oth

    def stage(p, kind, src):
        for q in range(G):
            for j in range(J):
                rows[p, 0, kind, q, j:j + 1, :] = src[kind, q, j, 0:16].astype(F32)[0:1]
                rows[p, 1, kind, q, j:j + 1, :] = src[kind, q, j, H - 16:H].astype(F32)[15:16]
        more = 16 * kind

        @pl.when(first)
        def _():
            for q in range(G):
                al[kind, q, 16:16 + S + more, :] = src[kind, q, 0, 0:S + more].astype(F32)
            for d in range(n_t):
                aps[p, d, kind] = al[kind, :, 15 + d * J:15 + d * J + E, :]

        @pl.when(last)
        def _():
            for q in range(G):
                al[kind, q, 16 - more:16 + S, :] = src[kind, q, J - 1, 2 * S - more:H].astype(F32)
            for d in range(n_t):
                aps[p, d, kind] = al[kind, :, 15 + d * J:15 + d * J + E, :]

    def start(p, src):
        right, left, seam, a_own, a_oth, b_own, b_oth, t_own, t_oth, d_own, d_oth = copies(p, src)

        @pl.when(first)
        def _():
            @pl.loop(0, n_t)
            def _(d):
                a_oth(n_t - 1 - d).start()
            if G > 1:
                @pl.loop(1, n_t)
                def _(d):
                    a_own(n_t - d).start()
                ap[p, :, 0:G - 1] = aps[p, 0, :, 1:G]
                tr[p, 0, :, 1:G] = rows[p, 0, :, 0:G - 1]

        @pl.when(last)
        def _():
            @pl.loop(0, n_t)
            def _(d):
                b_oth(d).start()
            if G > 1:
                @pl.loop(0, n_t - 1)
                def _(d):
                    b_own(d).start()
                bm[p, :, 1:G] = aps[p, n_t - 1, :, 0:G - 1]
                dr[p, n_t - 1, :, 0:G - 1] = rows[p, 1, :, 1:G]

        for cond, make in seam:
            @pl.when(cond)
            def _(make=make):
                make().start()
        t_oth(t).start()
        d_oth(t).start()
        if G > 1:
            @pl.when(inner_left)
            def _():
                t_own(t).start()

            @pl.when(inner_right)
            def _():
                d_own(t).start()

        @pl.when(inner_right)
        def _():
            right().start()

        @pl.when(inner_left)
        def _():
            left().start()

    def await_arrivals(p, src):
        right, left, seam, a_own, a_oth, b_own, b_oth, t_own, t_oth, d_own, d_oth = copies(p, src)

        @pl.when(inner_left)
        def _():
            right().wait_recv()
            if G > 1:
                a_own(0).wait_recv()

        @pl.when(inner_right)
        def _():
            left().wait_recv()
            if G > 1:
                b_own(0).wait_recv()

        a_oth(0).wait_recv()
        b_oth(0).wait_recv()

    def await_seam(p, src):
        seam = copies(p, src)[2]
        for cond, make in seam:
            @pl.when(last if cond is first else first)
            def _(make=make):
                make().wait_recv()

        @pl.when(first)
        def _():
            if G > 1:
                settle(tr.at[p, 1:n_t, :, 1:G], row_r.at[p, 0])
            settle(tr.at[p, :, :, 0:1], row_r.at[p, 1])
            for d in range(n_t):
                tl[:, :, 8 + d * J:8 + (d + 1) * J, :] = tr[p, d]

        @pl.when(last)
        def _():
            if G > 1:
                settle(dr.at[p, 0:n_t - 1, :, 0:G - 1], row_r.at[p, 0])
            settle(dr.at[p, :, :, G - 1:G], row_r.at[p, 1])
            for d in range(n_t):
                dl[:, :, 8 + d * J:8 + (d + 1) * J, :] = dr[p, d]

    def await_sends(p, src):
        right, left, seam, a_own, a_oth, b_own, b_oth, t_own, t_oth, d_own, d_oth = copies(p, src)

        @pl.when(inner_right)
        def _():
            right().wait_send()
            if G > 1:
                d_own(t).wait_send()

        @pl.when(inner_left)
        def _():
            left().wait_send()
            if G > 1:
                t_own(t).wait_send()

        for cond, make in seam:
            @pl.when(cond)
            def _(make=make):
                make().wait_send()
        t_oth(t).wait_send()
        d_oth(t).wait_send()

        @pl.when(jnp.logical_or(first, last))
        def _():
            if G > 1:
                settle(aps.at[p, 1:n_t, :, 1:G], line_s.at[p, 0])
            settle(aps.at[p, :, :, 0:1], line_s.at[p, 1])

    def fill_columns(src):
        for q in range(G):
            for j in range(J):
                pad[q, 1 + j, 8:8 + H, :] = src[q, j].astype(F32)

    def forward_taps(p, src, out, late):
        fill_columns(src)
        for q in range(G):
            @pl.when(inner_left)
            def _():
                pad[q, 0, 8:8 + H, :] = lh[p, 0, q].astype(F32)

            @pl.when(inner_right)
            def _():
                pad[q, J + 1, 8:8 + H, :] = rh[p, 0, q].astype(F32)

            if late:
                @pl.when(first)
                def _():
                    pad[q, 0, 8:8 + H, :] = jnp.zeros((H, C), F32)

                @pl.when(last)
                def _():
                    pad[q, J + 1, 8:8 + H, :] = jnp.zeros((H, C), F32)
            else:
                @pl.when(first)
                def _():
                    forward_edge(p, q, 0)

                @pl.when(last)
                def _():
                    forward_edge(p, q, J + 1)
            for j in range(E):
                pad[q, j, 7:8, :] = ap[p, 0, q, j:j + 1]
                pad[q, j, 8 + H:9 + H, :] = bm[p, 0, q, j:j + 1]
        for a in range(3):
            for b in range(3):
                for q in range(G):
                    for j in range(J):
                        m = (q * J + j) * H
                        out[3 * a + b, m:m + H, :] = pad[q, j + a, 7 + b:7 + b + H, :].astype(BF16)

    def forward_edge(p, q, j):
        if j == 0:
            pad[q, 0, 8:8 + S, :] = tl[0, q, 8:8 + S, :]
            pad[q, 0, 8 + S:8 + H, :] = lh[p, 0, q, 0:2 * S].astype(F32)
        else:
            pad[q, J + 1, 8:8 + 2 * S, :] = rh[p, 0, q, S:H].astype(F32)
            pad[q, J + 1, 8 + 2 * S:8 + H, :] = dl[0, q, 8:8 + S, :]

    def forward_late(p, out, k, total):
        for cond, a, j in ((first, 0, 0), (last, 2, J + 1)):
            @pl.when(cond)
            def _(a=a, j=j):
                for q in range(G):
                    forward_edge(p, q, j)
                    pad[q, j, 7:8, :] = jnp.zeros((1, C), F32)
                    pad[q, j, 8 + H:9 + H, :] = jnp.zeros((1, C), F32)
                    m = (q * J + j - a) * H
                    more = total[m:m + H, :]
                    for b in range(3):
                        tap = pad[q, j, 7 + b:7 + b + H, :].astype(BF16)
                        more = more + product(tap, k[a, b], 1, 0)
                        out[3 * a + b, m:m + H, :] += tap
                    total[m:m + H, :] = more

    def backward_taps(p, src, out, late):
        fill_columns(src)
        for q in range(G):
            @pl.when(inner_left)
            def _():
                pad[q, 0, 8:8 + H, :] = lh[p, 1, q].astype(F32)

            @pl.when(first)
            def _():
                pad[q, 0, :, :] = jnp.zeros((H + 16, C), F32)

            @pl.when(inner_right)
            def _():
                pad[q, J + 1, 8:8 + H, :] = rh[p, 1, q].astype(F32)

            @pl.when(last)
            def _():
                pad[q, J + 1, :, :] = jnp.zeros((H + 16, C), F32)
            for j in range(E):
                pad[q, j, 7:8, :] = jnp.zeros((1, C), F32)
                pad[q, j, 8 + H:9 + H, :] = jnp.zeros((1, C), F32)
        for a in range(3):
            for b in range(3):
                for q in range(G):
                    for j in range(J):
                        m = (q * J + j) * H
                        out[3 * a + b, m:m + H, :] = pad[q, j - a + 2, 9 - b:9 - b + H, :]
        for q in range(G):
            top = ap[p, 1, q]
            low = bm[p, 1, q]
            for b in range(3):
                for j in range(J):
                    m = (q * J + j) * H
                    out[b, m:m + 1, :] += top[j + 2 - b:j + 3 - b]
                    out[6 + b, m + H - 1:m + H, :] += low[j + 2 - b:j + 3 - b]
        if not late:
            backward_late(p, out, None, None)

    def backward_late(p, out, k, total):
        def add(n, m, rows_at, value):
            out[n, m + rows_at.start:m + rows_at.stop, :] += value
            if total is not None:
                here = slice(m + rows_at.start, m + rows_at.stop)
                total[here, :] += product(value.astype(BF16), k[n // 3, n % 3], 1, 1)

        @pl.when(last)
        def _():
            for q in range(G):
                m = (q * J + J - 1) * H
                pad[q, J + 1, 8:8 + H, :] = rh[p, 1, q].astype(F32)
                pad[q, J + 1, 8 + H:9 + H, :] = jnp.zeros((1, C), F32)
                for e in range(3):
                    add(e, m, slice(0, 2 * S), pad[q, J + 1, 8 + S + 1 - e:8 + H + 1 - e, :])
                    add(3 * e + 2, m, slice(2 * S, H), dl[1, q, 9 - e:9 - e + S, :])

        @pl.when(first)
        def _():
            for q in range(G):
                m = q * J * H
                pad[q, 0, 7:8, :] = jnp.zeros((1, C), F32)
                pad[q, 0, 8:8 + H, :] = lh[p, 1, q].astype(F32)
                for e in range(3):
                    add(3 * e, m, slice(0, S), tl[1, q, 9 - e:9 - e + S, :])
                    add(6 + e, m, slice(S, H), pad[q, 0, 9 - e:9 - e + 2 * S, :])

    def apply(taps, k, dim):
        total = product(taps[0].astype(BF16), k[0, 0], 1, dim)
        for n in range(1, 9):
            total = total + product(taps[n].astype(BF16), k[n // 3, n % 3], 1, dim)
        return total

    def flat(src):
        return jnp.concatenate([src[q, j] for q in range(G) for j in range(J)], axis=0)

    def unflat(value, dst):
        for q in range(G):
            for j in range(J):
                m = (q * J + j) * H
                dst[q, j] = value[m:m + H]

    def channel_major(value, dst):
        for q in range(G):
            for j in range(J):
                m = (q * J + j) * H
                dst[:, q, j, :] = value[m:m + H].T.astype(BF16)

    per = C // 16
    tiles = -(-9 * C // LANES)
    blocks = acc.shape[1]

    def pack(terms, w):
        spare = tiles * LANES - 9 * C
        wide = jnp.concatenate(terms + ([jnp.zeros((C, spare), F32)] if spare else []), axis=1)
        for n in range(tiles):
            acc[w, n * per:(n + 1) * per] = wide[:, n * LANES:(n + 1) * LANES].reshape(per, 16, LANES)

    def unpack(w, out):
        parts = [obuf[w, n * per:(n + 1) * per].astype(F32).reshape(C, LANES) for n in range(tiles)]
        wide = jnp.concatenate(parts, axis=1)
        for n in range(9):
            out[n // 3, n % 3] = wide[:, n * C:(n + 1) * C]

    class Sum:
        def __init__(self, w, out):
            self.out, self.at, self.over = out, 0, False
            self.w, self.lo, self.length, self.done = w, 0, blocks, []
            self.used = [0, 0]
            self.sem = 0

        def members(self, bits):
            mine = []
            for axis, s in bits:
                mine.append(lax.rem((t if axis == "tile" else f) // s, 2))
            found = []
            for k in reversed(range(1, 2 ** len(bits))):
                tile, face, digit = t, f, 0
                for pos, (axis, s) in enumerate(bits):
                    bit = mine[pos]
                    if (k >> pos) & 1:
                        if axis == "tile":
                            tile = tile + (1 - 2 * bit) * s
                        else:
                            face = face + (1 - 2 * bit) * s
                        bit = 1 - bit
                    digit = digit + bit * (1 << pos)
                found.append((digit, where_to(tile, face)))
            own = 0
            for pos, bit in enumerate(mine):
                own = own + bit * (1 << pos)
            return own, found

        def begin(self, n):
            bits, full, whole = groups[n]
            own, found = self.members(bits)
            w = self.w
            inbox = rfull if full else rlow
            at = self.used[full]
            part = self.length if whole else self.length // (len(found) + 1)
            self.flying = (inbox, at, part, len(found), whole)
            if whole:
                piece = pl.ds(self.lo, part)
                mine = pl.ds(at + own * part, part)
                sbuf[w, piece] = acc[w, piece].astype(BF16)
                for digit, dev in found:
                    remote(sbuf.at[w, piece], inbox.at[w, mine], w_s.at[w, self.sem], w_r.at[w, self.sem], dev).start()
                inbox[w, mine] = sbuf[w, piece]
                self.used[full] += part * (len(found) + 1)
                return
            for digit, dev in found:
                give = self.lo + digit * part
                if full:
                    out = acc.at[w, pl.ds(give, part)]
                else:
                    sbuf[w, pl.ds(give, part)] = acc[w, pl.ds(give, part)].astype(BF16)
                    out = sbuf.at[w, pl.ds(give, part)]
                at = self.used[full]
                self.used[full] += part
                remote(out, inbox.at[w, at:at + part], w_s.at[w, self.sem], w_r.at[w, self.sem], dev).start()
            keep = self.lo + own * part
            self.done.append((keep, part, found))
            self.lo, self.length = keep, part

        def end(self):
            inbox, at, part, count, whole = self.flying
            sent = inbox.at[self.w, at:at + count * part]
            settle(sent, w_s.at[self.w, self.sem])
            settle(sent, w_r.at[self.w, self.sem])
            self.sem += 1
            terms = [inbox[self.w, at + n * part:at + (n + 1) * part].astype(F32) for n in range(count + whole)]
            total = terms.pop(0) if whole else acc[self.w, pl.ds(self.lo, self.length)]
            for term in terms:
                total = total + term
            acc[self.w, pl.ds(self.lo, self.length)] = total

        def round(self):
            obuf[self.w, pl.ds(self.lo, self.length)] = acc[self.w, pl.ds(self.lo, self.length)].astype(BF16)

        def give(self):
            keep, part, found = self.done.pop()
            self.flying = (part, len(found))
            for digit, dev in found:
                remote(obuf.at[self.w, pl.ds(keep, part)], obuf.at[self.w, pl.ds(keep, part)],
                       w_s.at[self.w, self.sem], w_r.at[self.w, self.sem], dev).start()

        def given(self):
            part, count = self.flying
            whole = obuf.at[self.w, 0:count * part]
            settle(whole, w_s.at[self.w, self.sem])
            settle(whole, w_r.at[self.w, self.sem])
            self.sem += 1

        def advance(self):
            at, count = self.at, len(groups)
            self.at += 1
            if self.over:
                return
            if at < count:
                if at > 0:
                    self.end()
                self.begin(at)
                return
            if at == count:
                self.end()
                self.round()
            else:
                self.given()
            if self.done:
                self.give()
            else:
                unpack(self.w, self.out)
                self.over = True

    barrier = pltpu.get_barrier_semaphore()
    loads = [pltpu.make_async_copy(src, dst, in_s.at[n]) for n, (src, dst) in enumerate(
        ((fields_h, raw.at[0]), (upstream_h, raw.at[1]), (k1_h, k1), (k2_h, k2)))]
    for load in loads:
        load.start()

    @pl.loop(0, n_f)
    def _(df):
        @pl.loop(0, n_t)
        def _(dt):
            @pl.when(jnp.logical_or(df != f, dt != t))
            def _():
                pl.semaphore_signal(barrier, inc=1, device_id=where_to(dt, df), device_id_type=MESH)
    hidden, pre_grad = y.at[0], y.at[1]
    al[...] = jnp.zeros_like(al)
    tl[...] = jnp.zeros_like(tl)
    dl[...] = jnp.zeros_like(dl)
    for kind in range(2):
        loads[kind].wait()
        for q in range(G):
            for j in range(J):
                x[kind, q, j] = raw[kind, :, q, j, :].astype(F32).T.astype(BF16)
        stage(0, kind, x)
    if blocks > tiles * per:
        for w in range(2):
            acc[w, tiles * per:blocks] = jnp.zeros((blocks - tiles * per, 16, LANES), F32)
    pl.semaphore_wait(barrier, n_t * n_f - 1)

    start(0, x)
    loads[2].wait()
    loads[3].wait()
    await_arrivals(0, x)
    forward_taps(0, x.at[0], xf1, True)
    pre[...] = apply(xf1, k1, 0)
    backward_taps(0, x.at[1], xb, True)
    back[...] = apply(xb, k2, 1)
    await_seam(0, x)
    forward_late(0, xf1, k1, pre)
    backward_late(0, xb, k2, back)
    value, slope = gelu_parts(pre[...])
    unflat(value.astype(BF16), hidden)
    cot = (back[...] * slope).astype(BF16)
    unflat(cot, pre_grad)
    one, two = Sum(0, w1_o), Sum(1, w2_o)
    cells = flat(hidden)
    pack([product(cells, xb[n].astype(BF16), 0, 0) * scale for n in range(9)], 1)
    two.advance()
    pack([product(xf1[n], cot, 0, 0) * scale for n in range(9)], 0)
    one.advance()
    two.advance()
    one.advance()
    stage(1, 0, y)
    stage(1, 1, y)
    start(1, y)
    two.advance()
    one.advance()
    two.advance()
    one.advance()
    await_arrivals(1, y)
    await_seam(1, y)
    forward_taps(1, hidden, xf2, False)
    channel_major(apply(xf2, k2, 0), res_o)
    backward_taps(1, pre_grad, xb, False)
    channel_major(apply(xb, k1, 1), fg_o)
    while not (one.over and two.over):
        two.advance()
        one.advance()
    await_sends(0, x)
    await_sends(1, y)


def deliver(*refs):
    sources, targets, sems = refs[0:4], refs[4:8], refs[8]
    moves = [pltpu.make_async_copy(a, b, sems.at[n]) for n, (a, b) in enumerate(zip(sources, targets))]
    for move in moves:
        move.start()
    for move in moves:
        move.wait()


def plan(n_t, n_f):
    tile_bits = [("tile", 1 << i) for i in range(n_t.bit_length() - 1)]
    face_bits = [("face", 1 << i) for i in range(n_f.bit_length() - 1)]
    groups = [(tile_bits[:1], 1, 0)]
    middle, rest = face_bits + tile_bits[1:3], tile_bits[3:]
    while middle:
        groups.append((middle[:3], 0, 0))
        middle = middle[3:]
    while len(rest) > 2:
        groups.append((rest[:2], 0, 0))
        rest = rest[2:]
    if rest:
        groups.append((rest, 0, 1))
    return groups


def run(fields, upstream, k1, k2, n_t, n_f):
    C, G, J, H = fields.shape
    S = H // 3
    E = J + 2
    M = G * J * H
    scale = 1.0 / (S * 12.0 ** 0.5)
    groups = plan(n_t, n_f)
    cuts, stages = 1, 0
    for bits, full, whole in groups:
        cuts *= 1 if whole else 2 ** len(bits)
        stages += 1 if whole else 2
    blocks = -(-9 * C // LANES) * (C // 16)
    blocks = -(-blocks // cuts) * cuts
    length, room = blocks, [1, 1]
    for bits, full, whole in groups:
        members = 2 ** len(bits)
        if whole:
            room[full] += length * members
        else:
            length //= members
            room[full] += length * (members - 1)
    dma = pltpu.SemaphoreType.DMA
    vmem = pl.BlockSpec(memory_space=pltpu.VMEM)
    hbm = pl.BlockSpec(memory_space=pltpu.HBM)
    held = [pltpu.with_memory_space_constraint(a, pltpu.HBM) for a in (fields, upstream, k1, k2)]
    return pl.pallas_call(
        functools.partial(body, n_t, n_f, scale, groups),
        out_shape=(
            jax.ShapeDtypeStruct((C, G, J, H), BF16),
            jax.ShapeDtypeStruct((C, G, J, H), BF16),
            jax.ShapeDtypeStruct((3, 3, C, C), F32),
            jax.ShapeDtypeStruct((3, 3, C, C), F32),
        ),
        in_specs=[hbm] * 4,
        out_specs=[vmem] * 4,
        scratch_shapes=[
            pltpu.VMEM((2, C, G, J, H), BF16),
            pltpu.VMEM((2, G, J, H, C), BF16),
            pltpu.VMEM(k1.shape, BF16),
            pltpu.VMEM(k2.shape, BF16),
            pltpu.VMEM((2, G, J, H, C), BF16),
            pltpu.VMEM((2, 2, 2, G, J, C), F32),
            pltpu.VMEM((2, 2, G, H, C), BF16),
            pltpu.VMEM((2, 2, G, H, C), BF16),
            pltpu.VMEM((2, 2, G, E, C), F32),
            pltpu.VMEM((2, 2, G, E, C), F32),
            pltpu.VMEM((2, n_t, 2, G, E, C), F32),
            pltpu.VMEM((2, n_t, 2, G, J, C), F32),
            pltpu.VMEM((2, n_t, 2, G, J, C), F32),
            pltpu.VMEM((2, G, S + 16, C), F32),
            pltpu.VMEM((2, G, S + 16, C), F32),
            pltpu.VMEM((2, G, S + 32, C), F32),
            pltpu.VMEM((G, J + 2, H + 16, C), F32),
            pltpu.VMEM((9, M, C), F32),
            pltpu.VMEM((9, M, C), BF16),
            pltpu.VMEM((9, M, C), BF16),
            pltpu.VMEM((M, C), F32),
            pltpu.VMEM((M, C), F32),
            pltpu.VMEM((2, blocks, 16, LANES), F32),
            pltpu.VMEM((2, blocks, 16, LANES), BF16),
            pltpu.VMEM((2, room[0], 16, LANES), BF16),
            pltpu.VMEM((2, room[1], 16, LANES), F32),
            pltpu.VMEM((2, blocks, 16, LANES), BF16),
            dma((2, 4)), dma((2, 4)),
            dma((2, 2)), dma((2, 2)), dma((2, 2)),
            dma((2, 2)), dma((2, 2)), dma((2, 2)),
            dma((2, stages)), dma((2, stages)), dma((4,)),
        ],
        compiler_params=pltpu.CompilerParams(
            collective_id=0, has_side_effects=True, vmem_limit_bytes=24 * 1024 * 1024),
    )(*held)


def send_out(made):
    vmem = pl.BlockSpec(memory_space=pltpu.VMEM)
    hbm = pl.BlockSpec(memory_space=pltpu.HBM)
    return pl.pallas_call(
        deliver,
        out_shape=[jax.ShapeDtypeStruct(a.shape, a.dtype) for a in made],
        in_specs=[vmem] * 4,
        out_specs=[hbm] * 4,
        scratch_shapes=[pltpu.SemaphoreType.DMA((4,))],
    )(*[pltpu.with_memory_space_constraint(a, pltpu.VMEM) for a in made])


def on_device(n_sub, n_t, n_f, fields, upstream, k1, k2):
    own = fields.shape[0]
    if n_sub > 1:
        fields = lax.all_gather(fields, "sub", axis=0, tiled=True)
        upstream = lax.all_gather(upstream, "sub", axis=0, tiled=True)
    made = run(fields, upstream, k1, k2, n_t, n_f)
    if n_sub > 1:
        at = lax.axis_index("sub") * own
        res, fgrad, w1, w2 = made
        return (
            lax.dynamic_slice_in_dim(res, at, own, 0),
            lax.dynamic_slice_in_dim(fgrad, at, own, 0),
            lax.dynamic_slice_in_dim(w1, at, own, 3),
            lax.dynamic_slice_in_dim(w2, at, own, 3),
        )
    return tuple(send_out(made))


def solution(mesh):
    placed = (P("sub", "face", "tile", "parts"), P("sub", "face", "tile", "parts"), P(), P())
    sizes = mesh.shape
    return jax.shard_map(
        functools.partial(on_device, sizes["sub"], sizes["tile"], sizes["face"]),
        mesh=mesh,
        in_specs=placed,
        out_specs=(
            P("sub", "face", "tile", "parts"),
            P("sub", "face", "tile", "parts"),
            P("parts", None, None, "sub"),
            P("parts", None, None, "sub"),
        ),
        check_vma=False,
    )
```

```python
import functools

import jax
import jax.numpy as jnp
from jax import lax
from jax.experimental import pallas as pl
from jax.experimental.pallas import tpu as pltpu
from jax.sharding import PartitionSpec as P

MESH = pl.DeviceIdType.MESH
F32 = jnp.float32
BF16 = jnp.bfloat16
LANES = 128


def gelu_parts(v):
    root = 0.7978845608028654
    cube = 0.044715 * (v * v * v)
    th = jnp.tanh(root * (v + cube))
    value = v * (0.5 * (1.0 + th))
    slope = 0.5 * (1.0 + th) + 0.5 * v * (1.0 - th * th) * root * (1.0 + 0.134145 * (v * v))
    return value, slope


def product(a, b, da, db):
    return lax.dot_general(a, b, (((da,), (db,)), ((), ())), preferred_element_type=F32)


def body(n_t, n_f, scale, groups, fields_h, upstream_h, k1_h, k2_h, res_o, fg_o, w1_o, w2_o,
         raw, x, k1, k2, y, rows, lh, rh, ap, bm, aps, tr, dr, tl, dl, al, pad, xb, xf1, xf2, xc, kf, kb, pre, back,
         acc, sbuf, rlow, rfull, obuf,
         col_s, col_r, line_s, a_r, b_r, t_s, d_s, row_r, w_s, w_r):
    _, G, J, H, C = x.shape
    S = H // 3
    E = J + 2
    W = xc.shape[1] // 9
    t = lax.axis_index("tile")
    f = lax.axis_index("face")
    fn = lax.rem(f + 1, n_f)
    fp = lax.rem(f + n_f - 1, n_f)
    first = t == 0
    last = t == n_t - 1
    inner_left = jnp.logical_not(first)
    inner_right = jnp.logical_not(last)

    upper, lower = slice(S - 16, H), slice(0, 2 * S + 16)

    def where_to(tile, face):
        return {"tile": tile, "face": face}

    def remote(src, dst, s, r, dev):
        return pltpu.make_async_remote_copy(
            src_ref=src, dst_ref=dst, send_sem=s, recv_sem=r, device_id=dev, device_id_type=MESH)

    def settle(ref, sem):
        pltpu.make_async_copy(ref, ref, sem).wait()

    def copies(p, src):
        c0, cl = src.at[:, :, 0], src.at[:, :, J - 1]
        right = lambda: remote(cl, lh.at[p], col_s.at[0], col_r.at[p, 0], where_to(jnp.minimum(t + 1, n_t - 1), f))
        left = lambda: remote(c0, rh.at[p], col_s.at[1], col_r.at[p, 1], where_to(jnp.maximum(t - 1, 0), f))
        seam = []
        if G > 1:
            seam.append((first, lambda: remote(src.at[:, 1:G, 0, upper], rh.at[p, :, 0:G - 1, upper], col_s.at[1], col_r.at[p, 1], where_to(n_t - 1, f))))
            seam.append((last, lambda: remote(src.at[:, 0:G - 1, J - 1, lower], lh.at[p, :, 1:G, lower], col_s.at[0], col_r.at[p, 0], where_to(0, f))))
        seam.append((first, lambda: remote(src.at[:, 0:1, 0, upper], rh.at[p, :, G - 1:G, upper], col_s.at[1], col_r.at[p, 1], where_to(n_t - 1, fp))))
        seam.append((last, lambda: remote(src.at[:, G - 1:G, J - 1, lower], lh.at[p, :, 0:1, lower], col_s.at[0], col_r.at[p, 0], where_to(0, fn))))
        a_own = lambda d: remote(aps.at[p, d, :, 1:G], ap.at[p, :, 0:G - 1], line_s.at[0], a_r.at[p], where_to(d, f))
        a_oth = lambda d: remote(aps.at[p, d, :, 0:1], ap.at[p, :, G - 1:G], line_s.at[1], a_r.at[p], where_to(d, fp))
        b_own = lambda d: remote(aps.at[p, d, :, 0:G - 1], bm.at[p, :, 1:G], line_s.at[0], b_r.at[p], where_to(d, f))
        b_oth = lambda d: remote(aps.at[p, d, :, G - 1:G], bm.at[p, :, 0:1], line_s.at[1], b_r.at[p], where_to(d, fn))
        t_own = lambda d: remote(rows.at[p, 0, :, 0:G - 1], tr.at[p, d, :, 1:G], t_s.at[0], row_r.at[p, 0], where_to(0, f))
        t_oth = lambda d: remote(rows.at[p, 0, :, G - 1:G], tr.at[p, d, :, 0:1], t_s.at[0], row_r.at[p, 1], where_to(0, fn))
        d_own = lambda d: remote(rows.at[p, 1, :, 1:G], dr.at[p, d, :, 0:G - 1], d_s.at[0], row_r.at[p, 0], where_to(n_t - 1, f))
        d_oth = lambda d: remote(rows.at[p, 1, :, 0:1], dr.at[p, d, :, G - 1:G], d_s.at[0], row_r.at[p, 1], where_to(n_t - 1, fp))
        return right, left, seam, a_own, a_oth, b_own, b_oth, t_own, t_oth, d_own, d_oth

    def stage(p, kind, src):
        for q in range(G):
            for j in range(J):
                rows[p, 0, kind, q, j:j + 1, :] = src[kind, q, j, 0:16].astype(F32)[0:1]
                rows[p, 1, kind, q, j:j + 1, :] = src[kind, q, j, H - 16:H].astype(F32)[15:16]
        more = 16 * kind

        @pl.when(first)
        def _():
            for q in range(G):
                al[kind, q, 16:16 + S + more, :] = src[kind, q, 0, 0:S + more].astype(F32)
            for d in range(n_t):
                aps[p, d, kind] = al[kind, :, 15 + d * J:15 + d * J + E, :]

        @pl.when(last)
        def _():
            for q in range(G):
                al[kind, q, 16 - more:16 + S, :] = src[kind, q, J - 1, 2 * S - more:H].astype(F32)
            for d in range(n_t):
                aps[p, d, kind] = al[kind, :, 15 + d * J:15 + d * J + E, :]

    def start_far(p, src):
        right, left, seam, a_own, a_oth, b_own, b_oth, t_own, t_oth, d_own, d_oth = copies(p, src)

        @pl.when(first)
        def _():
            @pl.loop(0, n_t)
            def _(d):
                a_oth(n_t - 1 - d).start()
            if G > 1:
                @pl.loop(1, n_t)
                def _(d):
                    a_own(n_t - d).start()
                ap[p, :, 0:G - 1] = aps[p, 0, :, 1:G]
                tr[p, 0, :, 1:G] = rows[p, 0, :, 0:G - 1]

        @pl.when(last)
        def _():
            @pl.loop(0, n_t)
            def _(d):
                b_oth(d).start()
            if G > 1:
                @pl.loop(0, n_t - 1)
                def _(d):
                    b_own(d).start()
                bm[p, :, 1:G] = aps[p, n_t - 1, :, 0:G - 1]
                dr[p, n_t - 1, :, 0:G - 1] = rows[p, 1, :, 1:G]

        for cond, make in seam:
            @pl.when(cond)
            def _(make=make):
                make().start()
        t_oth(t).start()
        d_oth(t).start()
        if G > 1:
            @pl.when(inner_left)
            def _():
                t_own(t).start()

            @pl.when(inner_right)
            def _():
                d_own(t).start()

    def start_near(p, src):
        right, left = copies(p, src)[0:2]

        @pl.when(inner_right)
        def _():
            right().start()

        @pl.when(inner_left)
        def _():
            left().start()

    def await_arrivals(p, src):
        right, left = copies(p, src)[0:2]

        @pl.when(inner_left)
        def _():
            right().wait_recv()
            settle(ap.at[p], a_r.at[p])

        @pl.when(first)
        def _():
            settle(ap.at[p, :, G - 1:G], a_r.at[p])

        @pl.when(inner_right)
        def _():
            left().wait_recv()
            settle(bm.at[p], b_r.at[p])

        @pl.when(last)
        def _():
            settle(bm.at[p, :, 0:1], b_r.at[p])

    def await_seam(p):
        @pl.when(last)
        def _():
            settle(rh.at[p, :, :, upper], col_r.at[p, 1])

        @pl.when(first)
        def _():
            settle(lh.at[p, :, :, lower], col_r.at[p, 0])

        @pl.when(first)
        def _():
            if G > 1:
                settle(tr.at[p, 1:n_t, :, 1:G], row_r.at[p, 0])
            settle(tr.at[p, :, :, 0:1], row_r.at[p, 1])
            for d in range(n_t):
                tl[:, :, 8 + d * J:8 + (d + 1) * J, :] = tr[p, d]

        @pl.when(last)
        def _():
            if G > 1:
                settle(dr.at[p, 0:n_t - 1, :, 0:G - 1], row_r.at[p, 0])
            settle(dr.at[p, :, :, G - 1:G], row_r.at[p, 1])
            for d in range(n_t):
                dl[:, :, 8 + d * J:8 + (d + 1) * J, :] = dr[p, d]

    def await_sends(p, src):
        right, left = copies(p, src)[0:2]

        @pl.when(inner_right)
        def _():
            right().wait_send()
            settle(rows.at[p, 1], d_s.at[0])

        @pl.when(last)
        def _():
            settle(src.at[:, :, J - 1, lower], col_s.at[0])
            settle(rows.at[p, 1, :, 0:1], d_s.at[0])

        @pl.when(inner_left)
        def _():
            left().wait_send()
            settle(rows.at[p, 0], t_s.at[0])

        @pl.when(first)
        def _():
            settle(src.at[:, :, 0, upper], col_s.at[1])
            settle(rows.at[p, 0, :, G - 1:G], t_s.at[0])

        @pl.when(jnp.logical_or(first, last))
        def _():
            if G > 1:
                settle(aps.at[p, 1:n_t, :, 1:G], line_s.at[0])
            settle(aps.at[p, :, :, 0:1], line_s.at[1])

    def fill_columns(src):
        for q in range(G):
            for j in range(J):
                pad[q, 1 + j, 8:8 + H, :] = src[q, j].astype(F32)

    def forward_taps(p, src, out, late):
        fill_columns(src)
        for q in range(G):
            @pl.when(inner_left)
            def _():
                pad[q, 0, 8:8 + H, :] = lh[p, 0, q].astype(F32)

            @pl.when(inner_right)
            def _():
                pad[q, J + 1, 8:8 + H, :] = rh[p, 0, q].astype(F32)

            if late:
                @pl.when(first)
                def _():
                    pad[q, 0, 8:8 + H, :] = jnp.zeros((H, C), F32)

                @pl.when(last)
                def _():
                    pad[q, J + 1, 8:8 + H, :] = jnp.zeros((H, C), F32)
            else:
                @pl.when(first)
                def _():
                    forward_edge(p, q, 0)

                @pl.when(last)
                def _():
                    forward_edge(p, q, J + 1)
            for j in range(E):
                pad[q, j, 7:8, :] = ap[p, 0, q, j:j + 1]
                pad[q, j, 8 + H:9 + H, :] = bm[p, 0, q, j:j + 1]
        for a in range(3):
            for b in range(3):
                for q in range(G):
                    for j in range(J):
                        m = (q * J + j) * H
                        n = 3 * a + b
                        out[m:m + H, n * W:n * W + C] = pad[q, j + a, 7 + b:7 + b + H, :].astype(BF16)

    def forward_edge(p, q, j):
        if j == 0:
            pad[q, 0, 8:8 + S, :] = tl[0, q, 8:8 + S, :]
            pad[q, 0, 8 + S:8 + H, :] = lh[p, 0, q, 0:2 * S].astype(F32)
        else:
            pad[q, J + 1, 8:8 + 2 * S, :] = rh[p, 0, q, S:H].astype(F32)
            pad[q, J + 1, 8 + 2 * S:8 + H, :] = dl[0, q, 8:8 + S, :]

    def forward_late(p, out, k, total):
        for cond, a, j in ((first, 0, 0), (last, 2, J + 1)):
            @pl.when(cond)
            def _(a=a, j=j):
                for q in range(G):
                    forward_edge(p, q, j)
                    pad[q, j, 7:8, :] = jnp.zeros((1, C), F32)
                    pad[q, j, 8 + H:9 + H, :] = jnp.zeros((1, C), F32)
                    m = (q * J + j - a) * H
                    more = total[m:m + H, :]
                    for b in range(3):
                        tap = pad[q, j, 7 + b:7 + b + H, :].astype(BF16)
                        n = 3 * a + b
                        more = more + product(tap, k[n * W:n * W + C], 1, 0)
                        out[m:m + H, n * W:n * W + C] += tap
                    total[m:m + H, :] = more

    def backward_taps(p, src, out, late):
        fill_columns(src)
        for q in range(G):
            @pl.when(inner_left)
            def _():
                pad[q, 0, 8:8 + H, :] = lh[p, 1, q].astype(F32)

            @pl.when(first)
            def _():
                pad[q, 0, :, :] = jnp.zeros((H + 16, C), F32)

            @pl.when(inner_right)
            def _():
                pad[q, J + 1, 8:8 + H, :] = rh[p, 1, q].astype(F32)

            @pl.when(last)
            def _():
                pad[q, J + 1, :, :] = jnp.zeros((H + 16, C), F32)
            for j in range(E):
                pad[q, j, 7:8, :] = jnp.zeros((1, C), F32)
                pad[q, j, 8 + H:9 + H, :] = jnp.zeros((1, C), F32)
        for a in range(3):
            for b in range(3):
                for q in range(G):
                    for j in range(J):
                        m = (q * J + j) * H
                        out[3 * a + b, m:m + H, :] = pad[q, j - a + 2, 9 - b:9 - b + H, :]
        for q in range(G):
            top = ap[p, 1, q]
            low = bm[p, 1, q]
            for b in range(3):
                for j in range(J):
                    m = (q * J + j) * H
                    out[b, m:m + 1, :] += top[j + 2 - b:j + 3 - b]
                    out[6 + b, m + H - 1:m + H, :] += low[j + 2 - b:j + 3 - b]
        if not late:
            backward_late(p, out, None, None)
        for n in range(9):
            xc[:, n * W:n * W + C] = out[n].astype(BF16)

    def backward_late(p, out, k, total):
        def add(n, m, rows_at, value):
            here = slice(m + rows_at.start, m + rows_at.stop)
            out[n, here, :] += value
            if total is not None:
                xc[here, n * W:n * W + C] = out[n, here, :].astype(BF16)
                total[here, :] += product(value.astype(BF16), k[n * W:n * W + C], 1, 0)

        @pl.when(last)
        def _():
            for q in range(G):
                m = (q * J + J - 1) * H
                pad[q, J + 1, 8:8 + H, :] = rh[p, 1, q].astype(F32)
                pad[q, J + 1, 8 + H:9 + H, :] = jnp.zeros((1, C), F32)
                for e in range(3):
                    add(e, m, slice(0, 2 * S), pad[q, J + 1, 8 + S + 1 - e:8 + H + 1 - e, :])
                    add(3 * e + 2, m, slice(2 * S, H), dl[1, q, 9 - e:9 - e + S, :])

        @pl.when(first)
        def _():
            for q in range(G):
                m = q * J * H
                pad[q, 0, 7:8, :] = jnp.zeros((1, C), F32)
                pad[q, 0, 8:8 + H, :] = lh[p, 1, q].astype(F32)
                for e in range(3):
                    add(3 * e, m, slice(0, S), tl[1, q, 9 - e:9 - e + S, :])
                    add(6 + e, m, slice(S, H), pad[q, 0, 9 - e:9 - e + 2 * S, :])

    def lay_out(k, w):
        for n in range(9):
            tap = k[n // 3, n % 3]
            kf[w, n * W:n * W + C] = tap
            kb[w, n * W:n * W + C] = tap.astype(F32).T.astype(BF16)
            if W > C:
                kf[w, n * W + C:n * W + W] = jnp.zeros((W - C, C), BF16)
                kb[w, n * W + C:n * W + W] = jnp.zeros((W - C, C), BF16)

    def apply(taps, k):
        return product(taps[...], k[...], 1, 0)

    def unflat(value, dst):
        for q in range(G):
            for j in range(J):
                m = (q * J + j) * H
                dst[q, j] = value[m:m + H]

    def channel_major(value, dst):
        for q in range(G):
            for j in range(J):
                m = (q * J + j) * H
                dst[:, q, j, :] = value[m:m + H].T.astype(BF16)

    per = C // 16
    tiles = -(-9 * C // LANES)
    blocks = acc.shape[1]

    def pack(terms, w):
        spare = tiles * LANES - 9 * C
        wide = jnp.concatenate(terms + ([jnp.zeros((C, spare), F32)] if spare else []), axis=1)
        for n in range(tiles):
            acc[w, n * per:(n + 1) * per] = wide[:, n * LANES:(n + 1) * LANES].reshape(per, 16, LANES)

    def unpack(w, out):
        parts = [obuf[w, n * per:(n + 1) * per].astype(F32).reshape(C, LANES) for n in range(tiles)]
        wide = jnp.concatenate(parts, axis=1)
        for n in range(9):
            out[n // 3, n % 3] = wide[:, n * C:(n + 1) * C]

    class Sum:
        def __init__(self, w, out):
            self.out, self.at, self.over = out, 0, False
            self.w, self.lo, self.length, self.done = w, 0, blocks, []
            self.used = [0, 0]
            self.sem = 0

        def members(self, bits):
            mine = []
            for axis, s in bits:
                mine.append(lax.rem((t if axis == "tile" else f) // s, 2))
            found = []
            for k in reversed(range(1, 2 ** len(bits))):
                tile, face, digit = t, f, 0
                for pos, (axis, s) in enumerate(bits):
                    bit = mine[pos]
                    if (k >> pos) & 1:
                        if axis == "tile":
                            tile = tile + (1 - 2 * bit) * s
                        else:
                            face = face + (1 - 2 * bit) * s
                        bit = 1 - bit
                    digit = digit + bit * (1 << pos)
                found.append((digit, where_to(tile, face)))
            own = 0
            for pos, bit in enumerate(mine):
                own = own + bit * (1 << pos)
            return own, found

        def begin(self, n):
            bits, full, whole = groups[n]
            own, found = self.members(bits)
            w = self.w
            inbox = rfull if full else rlow
            at = self.used[full]
            part = self.length if whole else self.length // (len(found) + 1)
            self.flying = (inbox, at, part, len(found), whole)
            if whole:
                piece = pl.ds(self.lo, part)
                mine = pl.ds(at + own * part, part)
                sbuf[w, piece] = acc[w, piece].astype(BF16)
                for digit, dev in found:
                    remote(sbuf.at[w, piece], inbox.at[w, mine], w_s.at[w], w_r.at[w, self.sem], dev).start()
                inbox[w, mine] = sbuf[w, piece]
                self.used[full] += part * (len(found) + 1)
                return
            for digit, dev in found:
                give = self.lo + digit * part
                if full:
                    out = acc.at[w, pl.ds(give, part)]
                else:
                    sbuf[w, pl.ds(give, part)] = acc[w, pl.ds(give, part)].astype(BF16)
                    out = sbuf.at[w, pl.ds(give, part)]
                at = self.used[full]
                self.used[full] += part
                remote(out, inbox.at[w, at:at + part], w_s.at[w], w_r.at[w, self.sem], dev).start()
            keep = self.lo + own * part
            self.done.append((keep, part, found))
            self.lo, self.length = keep, part

        def end(self):
            inbox, at, part, count, whole = self.flying
            sent = inbox.at[self.w, at:at + count * part]
            settle(sent, w_s.at[self.w])
            settle(sent, w_r.at[self.w, self.sem])
            self.sem += 1
            terms = [inbox[self.w, at + n * part:at + (n + 1) * part].astype(F32) for n in range(count + whole)]
            total = terms.pop(0) if whole else acc[self.w, pl.ds(self.lo, self.length)]
            for term in terms:
                total = total + term
            acc[self.w, pl.ds(self.lo, self.length)] = total

        def round(self):
            obuf[self.w, pl.ds(self.lo, self.length)] = acc[self.w, pl.ds(self.lo, self.length)].astype(BF16)

        def give(self):
            keep, part, found = self.done.pop()
            self.flying = (part, len(found))
            for digit, dev in found:
                remote(obuf.at[self.w, pl.ds(keep, part)], obuf.at[self.w, pl.ds(keep, part)],
                       w_s.at[self.w], w_r.at[self.w, self.sem], dev).start()

        def given(self):
            part, count = self.flying
            whole = obuf.at[self.w, 0:count * part]
            settle(whole, w_s.at[self.w])
            settle(whole, w_r.at[self.w, self.sem])
            self.sem += 1

        def advance(self):
            at, count = self.at, len(groups)
            self.at += 1
            if self.over:
                return
            if at < count:
                if at > 0:
                    self.end()
                self.begin(at)
                return
            if at == count:
                self.end()
                self.round()
            else:
                self.given()
            if self.done:
                self.give()
            else:
                unpack(self.w, self.out)
                self.over = True

    barrier = pltpu.get_barrier_semaphore()
    loads = [pltpu.make_async_copy(src, dst, sem) for src, dst, sem in (
        (fields_h, raw.at[0], w_s.at[0]), (upstream_h, raw.at[1], w_s.at[1]),
        (k1_h, k1, line_s.at[0]), (k2_h, k2, line_s.at[1]))]
    for load in loads:
        load.start()

    @pl.loop(0, n_f)
    def _(df):
        @pl.loop(0, n_t)
        def _(dt):
            @pl.when(jnp.logical_or(df != f, dt != t))
            def _():
                pl.semaphore_signal(barrier, inc=1, device_id=where_to(dt, df), device_id_type=MESH)
    hidden, pre_grad = y.at[0], y.at[1]
    al[...] = jnp.zeros_like(al)
    tl[...] = jnp.zeros_like(tl)
    dl[...] = jnp.zeros_like(dl)
    for kind in range(2):
        loads[kind].wait()
        for q in range(G):
            for j in range(J):
                x[kind, q, j] = raw[kind, :, q, j, :].astype(F32).T.astype(BF16)
        stage(0, kind, x)
    if blocks > tiles * per:
        for w in range(2):
            acc[w, tiles * per:blocks] = jnp.zeros((blocks - tiles * per, 16, LANES), F32)
    pl.semaphore_wait(barrier, n_t * n_f - 1)

    loads[2].wait()
    loads[3].wait()
    start_far(0, x)
    start_near(0, x)
    lay_out(k1, 0)
    lay_out(k2, 1)
    for taps in (xf1, xf2, xc):
        taps[...] = jnp.zeros_like(taps)
    await_arrivals(0, x)
    forward_taps(0, x.at[0], xf1, True)
    pre[...] = apply(xf1, kf.at[0])
    backward_taps(0, x.at[1], xb, True)
    back[...] = apply(xc, kb.at[1])
    await_seam(0)
    forward_late(0, xf1, kf.at[0], pre)
    backward_late(0, xb, kb.at[1], back)
    value, slope = gelu_parts(pre[...])
    cells = value.astype(BF16)
    unflat(cells, hidden)
    one, two = Sum(0, w1_o), Sum(1, w2_o)
    wide = product(cells, xc[...], 0, 0)
    pack([wide[:, n * W:n * W + C] * scale for n in range(9)], 1)
    two.advance()
    cot = (back[...] * slope).astype(BF16)
    unflat(cot, pre_grad)
    pack([product(xf1[:, n * W:n * W + C], cot, 0, 0) * scale for n in range(9)], 0)
    one.advance()
    two.advance()
    one.advance()
    await_sends(0, x)
    stage(1, 0, y)
    stage(1, 1, y)
    start_far(1, y)
    two.advance()
    one.advance()
    start_near(1, y)
    two.advance()
    one.advance()
    await_arrivals(1, y)
    await_seam(1)
    forward_taps(1, hidden, xf2, False)
    channel_major(apply(xf2, kf.at[1]), res_o)
    backward_taps(1, pre_grad, xb, False)
    channel_major(apply(xc, kb.at[0]), fg_o)
    while not (one.over and two.over):
        two.advance()
        one.advance()
    await_sends(1, y)


def deliver(*refs):
    sources, targets, sems = refs[0:4], refs[4:8], refs[8]
    moves = [pltpu.make_async_copy(a, b, sems.at[n]) for n, (a, b) in enumerate(zip(sources, targets))]
    for move in moves:
        move.start()
    for move in moves:
        move.wait()


def plan(n_t, n_f):
    tile_bits = [("tile", 1 << i) for i in range(n_t.bit_length() - 1)]
    face_bits = [("face", 1 << i) for i in range(n_f.bit_length() - 1)]
    groups = [(tile_bits[:1], 1, 0)]
    middle, rest = face_bits + tile_bits[1:3], tile_bits[3:]
    while middle:
        groups.append((middle[:3], 0, 0))
        middle = middle[3:]
    while len(rest) > 2:
        groups.append((rest[:2], 0, 0))
        rest = rest[2:]
    if rest:
        groups.append((rest, 0, 1))
    return groups


def run(fields, upstream, k1, k2, n_t, n_f):
    C, G, J, H = fields.shape
    S = H // 3
    E = J + 2
    M = G * J * H
    W = -(-C // LANES) * LANES
    scale = 1.0 / (S * 12.0 ** 0.5)
    groups = plan(n_t, n_f)
    cuts, stages = 1, 0
    for bits, full, whole in groups:
        cuts *= 1 if whole else 2 ** len(bits)
        stages += 1 if whole else 2
    blocks = -(-9 * C // LANES) * (C // 16)
    blocks = -(-blocks // cuts) * cuts
    length, room = blocks, [1, 1]
    for bits, full, whole in groups:
        members = 2 ** len(bits)
        if whole:
            room[full] += length * members
        else:
            length //= members
            room[full] += length * (members - 1)
    dma = pltpu.SemaphoreType.DMA
    vmem = pl.BlockSpec(memory_space=pltpu.VMEM)
    hbm = pl.BlockSpec(memory_space=pltpu.HBM)
    held = [pltpu.with_memory_space_constraint(a, pltpu.HBM) for a in (fields, upstream, k1, k2)]
    return pl.pallas_call(
        functools.partial(body, n_t, n_f, scale, groups),
        out_shape=(
            jax.ShapeDtypeStruct((C, G, J, H), BF16),
            jax.ShapeDtypeStruct((C, G, J, H), BF16),
            jax.ShapeDtypeStruct((3, 3, C, C), F32),
            jax.ShapeDtypeStruct((3, 3, C, C), F32),
        ),
        in_specs=[hbm] * 4,
        out_specs=[vmem] * 4,
        scratch_shapes=[
            pltpu.VMEM((2, C, G, J, H), BF16),
            pltpu.VMEM((2, G, J, H, C), BF16),
            pltpu.VMEM(k1.shape, BF16),
            pltpu.VMEM(k2.shape, BF16),
            pltpu.VMEM((2, G, J, H, C), BF16),
            pltpu.VMEM((2, 2, 2, G, J, C), F32),
            pltpu.VMEM((2, 2, G, H, C), BF16),
            pltpu.VMEM((2, 2, G, H, C), BF16),
            pltpu.VMEM((2, 2, G, E, C), F32),
            pltpu.VMEM((2, 2, G, E, C), F32),
            pltpu.VMEM((2, n_t, 2, G, E, C), F32),
            pltpu.VMEM((2, n_t, 2, G, J, C), F32),
            pltpu.VMEM((2, n_t, 2, G, J, C), F32),
            pltpu.VMEM((2, G, S + 16, C), F32),
            pltpu.VMEM((2, G, S + 16, C), F32),
            pltpu.VMEM((2, G, S + 32, C), F32),
            pltpu.VMEM((G, J + 2, H + 16, C), F32),
            pltpu.VMEM((9, M, C), F32),
            pltpu.VMEM((M, 9 * W), BF16),
            pltpu.VMEM((M, 9 * W), BF16),
            pltpu.VMEM((M, 9 * W), BF16),
            pltpu.VMEM((2, 9 * W, C), BF16),
            pltpu.VMEM((2, 9 * W, C), BF16),
            pltpu.VMEM((M, C), F32),
            pltpu.VMEM((M, C), F32),
            pltpu.VMEM((2, blocks, 16, LANES), F32),
            pltpu.VMEM((2, blocks, 16, LANES), BF16),
            pltpu.VMEM((2, room[0], 16, LANES), BF16),
            pltpu.VMEM((2, room[1], 16, LANES), F32),
            pltpu.VMEM((2, blocks, 16, LANES), BF16),
            dma((2,)), dma((2, 2)),
            dma((2,)), dma((2,)), dma((2,)),
            dma((1,)), dma((1,)), dma((2, 2)),
            dma((2,)), dma((2, stages)),
        ],
        compiler_params=pltpu.CompilerParams(
            collective_id=0, has_side_effects=True, vmem_limit_bytes=24 * 1024 * 1024),
    )(*held)


def send_out(made):
    vmem = pl.BlockSpec(memory_space=pltpu.VMEM)
    hbm = pl.BlockSpec(memory_space=pltpu.HBM)
    return pl.pallas_call(
        deliver,
        out_shape=[jax.ShapeDtypeStruct(a.shape, a.dtype) for a in made],
        in_specs=[vmem] * 4,
        out_specs=[hbm] * 4,
        scratch_shapes=[pltpu.SemaphoreType.DMA((4,))],
    )(*[pltpu.with_memory_space_constraint(a, pltpu.VMEM) for a in made])


def on_device(n_sub, n_t, n_f, fields, upstream, k1, k2):
    own = fields.shape[0]
    if n_sub > 1:
        fields = lax.all_gather(fields, "sub", axis=0, tiled=True)
        upstream = lax.all_gather(upstream, "sub", axis=0, tiled=True)
    made = run(fields, upstream, k1, k2, n_t, n_f)
    if n_sub > 1:
        at = lax.axis_index("sub") * own
        res, fgrad, w1, w2 = made
        return (
            lax.dynamic_slice_in_dim(res, at, own, 0),
            lax.dynamic_slice_in_dim(fgrad, at, own, 0),
            lax.dynamic_slice_in_dim(w1, at, own, 3),
            lax.dynamic_slice_in_dim(w2, at, own, 3),
        )
    return tuple(send_out(made))


def solution(mesh):
    placed = (P("sub", "face", "tile", "parts"), P("sub", "face", "tile", "parts"), P(), P())
    sizes = mesh.shape
    return jax.shard_map(
        functools.partial(on_device, sizes["sub"], sizes["tile"], sizes["face"]),
        mesh=mesh,
        in_specs=placed,
        out_specs=(
            P("sub", "face", "tile", "parts"),
            P("sub", "face", "tile", "parts"),
            P("parts", None, None, "sub"),
            P("parts", None, None, "sub"),
        ),
        check_vma=False,
    )
```

```python
import functools

import jax
import jax.numpy as jnp
from jax import lax
from jax.experimental import pallas as pl
from jax.experimental.pallas import tpu as pltpu
from jax.sharding import PartitionSpec as P

MESH = pl.DeviceIdType.MESH
F32 = jnp.float32
BF16 = jnp.bfloat16
LANES = 128


def gelu_parts(v):
    root = 0.7978845608028654
    cube = 0.044715 * (v * v * v)
    th = jnp.tanh(root * (v + cube))
    value = v * (0.5 * (1.0 + th))
    slope = 0.5 * (1.0 + th) + 0.5 * v * (1.0 - th * th) * root * (1.0 + 0.134145 * (v * v))
    return value, slope


def product(a, b, da, db):
    return lax.dot_general(a, b, (((da,), (db,)), ((), ())), preferred_element_type=F32)


def body(n_t, n_f, scale, groups, fields_h, upstream_h, k1_h, k2_h, res_o, fg_o, w1_o, w2_o,
         raw, x, k1, k2, y, rows, lh, rh, ap, bm, aps, tr, dr, tl, dl, al, pad, xb, xf1, xf2, xc, kf, kb, kl, lm, pad2, pre, back,
         acc, sbuf, rlow, rfull, obuf,
         col_s, col_r, line_s, a_r, b_r, t_s, d_s, row_r, w_s, w_r):
    _, G, J, H, C = x.shape
    S = H // 3
    E = J + 2
    W = xc.shape[1] // 9
    t = lax.axis_index("tile")
    f = lax.axis_index("face")
    fn = lax.rem(f + 1, n_f)
    fp = lax.rem(f + n_f - 1, n_f)
    first = t == 0
    last = t == n_t - 1
    inner_left = jnp.logical_not(first)
    inner_right = jnp.logical_not(last)

    upper, lower = slice(S - 16, H), slice(0, 2 * S + 16)

    def where_to(tile, face):
        return {"tile": tile, "face": face}

    def remote(src, dst, s, r, dev):
        return pltpu.make_async_remote_copy(
            src_ref=src, dst_ref=dst, send_sem=s, recv_sem=r, device_id=dev, device_id_type=MESH)

    def settle(ref, sem):
        pltpu.make_async_copy(ref, ref, sem).wait()

    def copies(p, src):
        c0, cl = src.at[:, :, 0], src.at[:, :, J - 1]
        right = lambda: remote(cl, lh.at[p], col_s.at[0], col_r.at[p, 0], where_to(jnp.minimum(t + 1, n_t - 1), f))
        left = lambda: remote(c0, rh.at[p], col_s.at[1], col_r.at[p, 1], where_to(jnp.maximum(t - 1, 0), f))
        seam = []
        if G > 1:
            seam.append((first, lambda: remote(src.at[:, 1:G, 0, upper], rh.at[p, :, 0:G - 1, upper], col_s.at[1], col_r.at[p, 1], where_to(n_t - 1, f))))
            seam.append((last, lambda: remote(src.at[:, 0:G - 1, J - 1, lower], lh.at[p, :, 1:G, lower], col_s.at[0], col_r.at[p, 0], where_to(0, f))))
        seam.append((first, lambda: remote(src.at[:, 0:1, 0, upper], rh.at[p, :, G - 1:G, upper], col_s.at[1], col_r.at[p, 1], where_to(n_t - 1, fp))))
        seam.append((last, lambda: remote(src.at[:, G - 1:G, J - 1, lower], lh.at[p, :, 0:1, lower], col_s.at[0], col_r.at[p, 0], where_to(0, fn))))
        a_own = lambda d: remote(aps.at[p, d, :, 1:G], ap.at[p, :, 0:G - 1], line_s.at[0], a_r.at[p], where_to(d, f))
        a_oth = lambda d: remote(aps.at[p, d, :, 0:1], ap.at[p, :, G - 1:G], line_s.at[1], a_r.at[p], where_to(d, fp))
        b_own = lambda d: remote(aps.at[p, d, :, 0:G - 1], bm.at[p, :, 1:G], line_s.at[0], b_r.at[p], where_to(d, f))
        b_oth = lambda d: remote(aps.at[p, d, :, G - 1:G], bm.at[p, :, 0:1], line_s.at[1], b_r.at[p], where_to(d, fn))
        t_own = lambda d: remote(rows.at[p, 0, :, 0:G - 1], tr.at[p, d, :, 1:G], t_s.at[0], row_r.at[p, 0], where_to(0, f))
        t_oth = lambda d: remote(rows.at[p, 0, :, G - 1:G], tr.at[p, d, :, 0:1], t_s.at[0], row_r.at[p, 1], where_to(0, fn))
        d_own = lambda d: remote(rows.at[p, 1, :, 1:G], dr.at[p, d, :, 0:G - 1], d_s.at[0], row_r.at[p, 0], where_to(n_t - 1, f))
        d_oth = lambda d: remote(rows.at[p, 1, :, 0:1], dr.at[p, d, :, G - 1:G], d_s.at[0], row_r.at[p, 1], where_to(n_t - 1, fp))
        return right, left, seam, a_own, a_oth, b_own, b_oth, t_own, t_oth, d_own, d_oth

    def stage(p, kind, src):
        for q in range(G):
            for j in range(J):
                rows[p, 0, kind, q, j:j + 1, :] = src[kind, q, j, 0:16].astype(F32)[0:1]
                rows[p, 1, kind, q, j:j + 1, :] = src[kind, q, j, H - 16:H].astype(F32)[15:16]
        more = 16 * kind

        @pl.when(first)
        def _():
            for q in range(G):
                al[kind, q, 16:16 + S + more, :] = src[kind, q, 0, 0:S + more].astype(F32)
            for d in range(n_t):
                aps[p, d, kind] = al[kind, :, 15 + d * J:15 + d * J + E, :]

        @pl.when(last)
        def _():
            for q in range(G):
                al[kind, q, 16 - more:16 + S, :] = src[kind, q, J - 1, 2 * S - more:H].astype(F32)
            for d in range(n_t):
                aps[p, d, kind] = al[kind, :, 15 + d * J:15 + d * J + E, :]

    def start_far(p, src):
        right, left, seam, a_own, a_oth, b_own, b_oth, t_own, t_oth, d_own, d_oth = copies(p, src)

        @pl.when(first)
        def _():
            @pl.loop(0, n_t)
            def _(d):
                a_oth(n_t - 1 - d).start()
            if G > 1:
                @pl.loop(1, n_t)
                def _(d):
                    a_own(n_t - d).start()
                ap[p, :, 0:G - 1] = aps[p, 0, :, 1:G]
                tr[p, 0, :, 1:G] = rows[p, 0, :, 0:G - 1]

        @pl.when(last)
        def _():
            @pl.loop(0, n_t)
            def _(d):
                b_oth(d).start()
            if G > 1:
                @pl.loop(0, n_t - 1)
                def _(d):
                    b_own(d).start()
                bm[p, :, 1:G] = aps[p, n_t - 1, :, 0:G - 1]
                dr[p, n_t - 1, :, 0:G - 1] = rows[p, 1, :, 1:G]

        for cond, make in seam:
            @pl.when(cond)
            def _(make=make):
                make().start()
        t_oth(t).start()
        d_oth(t).start()
        if G > 1:
            @pl.when(inner_left)
            def _():
                t_own(t).start()

            @pl.when(inner_right)
            def _():
                d_own(t).start()

    def start_near(p, src):
        right, left = copies(p, src)[0:2]

        @pl.when(inner_right)
        def _():
            right().start()

        @pl.when(inner_left)
        def _():
            left().start()

    def await_arrivals(p, src):
        right, left = copies(p, src)[0:2]

        @pl.when(inner_left)
        def _():
            right().wait_recv()
            settle(ap.at[p], a_r.at[p])

        @pl.when(first)
        def _():
            settle(ap.at[p, :, G - 1:G], a_r.at[p])

        @pl.when(inner_right)
        def _():
            left().wait_recv()
            settle(bm.at[p], b_r.at[p])

        @pl.when(last)
        def _():
            settle(bm.at[p, :, 0:1], b_r.at[p])

    def await_seam(p):
        @pl.when(last)
        def _():
            settle(rh.at[p, :, :, upper], col_r.at[p, 1])

        @pl.when(first)
        def _():
            settle(lh.at[p, :, :, lower], col_r.at[p, 0])

        @pl.when(first)
        def _():
            if G > 1:
                settle(tr.at[p, 1:n_t, :, 1:G], row_r.at[p, 0])
            settle(tr.at[p, :, :, 0:1], row_r.at[p, 1])
            for d in range(n_t):
                tl[:, :, 8 + d * J:8 + (d + 1) * J, :] = tr[p, d]

        @pl.when(last)
        def _():
            if G > 1:
                settle(dr.at[p, 0:n_t - 1, :, 0:G - 1], row_r.at[p, 0])
            settle(dr.at[p, :, :, G - 1:G], row_r.at[p, 1])
            for d in range(n_t):
                dl[:, :, 8 + d * J:8 + (d + 1) * J, :] = dr[p, d]

    def await_sends(p, src):
        right, left = copies(p, src)[0:2]

        @pl.when(inner_right)
        def _():
            right().wait_send()
            settle(rows.at[p, 1], d_s.at[0])

        @pl.when(last)
        def _():
            settle(src.at[:, :, J - 1, lower], col_s.at[0])
            settle(rows.at[p, 1, :, 0:1], d_s.at[0])

        @pl.when(inner_left)
        def _():
            left().wait_send()
            settle(rows.at[p, 0], t_s.at[0])

        @pl.when(first)
        def _():
            settle(src.at[:, :, 0, upper], col_s.at[1])
            settle(rows.at[p, 0, :, G - 1:G], t_s.at[0])

        @pl.when(jnp.logical_or(first, last))
        def _():
            if G > 1:
                settle(aps.at[p, 1:n_t, :, 1:G], line_s.at[0])
            settle(aps.at[p, :, :, 0:1], line_s.at[1])

    def fill_columns(src):
        for q in range(G):
            for j in range(J):
                pad[q, 1 + j, 8:8 + H, :] = src[q, j].astype(F32)

    def forward_taps(p, src, out, late):
        fill_columns(src)
        for q in range(G):
            @pl.when(inner_left)
            def _():
                pad[q, 0, 8:8 + H, :] = lh[p, 0, q].astype(F32)

            @pl.when(inner_right)
            def _():
                pad[q, J + 1, 8:8 + H, :] = rh[p, 0, q].astype(F32)

            if late:
                @pl.when(first)
                def _():
                    pad[q, 0, 8:8 + H, :] = jnp.zeros((H, C), F32)

                @pl.when(last)
                def _():
                    pad[q, J + 1, 8:8 + H, :] = jnp.zeros((H, C), F32)
            else:
                @pl.when(first)
                def _():
                    forward_edge(p, q, 0)

                @pl.when(last)
                def _():
                    forward_edge(p, q, J + 1)
            for j in range(E):
                pad[q, j, 7:8, :] = ap[p, 0, q, j:j + 1]
                pad[q, j, 8 + H:9 + H, :] = bm[p, 0, q, j:j + 1]
        for a in range(3):
            for b in range(3):
                for q in range(G):
                    for j in range(J):
                        m = (q * J + j) * H
                        n = 3 * a + b
                        out[m:m + H, n * W:n * W + C] = pad[q, j + a, 7 + b:7 + b + H, :].astype(BF16)

    def forward_edge(p, q, j):
        if j == 0:
            pad[q, 0, 8:8 + S, :] = tl[0, q, 8:8 + S, :]
            pad[q, 0, 8 + S:8 + H, :] = lh[p, 0, q, 0:2 * S].astype(F32)
        else:
            pad[q, J + 1, 8:8 + 2 * S, :] = rh[p, 0, q, S:H].astype(F32)
            pad[q, J + 1, 8 + 2 * S:8 + H, :] = dl[0, q, 8:8 + S, :]

    def forward_late(p, out, k, total):
        for cond, a, j in ((first, 0, 0), (last, 2, J + 1)):
            @pl.when(cond)
            def _(a=a, j=j):
                for q in range(G):
                    forward_edge(p, q, j)
                    pad[q, j, 7:8, :] = jnp.zeros((1, C), F32)
                    pad[q, j, 8 + H:9 + H, :] = jnp.zeros((1, C), F32)
                    m = (q * J + j - a) * H
                    more = total[m:m + H, :]
                    for b in range(3):
                        tap = pad[q, j, 7 + b:7 + b + H, :].astype(BF16)
                        n = 3 * a + b
                        more = more + product(tap, k[n * W:n * W + C], 1, 0)
                        out[m:m + H, n * W:n * W + C] += tap
                    total[m:m + H, :] = more

    def backward_taps(p, src, out, late):
        fill_columns(src)
        for q in range(G):
            @pl.when(inner_left)
            def _():
                pad[q, 0, 8:8 + H, :] = lh[p, 1, q].astype(F32)

            @pl.when(first)
            def _():
                pad[q, 0, :, :] = jnp.zeros((H + 16, C), F32)

            @pl.when(inner_right)
            def _():
                pad[q, J + 1, 8:8 + H, :] = rh[p, 1, q].astype(F32)

            @pl.when(last)
            def _():
                pad[q, J + 1, :, :] = jnp.zeros((H + 16, C), F32)
            for j in range(E):
                pad[q, j, 7:8, :] = jnp.zeros((1, C), F32)
                pad[q, j, 8 + H:9 + H, :] = jnp.zeros((1, C), F32)
        for a in range(3):
            for b in range(3):
                for q in range(G):
                    for j in range(J):
                        m = (q * J + j) * H
                        out[3 * a + b, m:m + H, :] = pad[q, j - a + 2, 9 - b:9 - b + H, :]
        for q in range(G):
            top = ap[p, 1, q]
            low = bm[p, 1, q]
            for b in range(3):
                for j in range(J):
                    m = (q * J + j) * H
                    out[b, m:m + 1, :] += top[j + 2 - b:j + 3 - b]
                    out[6 + b, m + H - 1:m + H, :] += low[j + 2 - b:j + 3 - b]
        if not late:
            backward_late(p, out, None, None)
        for n in range(9):
            xc[:, n * W:n * W + C] = out[n].astype(BF16)

    def backward_late(p, out, k, total):
        def add(n, m, rows_at, value):
            here = slice(m + rows_at.start, m + rows_at.stop)
            out[n, here, :] += value
            if total is not None:
                xc[here, n * W:n * W + C] = out[n, here, :].astype(BF16)
                total[here, :] += product(value.astype(BF16), k[n * W:n * W + C], 1, 0)

        @pl.when(last)
        def _():
            for q in range(G):
                m = (q * J + J - 1) * H
                pad[q, J + 1, 8:8 + H, :] = rh[p, 1, q].astype(F32)
                pad[q, J + 1, 8 + H:9 + H, :] = jnp.zeros((1, C), F32)
                for e in range(3):
                    add(e, m, slice(0, 2 * S), pad[q, J + 1, 8 + S + 1 - e:8 + H + 1 - e, :])
                    add(3 * e + 2, m, slice(2 * S, H), dl[1, q, 9 - e:9 - e + S, :])

        @pl.when(first)
        def _():
            for q in range(G):
                m = q * J * H
                pad[q, 0, 7:8, :] = jnp.zeros((1, C), F32)
                pad[q, 0, 8:8 + H, :] = lh[p, 1, q].astype(F32)
                for e in range(3):
                    add(3 * e, m, slice(0, S), tl[1, q, 9 - e:9 - e + S, :])
                    add(6 + e, m, slice(S, H), pad[q, 0, 9 - e:9 - e + 2 * S, :])

    def own_forward(src, k, out, total):
        fill_columns(src)
        for q in range(G):
            for j in (0, J + 1):
                pad[q, j, :, :] = jnp.zeros((H + 16, C), F32)
            for j in range(1, J + 1):
                pad[q, j, 7:8, :] = jnp.zeros((1, C), F32)
                pad[q, j, 8 + H:9 + H, :] = jnp.zeros((1, C), F32)
        for a in range(3):
            for b in range(3):
                for q in range(G):
                    for j in range(J):
                        m, n = (q * J + j) * H, 3 * a + b
                        out[m:m + H, n * W:n * W + C] = pad[q, j + a, 7 + b:7 + b + H, :].astype(BF16)
        total[...] = apply(out, k)

    def more_forward(p, k, out, total):
        for q in range(G):
            @pl.when(inner_left)
            def _():
                pad[q, 0, 8:8 + H, :] = lh[p, 0, q].astype(F32)

            @pl.when(inner_right)
            def _():
                pad[q, J + 1, 8:8 + H, :] = rh[p, 0, q].astype(F32)
            for j in range(E):
                pad[q, j, 7:8, :] = ap[p, 0, q, j:j + 1]
                pad[q, j, 8 + H:9 + H, :] = bm[p, 0, q, j:j + 1]
        for q in range(G):
            for j in range(J):
                r = q * J + j
                m = r * H
                for a in range(3):
                    e = j + a
                    if e == 0 or e == J + 1:
                        for b in range(3):
                            n = 3 * a + b
                            out[m:m + H, n * W:n * W + C] = pad[q, e, 7 + b:7 + b + H, :].astype(BF16)
                        wide = slice(3 * a * W, 3 * (a + 1) * W)
                        total[m:m + H, :] += product(out[m:m + H, wide], k[wide], 1, 0)
                    else:
                        n = 3 * a
                        out[m:m + 16, n * W:n * W + C] = pad[q, e, 7:23, :].astype(BF16)
                        n = 3 * a + 2
                        out[m + H - 16:m + H, n * W:n * W + C] = pad[q, e, H - 7:H + 9, :].astype(BF16)
                        lm[0, r:r + 1, a * W:a * W + C] = ap[p, 0, q, e:e + 1]
                        lm[1, r:r + 1, a * W:a * W + C] = bm[p, 0, q, e:e + 1]
        add_lines(0, kl[0], kl[1], total)

    def add_lines(at, k_top, k_low, total):
        top = product(lm[at].astype(BF16), k_top, 1, 0)
        low = product(lm[at + 1].astype(BF16), k_low, 1, 0)
        for r in range(G * J):
            m = r * H
            total[m:m + 1, :] += top[r:r + 1]
            total[m + H - 1:m + H, :] += low[r:r + 1]

    def own_backward(src, k, out, total):
        for q in range(G):
            for j in (0, J + 1):
                pad2[q, j, :, :] = jnp.zeros((H + 16, C), F32)
            for j in range(J):
                pad2[q, 1 + j, 8:8 + H, :] = src[q, j].astype(F32)
                pad2[q, 1 + j, 7:8, :] = jnp.zeros((1, C), F32)
                pad2[q, 1 + j, 8 + H:9 + H, :] = jnp.zeros((1, C), F32)
        for a in range(3):
            for b in range(3):
                n = 3 * a + b
                for q in range(G):
                    for j in range(J):
                        m = (q * J + j) * H
                        out[n, m:m + H, :] = pad2[q, j - a + 2, 9 - b:9 - b + H, :]
                xc[:, n * W:n * W + C] = out[n].astype(BF16)
        total[...] = apply(xc, k)

    def more_backward(p, k, out, total):
        for q in range(G):
            @pl.when(inner_left)
            def _():
                pad2[q, 0, 8:8 + H, :] = lh[p, 1, q].astype(F32)

            @pl.when(inner_right)
            def _():
                pad2[q, J + 1, 8:8 + H, :] = rh[p, 1, q].astype(F32)
        for q in range(G):
            top = ap[p, 1, q]
            low = bm[p, 1, q]
            for j in range(J):
                r = q * J + j
                m = r * H
                for a, line, at, lines in ((0, 0, 2, top), (2, H - 1, 3, low)):
                    e = j - a + 2
                    outer = e == 0 or e == J + 1
                    for b in range(3):
                        n = 3 * a + b
                        add = lines[j + 2 - b:j + 3 - b]
                        if outer:
                            out[n, m:m + H, :] = pad2[q, e, 9 - b:9 - b + H, :]
                        else:
                            lm[at, r:r + 1, b * W:b * W + C] = add
                        out[n, m + line:m + line + 1, :] += add
                        span = slice(m, m + H) if outer else slice(m, m + 16) if a == 0 else slice(m + H - 16, m + H)
                        xc[span, n * W:n * W + C] = out[n, span, :].astype(BF16)
                    if outer:
                        wide = slice(3 * a * W, 3 * (a + 1) * W)
                        total[m:m + H, :] += product(xc[m:m + H, wide], k[wide], 1, 0)
        add_lines(2, k[0:3 * W], k[6 * W:9 * W], total)

    def lay_out(k, w):
        for n in range(9):
            tap = k[n // 3, n % 3]
            kf[w, n * W:n * W + C] = tap
            kb[w, n * W:n * W + C] = tap.astype(F32).T.astype(BF16)
            if W > C:
                kf[w, n * W + C:n * W + W] = jnp.zeros((W - C, C), BF16)
                kb[w, n * W + C:n * W + W] = jnp.zeros((W - C, C), BF16)

    def apply(taps, k):
        return product(taps[...], k[...], 1, 0)

    def unflat(value, dst):
        for q in range(G):
            for j in range(J):
                m = (q * J + j) * H
                dst[q, j] = value[m:m + H]

    def channel_major(value, dst):
        for q in range(G):
            sides = [value[(q * J + j) * H:(q * J + j + 1) * H].T.astype(BF16) for j in range(J)]
            dst[:, q, :, :] = jnp.stack(sides, axis=1)

    per = C // 16
    tiles = -(-9 * C // LANES)
    blocks = acc.shape[1]

    def pack(terms, w):
        spare = tiles * LANES - 9 * C
        wide = jnp.concatenate(terms + ([jnp.zeros((C, spare), F32)] if spare else []), axis=1)
        for n in range(tiles):
            acc[w, n * per:(n + 1) * per] = wide[:, n * LANES:(n + 1) * LANES].reshape(per, 16, LANES)

    def unpack(w, out):
        parts = [obuf[w, n * per:(n + 1) * per].astype(F32).reshape(C, LANES) for n in range(tiles)]
        wide = jnp.concatenate(parts, axis=1)
        for n in range(9):
            out[n // 3, n % 3] = wide[:, n * C:(n + 1) * C]

    class Sum:
        def __init__(self, w, out):
            self.out, self.at, self.over = out, 0, False
            self.w, self.lo, self.length, self.done = w, 0, blocks, []
            self.used = [0, 0]
            self.sem = 0

        def members(self, bits):
            mine = []
            for axis, s in bits:
                mine.append(lax.rem((t if axis == "tile" else f) // s, 2))
            found = []
            for k in reversed(range(1, 2 ** len(bits))):
                tile, face, digit = t, f, 0
                for pos, (axis, s) in enumerate(bits):
                    bit = mine[pos]
                    if (k >> pos) & 1:
                        if axis == "tile":
                            tile = tile + (1 - 2 * bit) * s
                        else:
                            face = face + (1 - 2 * bit) * s
                        bit = 1 - bit
                    digit = digit + bit * (1 << pos)
                found.append((digit, where_to(tile, face)))
            own = 0
            for pos, bit in enumerate(mine):
                own = own + bit * (1 << pos)
            return own, found

        def begin(self, n):
            bits, full, whole = groups[n]
            own, found = self.members(bits)
            w = self.w
            inbox = rfull if full else rlow
            at = self.used[full]
            part = self.length if whole else self.length // (len(found) + 1)
            self.flying = (inbox, at, part, len(found), whole)
            if whole:
                piece = pl.ds(self.lo, part)
                mine = pl.ds(at + own * part, part)
                sbuf[w, piece] = acc[w, piece].astype(BF16)
                for digit, dev in found:
                    remote(sbuf.at[w, piece], inbox.at[w, mine], w_s.at[w], w_r.at[w, self.sem], dev).start()
                inbox[w, mine] = sbuf[w, piece]
                self.used[full] += part * (len(found) + 1)
                return
            for digit, dev in found:
                give = self.lo + digit * part
                if full:
                    out = acc.at[w, pl.ds(give, part)]
                else:
                    sbuf[w, pl.ds(give, part)] = acc[w, pl.ds(give, part)].astype(BF16)
                    out = sbuf.at[w, pl.ds(give, part)]
                at = self.used[full]
                self.used[full] += part
                remote(out, inbox.at[w, at:at + part], w_s.at[w], w_r.at[w, self.sem], dev).start()
            keep = self.lo + own * part
            self.done.append((keep, part, found))
            self.lo, self.length = keep, part

        def end(self):
            inbox, at, part, count, whole = self.flying
            sent = inbox.at[self.w, at:at + count * part]
            settle(sent, w_s.at[self.w])
            settle(sent, w_r.at[self.w, self.sem])
            self.sem += 1
            terms = [inbox[self.w, at + n * part:at + (n + 1) * part].astype(F32) for n in range(count + whole)]
            total = terms.pop(0) if whole else acc[self.w, pl.ds(self.lo, self.length)]
            for term in terms:
                total = total + term
            acc[self.w, pl.ds(self.lo, self.length)] = total

        def round(self):
            obuf[self.w, pl.ds(self.lo, self.length)] = acc[self.w, pl.ds(self.lo, self.length)].astype(BF16)

        def give(self):
            keep, part, found = self.done.pop()
            self.flying = (part, len(found))
            for digit, dev in found:
                remote(obuf.at[self.w, pl.ds(keep, part)], obuf.at[self.w, pl.ds(keep, part)],
                       w_s.at[self.w], w_r.at[self.w, self.sem], dev).start()

        def given(self):
            part, count = self.flying
            whole = obuf.at[self.w, 0:count * part]
            settle(whole, w_s.at[self.w])
            settle(whole, w_r.at[self.w, self.sem])
            self.sem += 1

        def advance(self):
            at, count = self.at, len(groups)
            self.at += 1
            if self.over:
                return
            if at < count:
                if at > 0:
                    self.end()
                self.begin(at)
                return
            if at == count:
                self.end()
                self.round()
            else:
                self.given()
            if self.done:
                self.give()
            else:
                unpack(self.w, self.out)
                self.over = True

    barrier = pltpu.get_barrier_semaphore()
    loads = [pltpu.make_async_copy(src, dst, sem) for src, dst, sem in (
        (fields_h, raw.at[0], w_s.at[0]), (upstream_h, raw.at[1], w_s.at[1]),
        (k1_h, k1, line_s.at[0]), (k2_h, k2, line_s.at[1]))]
    for load in loads:
        load.start()

    @pl.loop(0, n_f)
    def _(df):
        @pl.loop(0, n_t)
        def _(dt):
            @pl.when(jnp.logical_or(df != f, dt != t))
            def _():
                pl.semaphore_signal(barrier, inc=1, device_id=where_to(dt, df), device_id_type=MESH)
    hidden, pre_grad = y.at[0], y.at[1]
    al[...] = jnp.zeros_like(al)
    tl[...] = jnp.zeros_like(tl)
    dl[...] = jnp.zeros_like(dl)
    for kind in range(2):
        loads[kind].wait()
        for q in range(G):
            for j in range(J):
                x[kind, q, j] = raw[kind, :, q, j, :].astype(F32).T.astype(BF16)
        stage(0, kind, x)
    if blocks > tiles * per:
        for w in range(2):
            acc[w, tiles * per:blocks] = jnp.zeros((blocks - tiles * per, 16, LANES), F32)
    pl.semaphore_wait(barrier, n_t * n_f - 1)

    loads[2].wait()
    loads[3].wait()
    start_far(0, x)
    start_near(0, x)
    lay_out(k1, 0)
    lay_out(k2, 1)
    for a in range(3):
        for side in range(2):
            n = 3 * a + 2 * side
            kl[side, a * W:(a + 1) * W] = kf[0, n * W:(n + 1) * W]
    lm[...] = jnp.zeros_like(lm)
    for taps in (xf1, xf2, xc):
        taps[...] = jnp.zeros_like(taps)
    own_forward(x.at[0], kf.at[0], xf1, pre)
    own_backward(x.at[1], kb.at[1], xb, back)
    await_arrivals(0, x)
    more_forward(0, kf.at[0], xf1, pre)
    more_backward(0, kb.at[1], xb, back)
    await_seam(0)
    forward_late(0, xf1, kf.at[0], pre)
    backward_late(0, xb, kb.at[1], back)
    value, slope = gelu_parts(pre[...])
    cells = value.astype(BF16)
    unflat(cells, hidden)
    one, two = Sum(0, w1_o), Sum(1, w2_o)
    wide = product(cells, xc[...], 0, 0)
    pack([wide[:, n * W:n * W + C] * scale for n in range(9)], 1)
    two.advance()
    cot = (back[...] * slope).astype(BF16)
    unflat(cot, pre_grad)
    pack([product(xf1[:, n * W:n * W + C], cot, 0, 0) * scale for n in range(9)], 0)
    one.advance()
    two.advance()
    one.advance()
    await_sends(0, x)
    stage(1, 0, y)
    stage(1, 1, y)
    start_far(1, y)
    two.advance()
    one.advance()
    start_near(1, y)
    two.advance()
    one.advance()
    await_arrivals(1, y)
    await_seam(1)
    forward_taps(1, hidden, xf2, False)
    channel_major(apply(xf2, kf.at[1]), res_o)
    backward_taps(1, pre_grad, xb, False)
    channel_major(apply(xc, kb.at[0]), fg_o)
    while not (one.over and two.over):
        two.advance()
        one.advance()
    await_sends(1, y)


def deliver(*refs):
    sources, targets, sems = refs[0:4], refs[4:8], refs[8]
    moves = [pltpu.make_async_copy(a, b, sems.at[n]) for n, (a, b) in enumerate(zip(sources, targets))]
    for move in moves:
        move.start()
    for move in moves:
        move.wait()


def plan(n_t, n_f):
    tile_bits = [("tile", 1 << i) for i in range(n_t.bit_length() - 1)]
    face_bits = [("face", 1 << i) for i in range(n_f.bit_length() - 1)]
    groups = [(tile_bits[:1], 1, 0)]
    middle, rest = face_bits + tile_bits[1:3], tile_bits[3:]
    while middle:
        groups.append((middle[:3], 0, 0))
        middle = middle[3:]
    while len(rest) > 2:
        groups.append((rest[:2], 0, 0))
        rest = rest[2:]
    if rest:
        groups.append((rest, 0, 1))
    return groups


def run(fields, upstream, k1, k2, n_t, n_f):
    C, G, J, H = fields.shape
    S = H // 3
    E = J + 2
    M = G * J * H
    W = -(-C // LANES) * LANES
    scale = 1.0 / (S * 12.0 ** 0.5)
    groups = plan(n_t, n_f)
    cuts, stages = 1, 0
    for bits, full, whole in groups:
        cuts *= 1 if whole else 2 ** len(bits)
        stages += 1 if whole else 2
    blocks = -(-9 * C // LANES) * (C // 16)
    blocks = -(-blocks // cuts) * cuts
    length, room = blocks, [1, 1]
    for bits, full, whole in groups:
        members = 2 ** len(bits)
        if whole:
            room[full] += length * members
        else:
            length //= members
            room[full] += length * (members - 1)
    dma = pltpu.SemaphoreType.DMA
    vmem = pl.BlockSpec(memory_space=pltpu.VMEM)
    hbm = pl.BlockSpec(memory_space=pltpu.HBM)
    held = [pltpu.with_memory_space_constraint(a, pltpu.HBM) for a in (fields, upstream, k1, k2)]
    return pl.pallas_call(
        functools.partial(body, n_t, n_f, scale, groups),
        out_shape=(
            jax.ShapeDtypeStruct((C, G, J, H), BF16),
            jax.ShapeDtypeStruct((C, G, J, H), BF16),
            jax.ShapeDtypeStruct((3, 3, C, C), F32),
            jax.ShapeDtypeStruct((3, 3, C, C), F32),
        ),
        in_specs=[hbm] * 4,
        out_specs=[vmem] * 4,
        scratch_shapes=[
            pltpu.VMEM((2, C, G, J, H), BF16),
            pltpu.VMEM((2, G, J, H, C), BF16),
            pltpu.VMEM(k1.shape, BF16),
            pltpu.VMEM(k2.shape, BF16),
            pltpu.VMEM((2, G, J, H, C), BF16),
            pltpu.VMEM((2, 2, 2, G, J, C), F32),
            pltpu.VMEM((2, 2, G, H, C), BF16),
            pltpu.VMEM((2, 2, G, H, C), BF16),
            pltpu.VMEM((2, 2, G, E, C), F32),
            pltpu.VMEM((2, 2, G, E, C), F32),
            pltpu.VMEM((2, n_t, 2, G, E, C), F32),
            pltpu.VMEM((2, n_t, 2, G, J, C), F32),
            pltpu.VMEM((2, n_t, 2, G, J, C), F32),
            pltpu.VMEM((2, G, S + 16, C), F32),
            pltpu.VMEM((2, G, S + 16, C), F32),
            pltpu.VMEM((2, G, S + 32, C), F32),
            pltpu.VMEM((G, J + 2, H + 16, C), F32),
            pltpu.VMEM((9, M, C), F32),
            pltpu.VMEM((M, 9 * W), BF16),
            pltpu.VMEM((M, 9 * W), BF16),
            pltpu.VMEM((M, 9 * W), BF16),
            pltpu.VMEM((2, 9 * W, C), BF16),
            pltpu.VMEM((2, 9 * W, C), BF16),
            pltpu.VMEM((2, 3 * W, C), BF16),
            pltpu.VMEM((4, -(-G * J // 16) * 16, 3 * W), F32),
            pltpu.VMEM((G, J + 2, H + 16, C), F32),
            pltpu.VMEM((M, C), F32),
            pltpu.VMEM((M, C), F32),
            pltpu.VMEM((2, blocks, 16, LANES), F32),
            pltpu.VMEM((2, blocks, 16, LANES), BF16),
            pltpu.VMEM((2, room[0], 16, LANES), BF16),
            pltpu.VMEM((2, room[1], 16, LANES), F32),
            pltpu.VMEM((2, blocks, 16, LANES), BF16),
            dma((2,)), dma((2, 2)),
            dma((2,)), dma((2,)), dma((2,)),
            dma((1,)), dma((1,)), dma((2, 2)),
            dma((2,)), dma((2, stages)),
        ],
        compiler_params=pltpu.CompilerParams(
            collective_id=0, has_side_effects=True, vmem_limit_bytes=24 * 1024 * 1024),
    )(*held)


def send_out(made):
    vmem = pl.BlockSpec(memory_space=pltpu.VMEM)
    hbm = pl.BlockSpec(memory_space=pltpu.HBM)
    return pl.pallas_call(
        deliver,
        out_shape=[jax.ShapeDtypeStruct(a.shape, a.dtype) for a in made],
        in_specs=[vmem] * 4,
        out_specs=[hbm] * 4,
        scratch_shapes=[pltpu.SemaphoreType.DMA((4,))],
    )(*[pltpu.with_memory_space_constraint(a, pltpu.VMEM) for a in made])


def on_device(n_sub, n_t, n_f, fields, upstream, k1, k2):
    own = fields.shape[0]
    if n_sub > 1:
        fields = lax.all_gather(fields, "sub", axis=0, tiled=True)
        upstream = lax.all_gather(upstream, "sub", axis=0, tiled=True)
    made = run(fields, upstream, k1, k2, n_t, n_f)
    if n_sub > 1:
        at = lax.axis_index("sub") * own
        res, fgrad, w1, w2 = made
        return (
            lax.dynamic_slice_in_dim(res, at, own, 0),
            lax.dynamic_slice_in_dim(fgrad, at, own, 0),
            lax.dynamic_slice_in_dim(w1, at, own, 3),
            lax.dynamic_slice_in_dim(w2, at, own, 3),
        )
    return tuple(send_out(made))


def solution(mesh):
    placed = (P("sub", "face", "tile", "parts"), P("sub", "face", "tile", "parts"), P(), P())
    sizes = mesh.shape
    return jax.shard_map(
        functools.partial(on_device, sizes["sub"], sizes["tile"], sizes["face"]),
        mesh=mesh,
        in_specs=placed,
        out_specs=(
            P("sub", "face", "tile", "parts"),
            P("sub", "face", "tile", "parts"),
            P("parts", None, None, "sub"),
            P("parts", None, None, "sub"),
        ),
        check_vma=False,
    )
```

```python
import functools

import jax
import jax.numpy as jnp
from jax import lax
from jax.experimental import pallas as pl
from jax.experimental.pallas import tpu as pltpu
from jax.sharding import PartitionSpec as P

MESH = pl.DeviceIdType.MESH
F32 = jnp.float32
BF16 = jnp.bfloat16
LANES = 128


def gelu_parts(v):
    root = 0.7978845608028654
    cube = 0.044715 * (v * v * v)
    th = jnp.tanh(root * (v + cube))
    value = v * (0.5 * (1.0 + th))
    slope = 0.5 * (1.0 + th) + 0.5 * v * (1.0 - th * th) * root * (1.0 + 0.134145 * (v * v))
    return value, slope


def product(a, b, da, db):
    return lax.dot_general(a, b, (((da,), (db,)), ((), ())), preferred_element_type=F32)


def body(n_t, n_f, scale, groups, fields_h, upstream_h, k1_h, k2_h, res_o, fg_o, w1_o, w2_o,
         raw, x, k1, k2, y, rows, lh, rh, ap, bm, aps, tr, dr, tl, dl, al, pad, xb, xf1, xf2, xc, kf, kb, kl, lm, pad2, pre, back,
         acc, sbuf, rlow, rfull, obuf,
         col_s, col_r, line_s, a_r, b_r, t_s, d_s, row_r, w_s, w_r):
    _, G, J, H, C = x.shape
    S = H // 3
    E = J + 2
    W = xc.shape[1] // 9
    t = lax.axis_index("tile")
    f = lax.axis_index("face")
    fn = lax.rem(f + 1, n_f)
    fp = lax.rem(f + n_f - 1, n_f)
    first = t == 0
    last = t == n_t - 1
    inner_left = jnp.logical_not(first)
    inner_right = jnp.logical_not(last)

    upper, lower = slice(S, H), slice(0, 2 * S)

    def where_to(tile, face):
        return {"tile": tile, "face": face}

    def remote(src, dst, s, r, dev):
        return pltpu.make_async_remote_copy(
            src_ref=src, dst_ref=dst, send_sem=s, recv_sem=r, device_id=dev, device_id_type=MESH)

    def settle(ref, sem):
        pltpu.make_async_copy(ref, ref, sem).wait()

    def copies(p, src):
        c0, cl = src.at[:, :, 0], src.at[:, :, J - 1]
        right = lambda: remote(cl, lh.at[p], col_s.at[0], col_r.at[p, 0], where_to(jnp.minimum(t + 1, n_t - 1), f))
        left = lambda: remote(c0, rh.at[p], col_s.at[1], col_r.at[p, 1], where_to(jnp.maximum(t - 1, 0), f))
        seam = []
        if G > 1:
            seam.append((first, lambda: remote(src.at[:, 1:G, 0, upper], rh.at[p, :, 0:G - 1, upper], col_s.at[1], col_r.at[p, 1], where_to(n_t - 1, f))))
            seam.append((last, lambda: remote(src.at[:, 0:G - 1, J - 1, lower], lh.at[p, :, 1:G, lower], col_s.at[0], col_r.at[p, 0], where_to(0, f))))
        seam.append((first, lambda: remote(src.at[:, 0:1, 0, upper], rh.at[p, :, G - 1:G, upper], col_s.at[1], col_r.at[p, 1], where_to(n_t - 1, fp))))
        seam.append((last, lambda: remote(src.at[:, G - 1:G, J - 1, lower], lh.at[p, :, 0:1, lower], col_s.at[0], col_r.at[p, 0], where_to(0, fn))))
        a_own = lambda d: remote(aps.at[p, d, :, 1:G], ap.at[p, :, 0:G - 1], line_s.at[0], a_r.at[p], where_to(d, f))
        a_oth = lambda d: remote(aps.at[p, d, :, 0:1], ap.at[p, :, G - 1:G], line_s.at[1], a_r.at[p], where_to(d, fp))
        b_own = lambda d: remote(aps.at[p, d, :, 0:G - 1], bm.at[p, :, 1:G], line_s.at[0], b_r.at[p], where_to(d, f))
        b_oth = lambda d: remote(aps.at[p, d, :, G - 1:G], bm.at[p, :, 0:1], line_s.at[1], b_r.at[p], where_to(d, fn))
        t_own = lambda d: remote(rows.at[p, 0, :, 0:G - 1], tr.at[p, d, :, 1:G], t_s.at[0], row_r.at[p, 0], where_to(0, f))
        t_oth = lambda d: remote(rows.at[p, 0, :, G - 1:G], tr.at[p, d, :, 0:1], t_s.at[0], row_r.at[p, 1], where_to(0, fn))
        d_own = lambda d: remote(rows.at[p, 1, :, 1:G], dr.at[p, d, :, 0:G - 1], d_s.at[0], row_r.at[p, 0], where_to(n_t - 1, f))
        d_oth = lambda d: remote(rows.at[p, 1, :, 0:1], dr.at[p, d, :, G - 1:G], d_s.at[0], row_r.at[p, 1], where_to(n_t - 1, fp))
        return right, left, seam, a_own, a_oth, b_own, b_oth, t_own, t_oth, d_own, d_oth

    def stage(p, kind, src):
        for q in range(G):
            for j in range(J):
                rows[p, 0, kind, q, j:j + 1, :] = src[kind, q, j, 0:16].astype(F32)[0:1]
                rows[p, 1, kind, q, j:j + 1, :] = src[kind, q, j, H - 16:H].astype(F32)[15:16]
        more = 16 * kind

        @pl.when(first)
        def _():
            for q in range(G):
                al[kind, q, 16:16 + S + more, :] = src[kind, q, 0, 0:S + more].astype(F32)
            for d in range(n_t):
                aps[p, d, kind] = al[kind, :, 15 + d * J:15 + d * J + E, :]

        @pl.when(last)
        def _():
            for q in range(G):
                al[kind, q, 16 - more:16 + S, :] = src[kind, q, J - 1, 2 * S - more:H].astype(F32)
            for d in range(n_t):
                aps[p, d, kind] = al[kind, :, 15 + d * J:15 + d * J + E, :]

    def start_far(p, src):
        right, left, seam, a_own, a_oth, b_own, b_oth, t_own, t_oth, d_own, d_oth = copies(p, src)
        half = n_t // 2

        @pl.when(first)
        def _():
            @pl.loop(0, n_t - half)
            def _(d):
                a_oth(n_t - 1 - d).start()
                if G > 1:
                    a_own(n_t - 1 - d).start()

        @pl.when(last)
        def _():
            @pl.loop(0, half)
            def _(d):
                b_oth(d).start()
                if G > 1:
                    b_own(d).start()
        for cond, make in seam:
            @pl.when(cond)
            def _(make=make):
                make().start()

        @pl.when(first)
        def _():
            a_oth(0).start()

            @pl.loop(1, half)
            def _(d):
                a_oth(half - d).start()
                if G > 1:
                    a_own(half - d).start()
            if G > 1:
                ap[p, :, 0:G - 1] = aps[p, 0, :, 1:G]
                tr[p, 0, :, 1:G] = rows[p, 0, :, 0:G - 1]

        @pl.when(last)
        def _():
            b_oth(n_t - 1).start()

            @pl.loop(half, n_t - 1)
            def _(d):
                b_oth(d).start()
                if G > 1:
                    b_own(d).start()
            if G > 1:
                bm[p, :, 1:G] = aps[p, n_t - 1, :, 0:G - 1]
                dr[p, n_t - 1, :, 0:G - 1] = rows[p, 1, :, 1:G]
        t_oth(t).start()
        d_oth(t).start()
        if G > 1:
            @pl.when(inner_left)
            def _():
                t_own(t).start()

            @pl.when(inner_right)
            def _():
                d_own(t).start()

    def start_near(p, src):
        right, left = copies(p, src)[0:2]

        @pl.when(inner_right)
        def _():
            right().start()

        @pl.when(inner_left)
        def _():
            left().start()

    def await_arrivals(p, src):
        right, left = copies(p, src)[0:2]

        @pl.when(inner_left)
        def _():
            right().wait_recv()
            settle(ap.at[p], a_r.at[p])

        @pl.when(first)
        def _():
            settle(ap.at[p, :, G - 1:G], a_r.at[p])

        @pl.when(inner_right)
        def _():
            left().wait_recv()
            settle(bm.at[p], b_r.at[p])

        @pl.when(last)
        def _():
            settle(bm.at[p, :, 0:1], b_r.at[p])

    def await_seam(p):
        @pl.when(last)
        def _():
            settle(rh.at[p, :, :, upper], col_r.at[p, 1])

        @pl.when(first)
        def _():
            settle(lh.at[p, :, :, lower], col_r.at[p, 0])

        @pl.when(first)
        def _():
            if G > 1:
                settle(tr.at[p, 1:n_t, :, 1:G], row_r.at[p, 0])
            settle(tr.at[p, :, :, 0:1], row_r.at[p, 1])
            for d in range(n_t):
                tl[:, :, 8 + d * J:8 + (d + 1) * J, :] = tr[p, d]

        @pl.when(last)
        def _():
            if G > 1:
                settle(dr.at[p, 0:n_t - 1, :, 0:G - 1], row_r.at[p, 0])
            settle(dr.at[p, :, :, G - 1:G], row_r.at[p, 1])
            for d in range(n_t):
                dl[:, :, 8 + d * J:8 + (d + 1) * J, :] = dr[p, d]

    def await_sends(p, src):
        right, left = copies(p, src)[0:2]

        @pl.when(inner_right)
        def _():
            right().wait_send()
            settle(rows.at[p, 1], d_s.at[0])

        @pl.when(last)
        def _():
            settle(src.at[:, :, J - 1, lower], col_s.at[0])
            settle(rows.at[p, 1, :, 0:1], d_s.at[0])

        @pl.when(inner_left)
        def _():
            left().wait_send()
            settle(rows.at[p, 0], t_s.at[0])

        @pl.when(first)
        def _():
            settle(src.at[:, :, 0, upper], col_s.at[1])
            settle(rows.at[p, 0, :, G - 1:G], t_s.at[0])

        @pl.when(jnp.logical_or(first, last))
        def _():
            if G > 1:
                settle(aps.at[p, 1:n_t, :, 1:G], line_s.at[0])
            settle(aps.at[p, :, :, 0:1], line_s.at[1])

    def fill_columns(src):
        for q in range(G):
            for j in range(J):
                pad[q, 1 + j, 8:8 + H, :] = src[q, j].astype(F32)

    def forward_taps(p, src, out, late):
        fill_columns(src)
        for q in range(G):
            @pl.when(inner_left)
            def _():
                pad[q, 0, 8:8 + H, :] = lh[p, 0, q].astype(F32)

            @pl.when(inner_right)
            def _():
                pad[q, J + 1, 8:8 + H, :] = rh[p, 0, q].astype(F32)

            if late:
                @pl.when(first)
                def _():
                    pad[q, 0, 8:8 + H, :] = jnp.zeros((H, C), F32)

                @pl.when(last)
                def _():
                    pad[q, J + 1, 8:8 + H, :] = jnp.zeros((H, C), F32)
            else:
                @pl.when(first)
                def _():
                    forward_edge(p, q, 0)

                @pl.when(last)
                def _():
                    forward_edge(p, q, J + 1)
            for j in range(E):
                pad[q, j, 7:8, :] = ap[p, 0, q, j:j + 1]
                pad[q, j, 8 + H:9 + H, :] = bm[p, 0, q, j:j + 1]
        for a in range(3):
            for b in range(3):
                for q in range(G):
                    for j in range(J):
                        m = (q * J + j) * H
                        n = 3 * a + b
                        out[m:m + H, n * W:n * W + C] = pad[q, j + a, 7 + b:7 + b + H, :].astype(BF16)

    def forward_edge(p, q, j):
        if j == 0:
            pad[q, 0, 8:8 + S, :] = tl[0, q, 8:8 + S, :]
            pad[q, 0, 8 + S:8 + H, :] = lh[p, 0, q, 0:2 * S].astype(F32)
        else:
            pad[q, J + 1, 8:8 + 2 * S, :] = rh[p, 0, q, S:H].astype(F32)
            pad[q, J + 1, 8 + 2 * S:8 + H, :] = dl[0, q, 8:8 + S, :]

    def forward_late(p, out, k, total):
        for cond, a, j in ((first, 0, 0), (last, 2, J + 1)):
            @pl.when(cond)
            def _(a=a, j=j):
                for q in range(G):
                    forward_edge(p, q, j)
                    m = (q * J + j - a) * H
                    for b in range(3):
                        n = 3 * a + b
                        out[m:m + H, n * W:n * W + C] = pad[q, j, 7 + b:7 + b + H, :].astype(BF16)
                    wide = slice(3 * a * W, 3 * (a + 1) * W)
                    total[m:m + H, :] += product(out[m:m + H, wide], k[wide], 1, 0)

    def backward_taps(p, src, out, late):
        fill_columns(src)
        for q in range(G):
            @pl.when(inner_left)
            def _():
                pad[q, 0, 8:8 + H, :] = lh[p, 1, q].astype(F32)

            @pl.when(first)
            def _():
                pad[q, 0, :, :] = jnp.zeros((H + 16, C), F32)

            @pl.when(inner_right)
            def _():
                pad[q, J + 1, 8:8 + H, :] = rh[p, 1, q].astype(F32)

            @pl.when(last)
            def _():
                pad[q, J + 1, :, :] = jnp.zeros((H + 16, C), F32)
            for j in range(E):
                pad[q, j, 7:8, :] = jnp.zeros((1, C), F32)
                pad[q, j, 8 + H:9 + H, :] = jnp.zeros((1, C), F32)
        for a in range(3):
            for b in range(3):
                for q in range(G):
                    for j in range(J):
                        m = (q * J + j) * H
                        out[3 * a + b, m:m + H, :] = pad[q, j - a + 2, 9 - b:9 - b + H, :]
        for q in range(G):
            top = ap[p, 1, q]
            low = bm[p, 1, q]
            for b in range(3):
                for j in range(J):
                    m = (q * J + j) * H
                    out[b, m:m + 1, :] += top[j + 2 - b:j + 3 - b]
                    out[6 + b, m + H - 1:m + H, :] += low[j + 2 - b:j + 3 - b]
        if not late:
            backward_late(p, out, None, None)
        for n in range(9):
            xc[:, n * W:n * W + C] = out[n].astype(BF16)

    def backward_late(p, out, k, total):
        def add(n, m, rows_at, value):
            here = slice(m + rows_at.start, m + rows_at.stop)
            out[n, here, :] += value
            if total is not None:
                xc[here, n * W:n * W + C] = out[n, here, :].astype(BF16)
                total[here, :] += product(value.astype(BF16), k[n * W:n * W + C], 1, 0)

        @pl.when(last)
        def _():
            for q in range(G):
                m = (q * J + J - 1) * H
                pad[q, J + 1, 8 + S:8 + H, :] = rh[p, 1, q, S:H].astype(F32)
                pad[q, J + 1, 7 + S:8 + S, :] = ap[p, 1, q, J:J + 1]
                pad[q, J + 1, 8 + H:9 + H, :] = jnp.zeros((1, C), F32)
                for e in range(3):
                    add(e, m, slice(0, 2 * S), pad[q, J + 1, 8 + S + 1 - e:8 + H + 1 - e, :])
                    add(3 * e + 2, m, slice(2 * S, H), dl[1, q, 9 - e:9 - e + S, :])

        @pl.when(first)
        def _():
            for q in range(G):
                m = q * J * H
                pad[q, 0, 7:8, :] = jnp.zeros((1, C), F32)
                pad[q, 0, 8:8 + 2 * S, :] = lh[p, 1, q, 0:2 * S].astype(F32)
                pad[q, 0, 8 + 2 * S:9 + 2 * S, :] = bm[p, 1, q, 1:2]
                for e in range(3):
                    add(3 * e, m, slice(0, S), tl[1, q, 9 - e:9 - e + S, :])
                    add(6 + e, m, slice(S, H), pad[q, 0, 9 - e:9 - e + 2 * S, :])

    def own_forward(src, k, out, total):
        fill_columns(src)
        for q in range(G):
            for j in (0, J + 1):
                pad[q, j, :, :] = jnp.zeros((H + 16, C), F32)
            for j in range(1, J + 1):
                pad[q, j, 7:8, :] = jnp.zeros((1, C), F32)
                pad[q, j, 8 + H:9 + H, :] = jnp.zeros((1, C), F32)
        for a in range(3):
            for b in range(3):
                for q in range(G):
                    for j in range(J):
                        m, n = (q * J + j) * H, 3 * a + b
                        out[m:m + H, n * W:n * W + C] = pad[q, j + a, 7 + b:7 + b + H, :].astype(BF16)
        total[...] = apply(out, k)

    def more_forward(p, k, out, total):
        for q in range(G):
            @pl.when(inner_left)
            def _():
                pad[q, 0, 8:8 + H, :] = lh[p, 0, q].astype(F32)

            @pl.when(inner_right)
            def _():
                pad[q, J + 1, 8:8 + H, :] = rh[p, 0, q].astype(F32)
            for j in range(E):
                pad[q, j, 7:8, :] = ap[p, 0, q, j:j + 1]
                pad[q, j, 8 + H:9 + H, :] = bm[p, 0, q, j:j + 1]
        for q in range(G):
            for j in range(J):
                r = q * J + j
                m = r * H
                for a in range(3):
                    e = j + a
                    if e == 0 or e == J + 1:
                        for b in range(3):
                            n = 3 * a + b
                            out[m:m + H, n * W:n * W + C] = pad[q, e, 7 + b:7 + b + H, :].astype(BF16)
                        wide = slice(3 * a * W, 3 * (a + 1) * W)
                        total[m:m + H, :] += product(out[m:m + H, wide], k[wide], 1, 0)
                    else:
                        n = 3 * a
                        out[m:m + 16, n * W:n * W + C] = pad[q, e, 7:23, :].astype(BF16)
                        n = 3 * a + 2
                        out[m + H - 16:m + H, n * W:n * W + C] = pad[q, e, H - 7:H + 9, :].astype(BF16)
                        lm[0, r:r + 1, a * W:a * W + C] = ap[p, 0, q, e:e + 1]
                        lm[1, r:r + 1, a * W:a * W + C] = bm[p, 0, q, e:e + 1]
        add_lines(0, kl[0], kl[1], total)

    def add_lines(at, k_top, k_low, total):
        top = product(lm[at].astype(BF16), k_top, 1, 0)
        low = product(lm[at + 1].astype(BF16), k_low, 1, 0)
        for r in range(G * J):
            m = r * H
            total[m:m + 1, :] += top[r:r + 1]
            total[m + H - 1:m + H, :] += low[r:r + 1]

    def own_backward(src, k, out, total):
        for q in range(G):
            for j in (0, J + 1):
                pad2[q, j, :, :] = jnp.zeros((H + 16, C), F32)
            for j in range(J):
                pad2[q, 1 + j, 8:8 + H, :] = src[q, j].astype(F32)
                pad2[q, 1 + j, 7:8, :] = jnp.zeros((1, C), F32)
                pad2[q, 1 + j, 8 + H:9 + H, :] = jnp.zeros((1, C), F32)
        for a in range(3):
            for b in range(3):
                n = 3 * a + b
                for q in range(G):
                    for j in range(J):
                        m = (q * J + j) * H
                        out[n, m:m + H, :] = pad2[q, j - a + 2, 9 - b:9 - b + H, :]
                xc[:, n * W:n * W + C] = out[n].astype(BF16)
        total[...] = apply(xc, k)

    def more_backward(p, k, out, total):
        for q in range(G):
            @pl.when(inner_left)
            def _():
                pad2[q, 0, 8:8 + H, :] = lh[p, 1, q].astype(F32)

            @pl.when(inner_right)
            def _():
                pad2[q, J + 1, 8:8 + H, :] = rh[p, 1, q].astype(F32)
        for q in range(G):
            top = ap[p, 1, q]
            low = bm[p, 1, q]
            for j in range(J):
                r = q * J + j
                m = r * H
                for a, line, at, lines in ((0, 0, 2, top), (2, H - 1, 3, low)):
                    e = j - a + 2
                    outer = e == 0 or e == J + 1
                    for b in range(3):
                        n = 3 * a + b
                        add = lines[j + 2 - b:j + 3 - b]
                        if outer:
                            out[n, m:m + H, :] = pad2[q, e, 9 - b:9 - b + H, :]
                        else:
                            lm[at, r:r + 1, b * W:b * W + C] = add
                        out[n, m + line:m + line + 1, :] += add
                        span = slice(m, m + H) if outer else slice(m, m + 16) if a == 0 else slice(m + H - 16, m + H)
                        xc[span, n * W:n * W + C] = out[n, span, :].astype(BF16)
                    if outer:
                        wide = slice(3 * a * W, 3 * (a + 1) * W)
                        total[m:m + H, :] += product(xc[m:m + H, wide], k[wide], 1, 0)
        add_lines(2, k[0:3 * W], k[6 * W:9 * W], total)

    def lay_out(k, w):
        for n in range(9):
            tap = k[n // 3, n % 3]
            kf[w, n * W:n * W + C] = tap
            kb[w, n * W:n * W + C] = tap.astype(F32).T.astype(BF16)
            if W > C:
                kf[w, n * W + C:n * W + W] = jnp.zeros((W - C, C), BF16)
                kb[w, n * W + C:n * W + W] = jnp.zeros((W - C, C), BF16)

    def apply(taps, k):
        return product(taps[...], k[...], 1, 0)

    def unflat(value, dst):
        for q in range(G):
            for j in range(J):
                m = (q * J + j) * H
                dst[q, j] = value[m:m + H]

    def channel_major(value, dst):
        for q in range(G):
            sides = [value[(q * J + j) * H:(q * J + j + 1) * H].T.astype(BF16) for j in range(J)]
            dst[:, q, :, :] = jnp.stack(sides, axis=1)

    per = C // 16
    tiles = -(-9 * C // LANES)
    blocks = acc.shape[1]

    def pack(terms, w):
        spare = tiles * LANES - 9 * C
        wide = jnp.concatenate(terms + ([jnp.zeros((C, spare), F32)] if spare else []), axis=1)
        for n in range(tiles):
            acc[w, n * per:(n + 1) * per] = wide[:, n * LANES:(n + 1) * LANES].reshape(per, 16, LANES)

    def unpack(w, out):
        parts = [obuf[w, n * per:(n + 1) * per].astype(F32).reshape(C, LANES) for n in range(tiles)]
        wide = jnp.concatenate(parts, axis=1)
        for n in range(9):
            out[n // 3, n % 3] = wide[:, n * C:(n + 1) * C]

    class Sum:
        def __init__(self, w, out):
            self.out, self.at, self.over = out, 0, False
            self.w, self.lo, self.length, self.done = w, 0, blocks, []
            self.used = [0, 0]
            self.sem = 0

        def members(self, bits):
            mine = []
            for axis, s in bits:
                mine.append(lax.rem((t if axis == "tile" else f) // s, 2))
            found = []
            for k in reversed(range(1, 2 ** len(bits))):
                tile, face, digit = t, f, 0
                for pos, (axis, s) in enumerate(bits):
                    bit = mine[pos]
                    if (k >> pos) & 1:
                        if axis == "tile":
                            tile = tile + (1 - 2 * bit) * s
                        else:
                            face = face + (1 - 2 * bit) * s
                        bit = 1 - bit
                    digit = digit + bit * (1 << pos)
                found.append((digit, where_to(tile, face)))
            own = 0
            for pos, bit in enumerate(mine):
                own = own + bit * (1 << pos)
            return own, found

        def begin(self, n):
            bits, full, whole = groups[n]
            own, found = self.members(bits)
            w = self.w
            inbox = rfull if full else rlow
            at = self.used[full]
            part = self.length if whole else self.length // (len(found) + 1)
            self.flying = (inbox, at, part, len(found), whole)
            if whole:
                piece = pl.ds(self.lo, part)
                mine = pl.ds(at + own * part, part)
                sbuf[w, piece] = acc[w, piece].astype(BF16)
                for digit, dev in found:
                    remote(sbuf.at[w, piece], inbox.at[w, mine], w_s.at[w], w_r.at[w, self.sem], dev).start()
                inbox[w, mine] = sbuf[w, piece]
                self.used[full] += part * (len(found) + 1)
                return
            for digit, dev in found:
                give = self.lo + digit * part
                if full:
                    out = acc.at[w, pl.ds(give, part)]
                else:
                    sbuf[w, pl.ds(give, part)] = acc[w, pl.ds(give, part)].astype(BF16)
                    out = sbuf.at[w, pl.ds(give, part)]
                at = self.used[full]
                self.used[full] += part
                remote(out, inbox.at[w, at:at + part], w_s.at[w], w_r.at[w, self.sem], dev).start()
            keep = self.lo + own * part
            self.done.append((keep, part, found))
            self.lo, self.length = keep, part

        def end(self):
            inbox, at, part, count, whole = self.flying
            sent = inbox.at[self.w, at:at + count * part]
            settle(sent, w_s.at[self.w])
            settle(sent, w_r.at[self.w, self.sem])
            self.sem += 1
            terms = [inbox[self.w, at + n * part:at + (n + 1) * part].astype(F32) for n in range(count + whole)]
            total = terms.pop(0) if whole else acc[self.w, pl.ds(self.lo, self.length)]
            for term in terms:
                total = total + term
            acc[self.w, pl.ds(self.lo, self.length)] = total

        def round(self):
            obuf[self.w, pl.ds(self.lo, self.length)] = acc[self.w, pl.ds(self.lo, self.length)].astype(BF16)

        def give(self):
            keep, part, found = self.done.pop()
            self.flying = (part, len(found))
            for digit, dev in found:
                remote(obuf.at[self.w, pl.ds(keep, part)], obuf.at[self.w, pl.ds(keep, part)],
                       w_s.at[self.w], w_r.at[self.w, self.sem], dev).start()

        def given(self):
            part, count = self.flying
            whole = obuf.at[self.w, 0:count * part]
            settle(whole, w_s.at[self.w])
            settle(whole, w_r.at[self.w, self.sem])
            self.sem += 1

        def advance(self):
            at, count = self.at, len(groups)
            self.at += 1
            if self.over:
                return
            if at < count:
                if at > 0:
                    self.end()
                self.begin(at)
                return
            if at == count:
                self.end()
                self.round()
            else:
                self.given()
            if self.done:
                self.give()
            else:
                unpack(self.w, self.out)
                self.over = True

    barrier = pltpu.get_barrier_semaphore()
    loads = [pltpu.make_async_copy(src, dst, sem) for src, dst, sem in (
        (fields_h, raw.at[0], w_s.at[0]), (upstream_h, raw.at[1], w_s.at[1]),
        (k1_h, k1, line_s.at[0]), (k2_h, k2, line_s.at[1]))]
    for load in loads:
        load.start()

    @pl.loop(0, n_f)
    def _(df):
        @pl.loop(0, n_t)
        def _(dt):
            @pl.when(jnp.logical_or(df != f, dt != t))
            def _():
                pl.semaphore_signal(barrier, inc=1, device_id=where_to(dt, df), device_id_type=MESH)
    hidden, pre_grad = y.at[0], y.at[1]
    al[...] = jnp.zeros_like(al)
    tl[...] = jnp.zeros_like(tl)
    dl[...] = jnp.zeros_like(dl)
    for kind in range(2):
        loads[kind].wait()
        for q in range(G):
            for j in range(J):
                x[kind, q, j] = raw[kind, :, q, j, :].astype(F32).T.astype(BF16)
        stage(0, kind, x)
    if blocks > tiles * per:
        for w in range(2):
            acc[w, tiles * per:blocks] = jnp.zeros((blocks - tiles * per, 16, LANES), F32)
    pl.semaphore_wait(barrier, n_t * n_f - 1)

    loads[2].wait()
    loads[3].wait()
    start_far(0, x)
    start_near(0, x)
    lay_out(k1, 0)
    lay_out(k2, 1)
    for a in range(3):
        for side in range(2):
            n = 3 * a + 2 * side
            kl[side, a * W:(a + 1) * W] = kf[0, n * W:(n + 1) * W]
    lm[...] = jnp.zeros_like(lm)
    for taps in (xf1, xf2, xc):
        taps[...] = jnp.zeros_like(taps)
    own_forward(x.at[0], kf.at[0], xf1, pre)
    own_backward(x.at[1], kb.at[1], xb, back)
    await_arrivals(0, x)
    more_forward(0, kf.at[0], xf1, pre)
    more_backward(0, kb.at[1], xb, back)
    await_seam(0)
    forward_late(0, xf1, kf.at[0], pre)
    backward_late(0, xb, kb.at[1], back)
    value, slope = gelu_parts(pre[...])
    cells = value.astype(BF16)
    unflat(cells, hidden)
    one, two = Sum(0, w1_o), Sum(1, w2_o)
    wide = product(cells, xc[...], 0, 0)
    pack([wide[:, n * W:n * W + C] * scale for n in range(9)], 1)
    two.advance()
    cot = (back[...] * slope).astype(BF16)
    unflat(cot, pre_grad)
    pack([product(xf1[:, n * W:n * W + C], cot, 0, 0) * scale for n in range(9)], 0)
    one.advance()
    two.advance()
    one.advance()
    await_sends(0, x)
    stage(1, 0, y)
    stage(1, 1, y)
    start_far(1, y)
    two.advance()
    one.advance()
    start_near(1, y)
    two.advance()
    one.advance()
    await_arrivals(1, y)
    await_seam(1)
    forward_taps(1, hidden, xf2, False)
    channel_major(apply(xf2, kf.at[1]), res_o)
    backward_taps(1, pre_grad, xb, False)
    channel_major(apply(xc, kb.at[0]), fg_o)
    while not (one.over and two.over):
        two.advance()
        one.advance()
    await_sends(1, y)


def deliver(*refs):
    sources, targets, sems = refs[0:4], refs[4:8], refs[8]
    moves = [pltpu.make_async_copy(a, b, sems.at[n]) for n, (a, b) in enumerate(zip(sources, targets))]
    for move in moves:
        move.start()
    for move in moves:
        move.wait()


def plan(n_t, n_f):
    tile_bits = [("tile", 1 << i) for i in range(n_t.bit_length() - 1)]
    face_bits = [("face", 1 << i) for i in range(n_f.bit_length() - 1)]
    groups = [(tile_bits[:1], 1, 0)]
    middle, rest = face_bits + tile_bits[1:3], tile_bits[3:]
    while middle:
        groups.append((middle[:3], 0, 0))
        middle = middle[3:]
    while len(rest) > 2:
        groups.append((rest[:2], 0, 0))
        rest = rest[2:]
    if rest:
        groups.append((rest, 0, 1))
    return groups


def run(fields, upstream, k1, k2, n_t, n_f):
    C, G, J, H = fields.shape
    S = H // 3
    E = J + 2
    M = G * J * H
    W = -(-C // LANES) * LANES
    scale = 1.0 / (S * 12.0 ** 0.5)
    groups = plan(n_t, n_f)
    cuts, stages = 1, 0
    for bits, full, whole in groups:
        cuts *= 1 if whole else 2 ** len(bits)
        stages += 1 if whole else 2
    blocks = -(-9 * C // LANES) * (C // 16)
    blocks = -(-blocks // cuts) * cuts
    length, room = blocks, [1, 1]
    for bits, full, whole in groups:
        members = 2 ** len(bits)
        if whole:
            room[full] += length * members
        else:
            length //= members
            room[full] += length * (members - 1)
    dma = pltpu.SemaphoreType.DMA
    vmem = pl.BlockSpec(memory_space=pltpu.VMEM)
    hbm = pl.BlockSpec(memory_space=pltpu.HBM)
    held = [pltpu.with_memory_space_constraint(a, pltpu.HBM) for a in (fields, upstream, k1, k2)]
    return pl.pallas_call(
        functools.partial(body, n_t, n_f, scale, groups),
        out_shape=(
            jax.ShapeDtypeStruct((C, G, J, H), BF16),
            jax.ShapeDtypeStruct((C, G, J, H), BF16),
            jax.ShapeDtypeStruct((3, 3, C, C), F32),
            jax.ShapeDtypeStruct((3, 3, C, C), F32),
        ),
        in_specs=[hbm] * 4,
        out_specs=[vmem] * 4,
        scratch_shapes=[
            pltpu.VMEM((2, C, G, J, H), BF16),
            pltpu.VMEM((2, G, J, H, C), BF16),
            pltpu.VMEM(k1.shape, BF16),
            pltpu.VMEM(k2.shape, BF16),
            pltpu.VMEM((2, G, J, H, C), BF16),
            pltpu.VMEM((2, 2, 2, G, J, C), F32),
            pltpu.VMEM((2, 2, G, H, C), BF16),
            pltpu.VMEM((2, 2, G, H, C), BF16),
            pltpu.VMEM((2, 2, G, E, C), F32),
            pltpu.VMEM((2, 2, G, E, C), F32),
            pltpu.VMEM((2, n_t, 2, G, E, C), F32),
            pltpu.VMEM((2, n_t, 2, G, J, C), F32),
            pltpu.VMEM((2, n_t, 2, G, J, C), F32),
            pltpu.VMEM((2, G, S + 16, C), F32),
            pltpu.VMEM((2, G, S + 16, C), F32),
            pltpu.VMEM((2, G, S + 32, C), F32),
            pltpu.VMEM((G, J + 2, H + 16, C), F32),
            pltpu.VMEM((9, M, C), F32),
            pltpu.VMEM((M, 9 * W), BF16),
            pltpu.VMEM((M, 9 * W), BF16),
            pltpu.VMEM((M, 9 * W), BF16),
            pltpu.VMEM((2, 9 * W, C), BF16),
            pltpu.VMEM((2, 9 * W, C), BF16),
            pltpu.VMEM((2, 3 * W, C), BF16),
            pltpu.VMEM((4, -(-G * J // 16) * 16, 3 * W), F32),
            pltpu.VMEM((G, J + 2, H + 16, C), F32),
            pltpu.VMEM((M, C), F32),
            pltpu.VMEM((M, C), F32),
            pltpu.VMEM((2, blocks, 16, LANES), F32),
            pltpu.VMEM((2, blocks, 16, LANES), BF16),
            pltpu.VMEM((2, room[0], 16, LANES), BF16),
            pltpu.VMEM((2, room[1], 16, LANES), F32),
            pltpu.VMEM((2, blocks, 16, LANES), BF16),
            dma((2,)), dma((2, 2)),
            dma((2,)), dma((2,)), dma((2,)),
            dma((1,)), dma((1,)), dma((2, 2)),
            dma((2,)), dma((2, stages)),
        ],
        compiler_params=pltpu.CompilerParams(
            collective_id=0, has_side_effects=True, vmem_limit_bytes=24 * 1024 * 1024),
    )(*held)


def send_out(made):
    vmem = pl.BlockSpec(memory_space=pltpu.VMEM)
    hbm = pl.BlockSpec(memory_space=pltpu.HBM)
    return pl.pallas_call(
        deliver,
        out_shape=[jax.ShapeDtypeStruct(a.shape, a.dtype) for a in made],
        in_specs=[vmem] * 4,
        out_specs=[hbm] * 4,
        scratch_shapes=[pltpu.SemaphoreType.DMA((4,))],
    )(*[pltpu.with_memory_space_constraint(a, pltpu.VMEM) for a in made])


def on_device(n_sub, n_t, n_f, fields, upstream, k1, k2):
    own = fields.shape[0]
    if n_sub > 1:
        fields = lax.all_gather(fields, "sub", axis=0, tiled=True)
        upstream = lax.all_gather(upstream, "sub", axis=0, tiled=True)
    made = run(fields, upstream, k1, k2, n_t, n_f)
    if n_sub > 1:
        at = lax.axis_index("sub") * own
        res, fgrad, w1, w2 = made
        return (
            lax.dynamic_slice_in_dim(res, at, own, 0),
            lax.dynamic_slice_in_dim(fgrad, at, own, 0),
            lax.dynamic_slice_in_dim(w1, at, own, 3),
            lax.dynamic_slice_in_dim(w2, at, own, 3),
        )
    return tuple(send_out(made))


def solution(mesh):
    placed = (P("sub", "face", "tile", "parts"), P("sub", "face", "tile", "parts"), P(), P())
    sizes = mesh.shape
    return jax.shard_map(
        functools.partial(on_device, sizes["sub"], sizes["tile"], sizes["face"]),
        mesh=mesh,
        in_specs=placed,
        out_specs=(
            P("sub", "face", "tile", "parts"),
            P("sub", "face", "tile", "parts"),
            P("parts", None, None, "sub"),
            P("parts", None, None, "sub"),
        ),
        check_vma=False,
    )
```

```python
import functools

import jax
import jax.numpy as jnp
from jax import lax
from jax.experimental import pallas as pl
from jax.experimental.pallas import tpu as pltpu
from jax.sharding import PartitionSpec as P

MESH = pl.DeviceIdType.MESH
F32 = jnp.float32
BF16 = jnp.bfloat16
LANES = 128


def gelu_parts(v):
    root = 0.7978845608028654
    cube = 0.044715 * (v * v * v)
    th = jnp.tanh(root * (v + cube))
    value = v * (0.5 * (1.0 + th))
    slope = 0.5 * (1.0 + th) + 0.5 * v * (1.0 - th * th) * root * (1.0 + 0.134145 * (v * v))
    return value, slope


def product(a, b, da, db):
    return lax.dot_general(a, b, (((da,), (db,)), ((), ())), preferred_element_type=F32)


def body(n_t, n_f, scale, groups, fields_h, upstream_h, k1_h, k2_h, res_o, fg_o, w1_o, w2_o,
         raw, x, k1, k2, y, rows, lh, rh, ap, bm, aps, tr, dr, tl, dl, al, pad, xb, xf1, xf2, xc, kf, kb, kl, lm, pad2, pre, back,
         acc, sbuf, rlow, rfull, obuf,
         col_s, col_r, line_s, a_r, b_r, t_s, d_s, row_r, w_s, w_r):
    _, G, J, H, C = x.shape
    S = H // 3
    E = J + 2
    W = xc.shape[1] // 9
    t = lax.axis_index("tile")
    f = lax.axis_index("face")
    fn = lax.rem(f + 1, n_f)
    fp = lax.rem(f + n_f - 1, n_f)
    first = t == 0
    last = t == n_t - 1
    inner_left = jnp.logical_not(first)
    inner_right = jnp.logical_not(last)

    upper, lower = slice(S, H), slice(0, 2 * S)

    def where_to(tile, face):
        return {"tile": tile, "face": face}

    def remote(src, dst, s, r, dev):
        return pltpu.make_async_remote_copy(
            src_ref=src, dst_ref=dst, send_sem=s, recv_sem=r, device_id=dev, device_id_type=MESH)

    def settle(ref, sem):
        pltpu.make_async_copy(ref, ref, sem).wait()

    def copies(p, src):
        c0, cl = src.at[:, :, 0], src.at[:, :, J - 1]
        right = lambda: remote(cl, lh.at[p], col_s.at[0], col_r.at[p, 0], where_to(jnp.minimum(t + 1, n_t - 1), f))
        left = lambda: remote(c0, rh.at[p], col_s.at[1], col_r.at[p, 1], where_to(jnp.maximum(t - 1, 0), f))
        seam = []
        if G > 1:
            seam.append((first, lambda: remote(src.at[:, 1:G, 0, upper], rh.at[p, :, 0:G - 1, upper], col_s.at[1], col_r.at[p, 1], where_to(n_t - 1, f))))
            seam.append((last, lambda: remote(src.at[:, 0:G - 1, J - 1, lower], lh.at[p, :, 1:G, lower], col_s.at[0], col_r.at[p, 0], where_to(0, f))))
        seam.append((first, lambda: remote(src.at[:, 0:1, 0, upper], rh.at[p, :, G - 1:G, upper], col_s.at[1], col_r.at[p, 1], where_to(n_t - 1, fp))))
        seam.append((last, lambda: remote(src.at[:, G - 1:G, J - 1, lower], lh.at[p, :, 0:1, lower], col_s.at[0], col_r.at[p, 0], where_to(0, fn))))
        a_own = lambda d: remote(aps.at[p, d, :, 1:G], ap.at[p, :, 0:G - 1], line_s.at[0], a_r.at[p], where_to(d, f))
        a_oth = lambda d: remote(aps.at[p, d, :, 0:1], ap.at[p, :, G - 1:G], line_s.at[1], a_r.at[p], where_to(d, fp))
        b_own = lambda d: remote(aps.at[p, d, :, 0:G - 1], bm.at[p, :, 1:G], line_s.at[0], b_r.at[p], where_to(d, f))
        b_oth = lambda d: remote(aps.at[p, d, :, G - 1:G], bm.at[p, :, 0:1], line_s.at[1], b_r.at[p], where_to(d, fn))
        t_own = lambda d: remote(rows.at[p, 0, :, 0:G - 1], tr.at[p, d, :, 1:G], t_s.at[0], row_r.at[p, 0], where_to(0, f))
        t_oth = lambda d: remote(rows.at[p, 0, :, G - 1:G], tr.at[p, d, :, 0:1], t_s.at[0], row_r.at[p, 1], where_to(0, fn))
        d_own = lambda d: remote(rows.at[p, 1, :, 1:G], dr.at[p, d, :, 0:G - 1], d_s.at[0], row_r.at[p, 0], where_to(n_t - 1, f))
        d_oth = lambda d: remote(rows.at[p, 1, :, 0:1], dr.at[p, d, :, G - 1:G], d_s.at[0], row_r.at[p, 1], where_to(n_t - 1, fp))
        return right, left, seam, a_own, a_oth, b_own, b_oth, t_own, t_oth, d_own, d_oth

    def stage(p, kind, src):
        for q in range(G):
            for j in range(J):
                rows[p, 0, kind, q, j:j + 1, :] = src[kind, q, j, 0:16].astype(F32)[0:1]
                rows[p, 1, kind, q, j:j + 1, :] = src[kind, q, j, H - 16:H].astype(F32)[15:16]
        more = 16 * kind

        @pl.when(first)
        def _():
            for q in range(G):
                al[kind, q, 16:16 + S + more, :] = src[kind, q, 0, 0:S + more].astype(F32)
            for d in range(n_t):
                aps[p, d, kind] = al[kind, :, 15 + d * J:15 + d * J + E, :]

        @pl.when(last)
        def _():
            for q in range(G):
                al[kind, q, 16 - more:16 + S, :] = src[kind, q, J - 1, 2 * S - more:H].astype(F32)
            for d in range(n_t):
                aps[p, d, kind] = al[kind, :, 15 + d * J:15 + d * J + E, :]

    def start_far(p, src):
        right, left, seam, a_own, a_oth, b_own, b_oth, t_own, t_oth, d_own, d_oth = copies(p, src)
        half = n_t // 2

        @pl.when(first)
        def _():
            @pl.loop(0, n_t - half)
            def _(d):
                a_oth(n_t - 1 - d).start()
                if G > 1:
                    a_own(n_t - 1 - d).start()

        @pl.when(last)
        def _():
            @pl.loop(0, half)
            def _(d):
                b_oth(d).start()
                if G > 1:
                    b_own(d).start()
        for cond, make in seam:
            @pl.when(cond)
            def _(make=make):
                make().start()

        @pl.when(first)
        def _():
            a_oth(0).start()

            @pl.loop(1, half)
            def _(d):
                a_oth(half - d).start()
                if G > 1:
                    a_own(half - d).start()
            if G > 1:
                ap[p, :, 0:G - 1] = aps[p, 0, :, 1:G]
                tr[p, 0, :, 1:G] = rows[p, 0, :, 0:G - 1]

        @pl.when(last)
        def _():
            b_oth(n_t - 1).start()

            @pl.loop(half, n_t - 1)
            def _(d):
                b_oth(d).start()
                if G > 1:
                    b_own(d).start()
            if G > 1:
                bm[p, :, 1:G] = aps[p, n_t - 1, :, 0:G - 1]
                dr[p, n_t - 1, :, 0:G - 1] = rows[p, 1, :, 1:G]
        t_oth(t).start()
        d_oth(t).start()
        if G > 1:
            @pl.when(inner_left)
            def _():
                t_own(t).start()

            @pl.when(inner_right)
            def _():
                d_own(t).start()

    def start_near(p, src):
        right, left = copies(p, src)[0:2]

        @pl.when(inner_right)
        def _():
            right().start()

        @pl.when(inner_left)
        def _():
            left().start()

    def await_arrivals(p, src):
        right, left = copies(p, src)[0:2]

        @pl.when(inner_left)
        def _():
            right().wait_recv()
            settle(ap.at[p], a_r.at[p])

        @pl.when(first)
        def _():
            settle(ap.at[p, :, G - 1:G], a_r.at[p])

        @pl.when(inner_right)
        def _():
            left().wait_recv()
            settle(bm.at[p], b_r.at[p])

        @pl.when(last)
        def _():
            settle(bm.at[p, :, 0:1], b_r.at[p])

    def await_seam(p):
        @pl.when(last)
        def _():
            settle(rh.at[p, :, :, upper], col_r.at[p, 1])

        @pl.when(first)
        def _():
            settle(lh.at[p, :, :, lower], col_r.at[p, 0])

        @pl.when(first)
        def _():
            if G > 1:
                settle(tr.at[p, 1:n_t, :, 1:G], row_r.at[p, 0])
            settle(tr.at[p, :, :, 0:1], row_r.at[p, 1])
            for d in range(n_t):
                tl[:, :, 8 + d * J:8 + (d + 1) * J, :] = tr[p, d]

        @pl.when(last)
        def _():
            if G > 1:
                settle(dr.at[p, 0:n_t - 1, :, 0:G - 1], row_r.at[p, 0])
            settle(dr.at[p, :, :, G - 1:G], row_r.at[p, 1])
            for d in range(n_t):
                dl[:, :, 8 + d * J:8 + (d + 1) * J, :] = dr[p, d]

    def await_sends(p, src):
        right, left = copies(p, src)[0:2]

        @pl.when(inner_right)
        def _():
            right().wait_send()
            settle(rows.at[p, 1], d_s.at[0])

        @pl.when(last)
        def _():
            settle(src.at[:, :, J - 1, lower], col_s.at[0])
            settle(rows.at[p, 1, :, 0:1], d_s.at[0])

        @pl.when(inner_left)
        def _():
            left().wait_send()
            settle(rows.at[p, 0], t_s.at[0])

        @pl.when(first)
        def _():
            settle(src.at[:, :, 0, upper], col_s.at[1])
            settle(rows.at[p, 0, :, G - 1:G], t_s.at[0])

        @pl.when(jnp.logical_or(first, last))
        def _():
            if G > 1:
                settle(aps.at[p, 1:n_t, :, 1:G], line_s.at[0])
            settle(aps.at[p, :, :, 0:1], line_s.at[1])

    def fill_columns(src):
        for q in range(G):
            for j in range(J):
                pad[q, 1 + j, 8:8 + H, :] = src[q, j].astype(F32)

    def forward_taps(p, src, out, late):
        fill_columns(src)
        for q in range(G):
            @pl.when(inner_left)
            def _():
                pad[q, 0, 8:8 + H, :] = lh[p, 0, q].astype(F32)

            @pl.when(inner_right)
            def _():
                pad[q, J + 1, 8:8 + H, :] = rh[p, 0, q].astype(F32)

            if late:
                @pl.when(first)
                def _():
                    pad[q, 0, 8:8 + H, :] = jnp.zeros((H, C), F32)

                @pl.when(last)
                def _():
                    pad[q, J + 1, 8:8 + H, :] = jnp.zeros((H, C), F32)
            else:
                @pl.when(first)
                def _():
                    forward_edge(p, q, 0)

                @pl.when(last)
                def _():
                    forward_edge(p, q, J + 1)
            for j in range(E):
                pad[q, j, 7:8, :] = ap[p, 0, q, j:j + 1]
                pad[q, j, 8 + H:9 + H, :] = bm[p, 0, q, j:j + 1]
        for a in range(3):
            for b in range(3):
                for q in range(G):
                    for j in range(J):
                        m = (q * J + j) * H
                        n = 3 * a + b
                        out[m:m + H, n * W:n * W + C] = pad[q, j + a, 7 + b:7 + b + H, :].astype(BF16)

    def forward_edge(p, q, j):
        if j == 0:
            pad[q, 0, 8:8 + S, :] = tl[0, q, 8:8 + S, :]
            pad[q, 0, 8 + S:8 + H, :] = lh[p, 0, q, 0:2 * S].astype(F32)
        else:
            pad[q, J + 1, 8:8 + 2 * S, :] = rh[p, 0, q, S:H].astype(F32)
            pad[q, J + 1, 8 + 2 * S:8 + H, :] = dl[0, q, 8:8 + S, :]

    def forward_late(p, out, k, total):
        for cond, a, j in ((first, 0, 0), (last, 2, J + 1)):
            @pl.when(cond)
            def _(a=a, j=j):
                for q in range(G):
                    forward_edge(p, q, j)
                    m = (q * J + j - a) * H
                    for b in range(3):
                        n = 3 * a + b
                        out[m:m + H, n * W:n * W + C] = pad[q, j, 7 + b:7 + b + H, :].astype(BF16)
                    wide = slice(3 * a * W, 3 * (a + 1) * W)
                    total[m:m + H, :] += product(out[m:m + H, wide], k[wide], 1, 0)

    def backward_taps(p, src, out, late):
        fill_columns(src)
        for q in range(G):
            @pl.when(inner_left)
            def _():
                pad[q, 0, 8:8 + H, :] = lh[p, 1, q].astype(F32)

            @pl.when(first)
            def _():
                pad[q, 0, :, :] = jnp.zeros((H + 16, C), F32)

            @pl.when(inner_right)
            def _():
                pad[q, J + 1, 8:8 + H, :] = rh[p, 1, q].astype(F32)

            @pl.when(last)
            def _():
                pad[q, J + 1, :, :] = jnp.zeros((H + 16, C), F32)
            for j in range(E):
                pad[q, j, 7:8, :] = jnp.zeros((1, C), F32)
                pad[q, j, 8 + H:9 + H, :] = jnp.zeros((1, C), F32)
        for a in range(3):
            for b in range(3):
                for q in range(G):
                    for j in range(J):
                        m = (q * J + j) * H
                        out[3 * a + b, m:m + H, :] = pad[q, j - a + 2, 9 - b:9 - b + H, :]
        for q in range(G):
            top = ap[p, 1, q]
            low = bm[p, 1, q]
            for b in range(3):
                for j in range(J):
                    m = (q * J + j) * H
                    out[b, m:m + 1, :] += top[j + 2 - b:j + 3 - b]
                    out[6 + b, m + H - 1:m + H, :] += low[j + 2 - b:j + 3 - b]
        if not late:
            backward_late(p, out, None, None)
        for n in range(9):
            xc[:, n * W:n * W + C] = out[n].astype(BF16)

    def backward_late(p, out, k, total):
        def add(n, m, rows_at, value):
            here = slice(m + rows_at.start, m + rows_at.stop)
            out[n, here, :] += value
            if total is not None:
                xc[here, n * W:n * W + C] = out[n, here, :].astype(BF16)
                total[here, :] += product(value.astype(BF16), k[n * W:n * W + C], 1, 0)

        @pl.when(last)
        def _():
            for q in range(G):
                m = (q * J + J - 1) * H
                pad[q, J + 1, 8 + S:8 + H, :] = rh[p, 1, q, S:H].astype(F32)
                pad[q, J + 1, 7 + S:8 + S, :] = ap[p, 1, q, J:J + 1]
                pad[q, J + 1, 8 + H:9 + H, :] = jnp.zeros((1, C), F32)
                for e in range(3):
                    add(e, m, slice(0, 2 * S), pad[q, J + 1, 8 + S + 1 - e:8 + H + 1 - e, :])
                    add(3 * e + 2, m, slice(2 * S, H), dl[1, q, 9 - e:9 - e + S, :])

        @pl.when(first)
        def _():
            for q in range(G):
                m = q * J * H
                pad[q, 0, 7:8, :] = jnp.zeros((1, C), F32)
                pad[q, 0, 8:8 + 2 * S, :] = lh[p, 1, q, 0:2 * S].astype(F32)
                pad[q, 0, 8 + 2 * S:9 + 2 * S, :] = bm[p, 1, q, 1:2]
                for e in range(3):
                    add(3 * e, m, slice(0, S), tl[1, q, 9 - e:9 - e + S, :])
                    add(6 + e, m, slice(S, H), pad[q, 0, 9 - e:9 - e + 2 * S, :])

    def own_forward(src, k, out, total):
        fill_columns(src)
        for q in range(G):
            for j in (0, J + 1):
                pad[q, j, :, :] = jnp.zeros((H + 16, C), F32)
            for j in range(1, J + 1):
                pad[q, j, 7:8, :] = jnp.zeros((1, C), F32)
                pad[q, j, 8 + H:9 + H, :] = jnp.zeros((1, C), F32)
        for a in range(3):
            for b in range(3):
                for q in range(G):
                    for j in range(J):
                        m, n = (q * J + j) * H, 3 * a + b
                        out[m:m + H, n * W:n * W + C] = pad[q, j + a, 7 + b:7 + b + H, :].astype(BF16)
        total[...] = apply(out, k)

    def more_forward(p, k, out, total):
        for q in range(G):
            @pl.when(inner_left)
            def _():
                pad[q, 0, 8:8 + H, :] = lh[p, 0, q].astype(F32)

            @pl.when(inner_right)
            def _():
                pad[q, J + 1, 8:8 + H, :] = rh[p, 0, q].astype(F32)
            for j in range(E):
                pad[q, j, 7:8, :] = ap[p, 0, q, j:j + 1]
                pad[q, j, 8 + H:9 + H, :] = bm[p, 0, q, j:j + 1]
        for q in range(G):
            for j in range(J):
                r = q * J + j
                m = r * H
                for a in range(3):
                    e = j + a
                    if e == 0 or e == J + 1:
                        for b in range(3):
                            n = 3 * a + b
                            out[m:m + H, n * W:n * W + C] = pad[q, e, 7 + b:7 + b + H, :].astype(BF16)
                        wide = slice(3 * a * W, 3 * (a + 1) * W)
                        total[m:m + H, :] += product(out[m:m + H, wide], k[wide], 1, 0)
                    else:
                        n = 3 * a
                        out[m:m + 16, n * W:n * W + C] = pad[q, e, 7:23, :].astype(BF16)
                        n = 3 * a + 2
                        out[m + H - 16:m + H, n * W:n * W + C] = pad[q, e, H - 7:H + 9, :].astype(BF16)
                        lm[0, r:r + 1, a * W:a * W + C] = ap[p, 0, q, e:e + 1]
                        lm[1, r:r + 1, a * W:a * W + C] = bm[p, 0, q, e:e + 1]
        add_lines(0, kl[0], kl[1], total)

    def add_lines(at, k_top, k_low, total):
        top = product(lm[at].astype(BF16), k_top, 1, 0)
        low = product(lm[at + 1].astype(BF16), k_low, 1, 0)
        for r in range(G * J):
            m = r * H
            total[m:m + 1, :] += top[r:r + 1]
            total[m + H - 1:m + H, :] += low[r:r + 1]

    def own_backward(src, k, out, total):
        for q in range(G):
            for j in (0, J + 1):
                pad2[q, j, :, :] = jnp.zeros((H + 16, C), F32)
            for j in range(J):
                pad2[q, 1 + j, 8:8 + H, :] = src[q, j].astype(F32)
                pad2[q, 1 + j, 7:8, :] = jnp.zeros((1, C), F32)
                pad2[q, 1 + j, 8 + H:9 + H, :] = jnp.zeros((1, C), F32)
        for a in range(3):
            for b in range(3):
                n = 3 * a + b
                for q in range(G):
                    for j in range(J):
                        m = (q * J + j) * H
                        out[n, m:m + H, :] = pad2[q, j - a + 2, 9 - b:9 - b + H, :]
                xc[:, n * W:n * W + C] = out[n].astype(BF16)
        total[...] = apply(xc, k)

    def more_backward(p, k, out, total):
        for q in range(G):
            @pl.when(inner_left)
            def _():
                pad2[q, 0, 8:8 + H, :] = lh[p, 1, q].astype(F32)

            @pl.when(inner_right)
            def _():
                pad2[q, J + 1, 8:8 + H, :] = rh[p, 1, q].astype(F32)
        for q in range(G):
            top = ap[p, 1, q]
            low = bm[p, 1, q]
            for j in range(J):
                r = q * J + j
                m = r * H
                for a, line, at, lines in ((0, 0, 2, top), (2, H - 1, 3, low)):
                    e = j - a + 2
                    outer = e == 0 or e == J + 1
                    for b in range(3):
                        n = 3 * a + b
                        add = lines[j + 2 - b:j + 3 - b]
                        if outer:
                            out[n, m:m + H, :] = pad2[q, e, 9 - b:9 - b + H, :]
                        else:
                            lm[at, r:r + 1, b * W:b * W + C] = add
                        out[n, m + line:m + line + 1, :] += add
                        span = slice(m, m + H) if outer else slice(m, m + 16) if a == 0 else slice(m + H - 16, m + H)
                        xc[span, n * W:n * W + C] = out[n, span, :].astype(BF16)
                    if outer:
                        wide = slice(3 * a * W, 3 * (a + 1) * W)
                        total[m:m + H, :] += product(xc[m:m + H, wide], k[wide], 1, 0)
        add_lines(2, k[0:3 * W], k[6 * W:9 * W], total)

    def lay_out(k, w):
        for n in range(9):
            tap = k[n // 3, n % 3]
            kf[w, n * W:n * W + C] = tap
            kb[w, n * W:n * W + C] = tap.astype(F32).T.astype(BF16)
            if W > C:
                kf[w, n * W + C:n * W + W] = jnp.zeros((W - C, C), BF16)
                kb[w, n * W + C:n * W + W] = jnp.zeros((W - C, C), BF16)

    def apply(taps, k):
        return product(taps[...], k[...], 1, 0)

    def unflat(value, dst):
        for q in range(G):
            for j in range(J):
                m = (q * J + j) * H
                dst[q, j] = value[m:m + H]

    def channel_major(value, dst):
        for q in range(G):
            sides = [value[(q * J + j) * H:(q * J + j + 1) * H].T.astype(BF16) for j in range(J)]
            dst[:, q, :, :] = jnp.stack(sides, axis=1)

    per = C // 16
    tiles = -(-9 * C // LANES)
    blocks = acc.shape[1]

    def pack(terms, w):
        spare = tiles * LANES - 9 * C
        wide = jnp.concatenate(terms + ([jnp.zeros((C, spare), F32)] if spare else []), axis=1)
        for n in range(tiles):
            acc[w, n * per:(n + 1) * per] = wide[:, n * LANES:(n + 1) * LANES].reshape(per, 16, LANES)

    def unpack(w, out):
        parts = [obuf[w, n * per:(n + 1) * per].astype(F32).reshape(C, LANES) for n in range(tiles)]
        wide = jnp.concatenate(parts, axis=1)
        for n in range(9):
            out[n // 3, n % 3] = wide[:, n * C:(n + 1) * C]

    class Sum:
        def __init__(self, w, out):
            self.out, self.at, self.over = out, 0, False
            self.w, self.lo, self.length, self.done = w, 0, blocks, []
            self.used = [0, 0]
            self.sem = 0

        def members(self, bits):
            mine = []
            for axis, s in bits:
                mine.append(lax.rem((t if axis == "tile" else f) // s, 2))
            found = []
            for k in reversed(range(1, 2 ** len(bits))):
                tile, face, digit = t, f, 0
                for pos, (axis, s) in enumerate(bits):
                    bit = mine[pos]
                    if (k >> pos) & 1:
                        if axis == "tile":
                            tile = tile + (1 - 2 * bit) * s
                        else:
                            face = face + (1 - 2 * bit) * s
                        bit = 1 - bit
                    digit = digit + bit * (1 << pos)
                found.append((digit, where_to(tile, face)))
            own = 0
            for pos, bit in enumerate(mine):
                own = own + bit * (1 << pos)
            return own, found

        def begin(self, n):
            bits, full, whole = groups[n]
            own, found = self.members(bits)
            w = self.w
            inbox = rfull if full else rlow
            at = self.used[full]
            part = self.length if whole else self.length // (len(found) + 1)
            self.flying = (inbox, at, part, len(found), whole)
            if whole:
                piece = pl.ds(self.lo, part)
                mine = pl.ds(at + own * part, part)
                sbuf[w, piece] = acc[w, piece].astype(BF16)
                for digit, dev in found:
                    remote(sbuf.at[w, piece], inbox.at[w, mine], w_s.at[w], w_r.at[w, self.sem], dev).start()
                inbox[w, mine] = sbuf[w, piece]
                self.used[full] += part * (len(found) + 1)
                return
            for digit, dev in found:
                give = self.lo + digit * part
                if full:
                    out = acc.at[w, pl.ds(give, part)]
                else:
                    sbuf[w, pl.ds(give, part)] = acc[w, pl.ds(give, part)].astype(BF16)
                    out = sbuf.at[w, pl.ds(give, part)]
                at = self.used[full]
                self.used[full] += part
                remote(out, inbox.at[w, at:at + part], w_s.at[w], w_r.at[w, self.sem], dev).start()
            keep = self.lo + own * part
            self.done.append((keep, part, found))
            self.lo, self.length = keep, part

        def end(self):
            inbox, at, part, count, whole = self.flying
            sent = inbox.at[self.w, at:at + count * part]
            settle(sent, w_s.at[self.w])
            settle(sent, w_r.at[self.w, self.sem])
            self.sem += 1
            terms = [inbox[self.w, at + n * part:at + (n + 1) * part].astype(F32) for n in range(count + whole)]
            total = terms.pop(0) if whole else acc[self.w, pl.ds(self.lo, self.length)]
            for term in terms:
                total = total + term
            acc[self.w, pl.ds(self.lo, self.length)] = total

        def round(self):
            obuf[self.w, pl.ds(self.lo, self.length)] = acc[self.w, pl.ds(self.lo, self.length)].astype(BF16)

        def give(self):
            keep, part, found = self.done.pop()
            self.flying = (part, len(found))
            for digit, dev in found:
                remote(obuf.at[self.w, pl.ds(keep, part)], obuf.at[self.w, pl.ds(keep, part)],
                       w_s.at[self.w], w_r.at[self.w, self.sem], dev).start()

        def given(self):
            part, count = self.flying
            whole = obuf.at[self.w, 0:count * part]
            settle(whole, w_s.at[self.w])
            settle(whole, w_r.at[self.w, self.sem])
            self.sem += 1

        def advance(self):
            at, count = self.at, len(groups)
            self.at += 1
            if self.over:
                return
            if at < count:
                if at > 0:
                    self.end()
                self.begin(at)
                return
            if at == count:
                self.end()
                self.round()
            else:
                self.given()
            if self.done:
                self.give()
            else:
                unpack(self.w, self.out)
                self.over = True

    barrier = pltpu.get_barrier_semaphore()
    loads = [pltpu.make_async_copy(src, dst, sem) for src, dst, sem in (
        (fields_h, raw.at[0], w_s.at[0]), (upstream_h, raw.at[1], w_s.at[1]),
        (k1_h, k1, line_s.at[0]), (k2_h, k2, line_s.at[1]))]
    for load in loads:
        load.start()

    @pl.loop(0, n_f)
    def _(df):
        @pl.loop(0, n_t)
        def _(dt):
            @pl.when(jnp.logical_or(df != f, dt != t))
            def _():
                pl.semaphore_signal(barrier, inc=1, device_id=where_to(dt, df), device_id_type=MESH)
    hidden, pre_grad = y.at[0], y.at[1]
    al[...] = jnp.zeros_like(al)
    tl[...] = jnp.zeros_like(tl)
    dl[...] = jnp.zeros_like(dl)
    for kind in range(2):
        loads[kind].wait()
        for q in range(G):
            for j in range(J):
                x[kind, q, j] = raw[kind, :, q, j, :].astype(F32).T.astype(BF16)
        stage(0, kind, x)
    if blocks > tiles * per:
        for w in range(2):
            acc[w, tiles * per:blocks] = jnp.zeros((blocks - tiles * per, 16, LANES), F32)
    pl.semaphore_wait(barrier, n_t * n_f - 1)

    loads[2].wait()
    loads[3].wait()
    start_far(0, x)
    start_near(0, x)
    lay_out(k1, 0)
    lay_out(k2, 1)
    for a in range(3):
        for side in range(2):
            n = 3 * a + 2 * side
            kl[side, a * W:(a + 1) * W] = kf[0, n * W:(n + 1) * W]
    lm[...] = jnp.zeros_like(lm)
    for taps in (xf1, xf2, xc):
        taps[...] = jnp.zeros_like(taps)
    own_forward(x.at[0], kf.at[0], xf1, pre)
    own_backward(x.at[1], kb.at[1], xb, back)
    await_arrivals(0, x)
    more_forward(0, kf.at[0], xf1, pre)
    more_backward(0, kb.at[1], xb, back)
    await_seam(0)
    forward_late(0, xf1, kf.at[0], pre)
    backward_late(0, xb, kb.at[1], back)
    value, slope = gelu_parts(pre[...])
    cells = value.astype(BF16)
    unflat(cells, hidden)
    one, two = Sum(0, w1_o), Sum(1, w2_o)
    wide = product(cells, xc[...], 0, 0)
    pack([wide[:, n * W:n * W + C] * scale for n in range(9)], 1)
    two.advance()
    cot = (back[...] * slope).astype(BF16)
    unflat(cot, pre_grad)
    pack([product(xf1[:, n * W:n * W + C], cot, 0, 0) * scale for n in range(9)], 0)
    one.advance()
    two.advance()
    one.advance()
    await_sends(0, x)
    stage(1, 0, y)
    stage(1, 1, y)
    start_far(1, y)
    two.advance()
    one.advance()
    start_near(1, y)
    two.advance()
    one.advance()
    await_arrivals(1, y)
    await_seam(1)
    forward_taps(1, hidden, xf2, False)
    channel_major(apply(xf2, kf.at[1]), res_o)
    backward_taps(1, pre_grad, xb, False)
    channel_major(apply(xc, kb.at[0]), fg_o)
    while not (one.over and two.over):
        two.advance()
        one.advance()
    await_sends(1, y)


def deliver(*refs):
    sources, targets, sems = refs[0:4], refs[4:8], refs[8]
    moves = [pltpu.make_async_copy(a, b, sems.at[n]) for n, (a, b) in enumerate(zip(sources, targets))]
    for move in moves:
        move.start()
    for move in moves:
        move.wait()


def plan(n_t, n_f):
    tile_bits = [("tile", 1 << i) for i in range(n_t.bit_length() - 1)]
    face_bits = [("face", 1 << i) for i in range(n_f.bit_length() - 1)]
    groups = [(tile_bits[:1], 0, 0)]
    middle, rest = face_bits + tile_bits[1:3], tile_bits[3:]
    while middle:
        groups.append((middle[:3], 0, 0))
        middle = middle[3:]
    while len(rest) > 2:
        groups.append((rest[:2], 0, 0))
        rest = rest[2:]
    if rest:
        groups.append((rest, 0, 1))
    return groups


def run(fields, upstream, k1, k2, n_t, n_f):
    C, G, J, H = fields.shape
    S = H // 3
    E = J + 2
    M = G * J * H
    W = -(-C // LANES) * LANES
    scale = 1.0 / (S * 12.0 ** 0.5)
    groups = plan(n_t, n_f)
    cuts, stages = 1, 0
    for bits, full, whole in groups:
        cuts *= 1 if whole else 2 ** len(bits)
        stages += 1 if whole else 2
    blocks = -(-9 * C // LANES) * (C // 16)
    blocks = -(-blocks // cuts) * cuts
    length, room = blocks, [1, 1]
    for bits, full, whole in groups:
        members = 2 ** len(bits)
        if whole:
            room[full] += length * members
        else:
            length //= members
            room[full] += length * (members - 1)
    dma = pltpu.SemaphoreType.DMA
    vmem = pl.BlockSpec(memory_space=pltpu.VMEM)
    hbm = pl.BlockSpec(memory_space=pltpu.HBM)
    held = [pltpu.with_memory_space_constraint(a, pltpu.HBM) for a in (fields, upstream, k1, k2)]
    return pl.pallas_call(
        functools.partial(body, n_t, n_f, scale, groups),
        out_shape=(
            jax.ShapeDtypeStruct((C, G, J, H), BF16),
            jax.ShapeDtypeStruct((C, G, J, H), BF16),
            jax.ShapeDtypeStruct((3, 3, C, C), F32),
            jax.ShapeDtypeStruct((3, 3, C, C), F32),
        ),
        in_specs=[hbm] * 4,
        out_specs=[vmem] * 4,
        scratch_shapes=[
            pltpu.VMEM((2, C, G, J, H), BF16),
            pltpu.VMEM((2, G, J, H, C), BF16),
            pltpu.VMEM(k1.shape, BF16),
            pltpu.VMEM(k2.shape, BF16),
            pltpu.VMEM((2, G, J, H, C), BF16),
            pltpu.VMEM((2, 2, 2, G, J, C), F32),
            pltpu.VMEM((2, 2, G, H, C), BF16),
            pltpu.VMEM((2, 2, G, H, C), BF16),
            pltpu.VMEM((2, 2, G, E, C), F32),
            pltpu.VMEM((2, 2, G, E, C), F32),
            pltpu.VMEM((2, n_t, 2, G, E, C), F32),
            pltpu.VMEM((2, n_t, 2, G, J, C), F32),
            pltpu.VMEM((2, n_t, 2, G, J, C), F32),
            pltpu.VMEM((2, G, S + 16, C), F32),
            pltpu.VMEM((2, G, S + 16, C), F32),
            pltpu.VMEM((2, G, S + 32, C), F32),
            pltpu.VMEM((G, J + 2, H + 16, C), F32),
            pltpu.VMEM((9, M, C), F32),
            pltpu.VMEM((M, 9 * W), BF16),
            pltpu.VMEM((M, 9 * W), BF16),
            pltpu.VMEM((M, 9 * W), BF16),
            pltpu.VMEM((2, 9 * W, C), BF16),
            pltpu.VMEM((2, 9 * W, C), BF16),
            pltpu.VMEM((2, 3 * W, C), BF16),
            pltpu.VMEM((4, -(-G * J // 16) * 16, 3 * W), F32),
            pltpu.VMEM((G, J + 2, H + 16, C), F32),
            pltpu.VMEM((M, C), F32),
            pltpu.VMEM((M, C), F32),
            pltpu.VMEM((2, blocks, 16, LANES), F32),
            pltpu.VMEM((2, blocks, 16, LANES), BF16),
            pltpu.VMEM((2, room[0], 16, LANES), BF16),
            pltpu.VMEM((2, room[1], 16, LANES), F32),
            pltpu.VMEM((2, blocks, 16, LANES), BF16),
            dma((2,)), dma((2, 2)),
            dma((2,)), dma((2,)), dma((2,)),
            dma((1,)), dma((1,)), dma((2, 2)),
            dma((2,)), dma((2, stages)),
        ],
        compiler_params=pltpu.CompilerParams(
            collective_id=0, has_side_effects=True, vmem_limit_bytes=24 * 1024 * 1024),
    )(*held)


def send_out(made):
    vmem = pl.BlockSpec(memory_space=pltpu.VMEM)
    hbm = pl.BlockSpec(memory_space=pltpu.HBM)
    return pl.pallas_call(
        deliver,
        out_shape=[jax.ShapeDtypeStruct(a.shape, a.dtype) for a in made],
        in_specs=[vmem] * 4,
        out_specs=[hbm] * 4,
        scratch_shapes=[pltpu.SemaphoreType.DMA((4,))],
    )(*[pltpu.with_memory_space_constraint(a, pltpu.VMEM) for a in made])


def on_device(n_sub, n_t, n_f, fields, upstream, k1, k2):
    own = fields.shape[0]
    if n_sub > 1:
        fields = lax.all_gather(fields, "sub", axis=0, tiled=True)
        upstream = lax.all_gather(upstream, "sub", axis=0, tiled=True)
    made = run(fields, upstream, k1, k2, n_t, n_f)
    if n_sub > 1:
        at = lax.axis_index("sub") * own
        res, fgrad, w1, w2 = made
        return (
            lax.dynamic_slice_in_dim(res, at, own, 0),
            lax.dynamic_slice_in_dim(fgrad, at, own, 0),
            lax.dynamic_slice_in_dim(w1, at, own, 3),
            lax.dynamic_slice_in_dim(w2, at, own, 3),
        )
    return tuple(send_out(made))


def solution(mesh):
    placed = (P("sub", "face", "tile", "parts"), P("sub", "face", "tile", "parts"), P(), P())
    sizes = mesh.shape
    return jax.shard_map(
        functools.partial(on_device, sizes["sub"], sizes["tile"], sizes["face"]),
        mesh=mesh,
        in_specs=placed,
        out_specs=(
            P("sub", "face", "tile", "parts"),
            P("sub", "face", "tile", "parts"),
            P("parts", None, None, "sub"),
            P("parts", None, None, "sub"),
        ),
        check_vma=False,
    )
```

```python
import functools

import jax
import jax.numpy as jnp
from jax import lax
from jax.experimental import pallas as pl
from jax.experimental.pallas import tpu as pltpu
from jax.sharding import PartitionSpec as P

MESH = pl.DeviceIdType.MESH
F32 = jnp.float32
BF16 = jnp.bfloat16
LANES = 128


def gelu_parts(v):
    root = 0.7978845608028654
    cube = 0.044715 * (v * v * v)
    th = jnp.tanh(root * (v + cube))
    value = v * (0.5 * (1.0 + th))
    slope = 0.5 * (1.0 + th) + 0.5 * v * (1.0 - th * th) * root * (1.0 + 0.134145 * (v * v))
    return value, slope


def product(a, b, da, db):
    return lax.dot_general(a, b, (((da,), (db,)), ((), ())), preferred_element_type=F32)


def body(n_t, n_f, scale, groups, fields_h, upstream_h, k1_h, k2_h, res_o, fg_o, w1_o, w2_o,
         raw, x, k1, k2, y, rows, lh, rh, ap, bm, aps, tr, dr, tl, dl, al, pad, xb, xf1, xf2, xc, kf, kb, kl, lm, pad2, pre, back,
         acc, sbuf, rlow, rfull, obuf,
         col_s, col_r, line_s, a_r, b_r, t_s, d_s, row_r, w_s, w_r):
    _, G, J, H, C = x.shape
    S = H // 3
    E = J + 2
    W = xc.shape[1] // 9
    t = lax.axis_index("tile")
    f = lax.axis_index("face")
    fn = lax.rem(f + 1, n_f)
    fp = lax.rem(f + n_f - 1, n_f)
    first = t == 0
    last = t == n_t - 1
    inner_left = jnp.logical_not(first)
    inner_right = jnp.logical_not(last)

    upper, lower = slice(S, H), slice(0, 2 * S)

    def where_to(tile, face):
        return {"tile": tile, "face": face}

    def remote(src, dst, s, r, dev):
        return pltpu.make_async_remote_copy(
            src_ref=src, dst_ref=dst, send_sem=s, recv_sem=r, device_id=dev, device_id_type=MESH)

    def settle(ref, sem):
        pltpu.make_async_copy(ref, ref, sem).wait()

    def copies(p, src):
        c0, cl = src.at[:, :, 0], src.at[:, :, J - 1]
        right = lambda: remote(cl, lh.at[p], col_s.at[0], col_r.at[p, 0], where_to(jnp.minimum(t + 1, n_t - 1), f))
        left = lambda: remote(c0, rh.at[p], col_s.at[1], col_r.at[p, 1], where_to(jnp.maximum(t - 1, 0), f))
        seam = []
        if G > 1:
            seam.append((first, lambda: remote(src.at[:, 1:G, 0, upper], rh.at[p, :, 0:G - 1, upper], col_s.at[1], col_r.at[p, 1], where_to(n_t - 1, f))))
            seam.append((last, lambda: remote(src.at[:, 0:G - 1, J - 1, lower], lh.at[p, :, 1:G, lower], col_s.at[0], col_r.at[p, 0], where_to(0, f))))
        seam.append((first, lambda: remote(src.at[:, 0:1, 0, upper], rh.at[p, :, G - 1:G, upper], col_s.at[1], col_r.at[p, 1], where_to(n_t - 1, fp))))
        seam.append((last, lambda: remote(src.at[:, G - 1:G, J - 1, lower], lh.at[p, :, 0:1, lower], col_s.at[0], col_r.at[p, 0], where_to(0, fn))))
        a_own = lambda d: remote(aps.at[p, d, :, 1:G], ap.at[p, :, 0:G - 1], line_s.at[0], a_r.at[p], where_to(d, f))
        a_oth = lambda d: remote(aps.at[p, d, :, 0:1], ap.at[p, :, G - 1:G], line_s.at[1], a_r.at[p], where_to(d, fp))
        b_own = lambda d: remote(aps.at[p, d, :, 0:G - 1], bm.at[p, :, 1:G], line_s.at[0], b_r.at[p], where_to(d, f))
        b_oth = lambda d: remote(aps.at[p, d, :, G - 1:G], bm.at[p, :, 0:1], line_s.at[1], b_r.at[p], where_to(d, fn))
        t_own = lambda d: remote(rows.at[p, 0, :, 0:G - 1], tr.at[p, d, :, 1:G], t_s.at[0], row_r.at[p, 0], where_to(0, f))
        t_oth = lambda d: remote(rows.at[p, 0, :, G - 1:G], tr.at[p, d, :, 0:1], t_s.at[0], row_r.at[p, 1], where_to(0, fn))
        d_own = lambda d: remote(rows.at[p, 1, :, 1:G], dr.at[p, d, :, 0:G - 1], d_s.at[0], row_r.at[p, 0], where_to(n_t - 1, f))
        d_oth = lambda d: remote(rows.at[p, 1, :, 0:1], dr.at[p, d, :, G - 1:G], d_s.at[0], row_r.at[p, 1], where_to(n_t - 1, fp))
        return right, left, seam, a_own, a_oth, b_own, b_oth, t_own, t_oth, d_own, d_oth

    def stage(p, kind, src):
        for q in range(G):
            for j in range(J):
                rows[p, 0, kind, q, j:j + 1, :] = src[kind, q, j, 0:16].astype(F32)[0:1]
                rows[p, 1, kind, q, j:j + 1, :] = src[kind, q, j, H - 16:H].astype(F32)[15:16]
        more = 16 * kind

        @pl.when(first)
        def _():
            for q in range(G):
                al[kind, q, 16:16 + S + more, :] = src[kind, q, 0, 0:S + more].astype(F32)
            for d in range(n_t):
                aps[p, d, kind] = al[kind, :, 15 + d * J:15 + d * J + E, :]

        @pl.when(last)
        def _():
            for q in range(G):
                al[kind, q, 16 - more:16 + S, :] = src[kind, q, J - 1, 2 * S - more:H].astype(F32)
            for d in range(n_t):
                aps[p, d, kind] = al[kind, :, 15 + d * J:15 + d * J + E, :]

    def start_far(p, src):
        right, left, seam, a_own, a_oth, b_own, b_oth, t_own, t_oth, d_own, d_oth = copies(p, src)
        half = n_t // 2

        @pl.when(first)
        def _():
            @pl.loop(0, n_t - half)
            def _(d):
                a_oth(n_t - 1 - d).start()
                if G > 1:
                    a_own(n_t - 1 - d).start()

        @pl.when(last)
        def _():
            @pl.loop(0, half)
            def _(d):
                b_oth(d).start()
                if G > 1:
                    b_own(d).start()
        for cond, make in seam:
            @pl.when(cond)
            def _(make=make):
                make().start()

        @pl.when(first)
        def _():
            a_oth(0).start()

            @pl.loop(1, half)
            def _(d):
                a_oth(half - d).start()
                if G > 1:
                    a_own(half - d).start()
            if G > 1:
                ap[p, :, 0:G - 1] = aps[p, 0, :, 1:G]
                tr[p, 0, :, 1:G] = rows[p, 0, :, 0:G - 1]

        @pl.when(last)
        def _():
            b_oth(n_t - 1).start()

            @pl.loop(half, n_t - 1)
            def _(d):
                b_oth(d).start()
                if G > 1:
                    b_own(d).start()
            if G > 1:
                bm[p, :, 1:G] = aps[p, n_t - 1, :, 0:G - 1]
                dr[p, n_t - 1, :, 0:G - 1] = rows[p, 1, :, 1:G]
        t_oth(t).start()
        d_oth(t).start()
        if G > 1:
            @pl.when(inner_left)
            def _():
                t_own(t).start()

            @pl.when(inner_right)
            def _():
                d_own(t).start()

    def start_near(p, src):
        right, left = copies(p, src)[0:2]

        @pl.when(inner_right)
        def _():
            right().start()

        @pl.when(inner_left)
        def _():
            left().start()

    def await_arrivals(p, src):
        right, left = copies(p, src)[0:2]

        @pl.when(inner_left)
        def _():
            right().wait_recv()
            settle(ap.at[p], a_r.at[p])

        @pl.when(first)
        def _():
            settle(ap.at[p, :, G - 1:G], a_r.at[p])

        @pl.when(inner_right)
        def _():
            left().wait_recv()
            settle(bm.at[p], b_r.at[p])

        @pl.when(last)
        def _():
            settle(bm.at[p, :, 0:1], b_r.at[p])

    def await_seam(p):
        @pl.when(last)
        def _():
            settle(rh.at[p, :, :, upper], col_r.at[p, 1])

        @pl.when(first)
        def _():
            settle(lh.at[p, :, :, lower], col_r.at[p, 0])

        @pl.when(first)
        def _():
            if G > 1:
                settle(tr.at[p, 1:n_t, :, 1:G], row_r.at[p, 0])
            settle(tr.at[p, :, :, 0:1], row_r.at[p, 1])
            for d in range(n_t):
                tl[:, :, 8 + d * J:8 + (d + 1) * J, :] = tr[p, d]

        @pl.when(last)
        def _():
            if G > 1:
                settle(dr.at[p, 0:n_t - 1, :, 0:G - 1], row_r.at[p, 0])
            settle(dr.at[p, :, :, G - 1:G], row_r.at[p, 1])
            for d in range(n_t):
                dl[:, :, 8 + d * J:8 + (d + 1) * J, :] = dr[p, d]

    def await_sends(p, src):
        right, left = copies(p, src)[0:2]

        @pl.when(inner_right)
        def _():
            right().wait_send()
            settle(rows.at[p, 1], d_s.at[0])

        @pl.when(last)
        def _():
            settle(src.at[:, :, J - 1, lower], col_s.at[0])
            settle(rows.at[p, 1, :, 0:1], d_s.at[0])

        @pl.when(inner_left)
        def _():
            left().wait_send()
            settle(rows.at[p, 0], t_s.at[0])

        @pl.when(first)
        def _():
            settle(src.at[:, :, 0, upper], col_s.at[1])
            settle(rows.at[p, 0, :, G - 1:G], t_s.at[0])

        @pl.when(jnp.logical_or(first, last))
        def _():
            if G > 1:
                settle(aps.at[p, 1:n_t, :, 1:G], line_s.at[0])
            settle(aps.at[p, :, :, 0:1], line_s.at[1])

    def fill_columns(src):
        for q in range(G):
            for j in range(J):
                pad[q, 1 + j, 8:8 + H, :] = src[q, j].astype(F32)

    def forward_taps(p, src, out, late):
        fill_columns(src)
        for q in range(G):
            @pl.when(inner_left)
            def _():
                pad[q, 0, 8:8 + H, :] = lh[p, 0, q].astype(F32)

            @pl.when(inner_right)
            def _():
                pad[q, J + 1, 8:8 + H, :] = rh[p, 0, q].astype(F32)

            if late:
                @pl.when(first)
                def _():
                    pad[q, 0, 8:8 + H, :] = jnp.zeros((H, C), F32)

                @pl.when(last)
                def _():
                    pad[q, J + 1, 8:8 + H, :] = jnp.zeros((H, C), F32)
            else:
                @pl.when(first)
                def _():
                    forward_edge(p, q, 0)

                @pl.when(last)
                def _():
                    forward_edge(p, q, J + 1)
            for j in range(E):
                pad[q, j, 7:8, :] = ap[p, 0, q, j:j + 1]
                pad[q, j, 8 + H:9 + H, :] = bm[p, 0, q, j:j + 1]
        for a in range(3):
            for b in range(3):
                for q in range(G):
                    for j in range(J):
                        m = (q * J + j) * H
                        n = 3 * a + b
                        out[m:m + H, n * W:n * W + C] = pad[q, j + a, 7 + b:7 + b + H, :].astype(BF16)

    def forward_edge(p, q, j):
        if j == 0:
            pad[q, 0, 8:8 + S, :] = tl[0, q, 8:8 + S, :]
            pad[q, 0, 8 + S:8 + H, :] = lh[p, 0, q, 0:2 * S].astype(F32)
        else:
            pad[q, J + 1, 8:8 + 2 * S, :] = rh[p, 0, q, S:H].astype(F32)
            pad[q, J + 1, 8 + 2 * S:8 + H, :] = dl[0, q, 8:8 + S, :]

    def forward_late(p, out, k, total):
        for cond, a, j in ((first, 0, 0), (last, 2, J + 1)):
            @pl.when(cond)
            def _(a=a, j=j):
                for q in range(G):
                    forward_edge(p, q, j)
                    m = (q * J + j - a) * H
                    for b in range(3):
                        n = 3 * a + b
                        out[m:m + H, n * W:n * W + C] = pad[q, j, 7 + b:7 + b + H, :].astype(BF16)
                    wide = slice(3 * a * W, 3 * (a + 1) * W)
                    total[m:m + H, :] += product(out[m:m + H, wide], k[wide], 1, 0)

    def backward_taps(p, src, out, late):
        fill_columns(src)
        for q in range(G):
            @pl.when(inner_left)
            def _():
                pad[q, 0, 8:8 + H, :] = lh[p, 1, q].astype(F32)

            @pl.when(first)
            def _():
                pad[q, 0, :, :] = jnp.zeros((H + 16, C), F32)

            @pl.when(inner_right)
            def _():
                pad[q, J + 1, 8:8 + H, :] = rh[p, 1, q].astype(F32)

            @pl.when(last)
            def _():
                pad[q, J + 1, :, :] = jnp.zeros((H + 16, C), F32)
            for j in range(E):
                pad[q, j, 7:8, :] = jnp.zeros((1, C), F32)
                pad[q, j, 8 + H:9 + H, :] = jnp.zeros((1, C), F32)
        for a in range(3):
            for b in range(3):
                for q in range(G):
                    for j in range(J):
                        m = (q * J + j) * H
                        out[3 * a + b, m:m + H, :] = pad[q, j - a + 2, 9 - b:9 - b + H, :]
        for q in range(G):
            top = ap[p, 1, q]
            low = bm[p, 1, q]
            for b in range(3):
                for j in range(J):
                    m = (q * J + j) * H
                    out[b, m:m + 1, :] += top[j + 2 - b:j + 3 - b]
                    out[6 + b, m + H - 1:m + H, :] += low[j + 2 - b:j + 3 - b]
        if not late:
            backward_late(p, out, None, None)
        for n in range(9):
            xc[:, n * W:n * W + C] = out[n].astype(BF16)

    def backward_late(p, out, k, total):
        def add(n, m, rows_at, value):
            here = slice(m + rows_at.start, m + rows_at.stop)
            out[n, here, :] += value
            if total is not None:
                xc[here, n * W:n * W + C] = out[n, here, :].astype(BF16)
                total[here, :] += product(value.astype(BF16), k[n * W:n * W + C], 1, 0)

        @pl.when(last)
        def _():
            for q in range(G):
                m = (q * J + J - 1) * H
                pad[q, J + 1, 8 + S:8 + H, :] = rh[p, 1, q, S:H].astype(F32)
                pad[q, J + 1, 7 + S:8 + S, :] = ap[p, 1, q, J:J + 1]
                pad[q, J + 1, 8 + H:9 + H, :] = jnp.zeros((1, C), F32)
                for e in range(3):
                    add(e, m, slice(0, 2 * S), pad[q, J + 1, 8 + S + 1 - e:8 + H + 1 - e, :])
                    add(3 * e + 2, m, slice(2 * S, H), dl[1, q, 9 - e:9 - e + S, :])

        @pl.when(first)
        def _():
            for q in range(G):
                m = q * J * H
                pad[q, 0, 7:8, :] = jnp.zeros((1, C), F32)
                pad[q, 0, 8:8 + 2 * S, :] = lh[p, 1, q, 0:2 * S].astype(F32)
                pad[q, 0, 8 + 2 * S:9 + 2 * S, :] = bm[p, 1, q, 1:2]
                for e in range(3):
                    add(3 * e, m, slice(0, S), tl[1, q, 9 - e:9 - e + S, :])
                    add(6 + e, m, slice(S, H), pad[q, 0, 9 - e:9 - e + 2 * S, :])

    def own_forward(src, k, out, total):
        fill_columns(src)
        for q in range(G):
            for j in (0, J + 1):
                pad[q, j, :, :] = jnp.zeros((H + 16, C), F32)
            for j in range(1, J + 1):
                pad[q, j, 7:8, :] = jnp.zeros((1, C), F32)
                pad[q, j, 8 + H:9 + H, :] = jnp.zeros((1, C), F32)
        for a in range(3):
            for b in range(3):
                for q in range(G):
                    for j in range(J):
                        m, n = (q * J + j) * H, 3 * a + b
                        out[m:m + H, n * W:n * W + C] = pad[q, j + a, 7 + b:7 + b + H, :].astype(BF16)
        total[...] = apply(out, k)

    def more_forward(p, k, out, total):
        for q in range(G):
            @pl.when(inner_left)
            def _():
                pad[q, 0, 8:8 + H, :] = lh[p, 0, q].astype(F32)

            @pl.when(inner_right)
            def _():
                pad[q, J + 1, 8:8 + H, :] = rh[p, 0, q].astype(F32)
            for j in range(E):
                pad[q, j, 7:8, :] = ap[p, 0, q, j:j + 1]
                pad[q, j, 8 + H:9 + H, :] = bm[p, 0, q, j:j + 1]
        for q in range(G):
            for j in range(J):
                r = q * J + j
                m = r * H
                for a in range(3):
                    e = j + a
                    if e == 0 or e == J + 1:
                        for b in range(3):
                            n = 3 * a + b
                            out[m:m + H, n * W:n * W + C] = pad[q, e, 7 + b:7 + b + H, :].astype(BF16)
                        wide = slice(3 * a * W, 3 * (a + 1) * W)
                        total[m:m + H, :] += product(out[m:m + H, wide], k[wide], 1, 0)
                    else:
                        n = 3 * a
                        out[m:m + 16, n * W:n * W + C] = pad[q, e, 7:23, :].astype(BF16)
                        n = 3 * a + 2
                        out[m + H - 16:m + H, n * W:n * W + C] = pad[q, e, H - 7:H + 9, :].astype(BF16)
                        lm[0, r:r + 1, a * W:a * W + C] = ap[p, 0, q, e:e + 1]
                        lm[1, r:r + 1, a * W:a * W + C] = bm[p, 0, q, e:e + 1]
        add_lines(0, kl[0], kl[1], total)

    def add_lines(at, k_top, k_low, total):
        top = product(lm[at].astype(BF16), k_top, 1, 0)
        low = product(lm[at + 1].astype(BF16), k_low, 1, 0)
        for r in range(G * J):
            m = r * H
            total[m:m + 1, :] += top[r:r + 1]
            total[m + H - 1:m + H, :] += low[r:r + 1]

    def own_backward(src, k, out, total):
        for q in range(G):
            for j in (0, J + 1):
                pad2[q, j, :, :] = jnp.zeros((H + 16, C), F32)
            for j in range(J):
                pad2[q, 1 + j, 8:8 + H, :] = src[q, j].astype(F32)
                pad2[q, 1 + j, 7:8, :] = jnp.zeros((1, C), F32)
                pad2[q, 1 + j, 8 + H:9 + H, :] = jnp.zeros((1, C), F32)
        for a in range(3):
            for b in range(3):
                n = 3 * a + b
                for q in range(G):
                    for j in range(J):
                        m = (q * J + j) * H
                        out[n, m:m + H, :] = pad2[q, j - a + 2, 9 - b:9 - b + H, :]
                xc[:, n * W:n * W + C] = out[n].astype(BF16)
        total[...] = apply(xc, k)

    def more_backward(p, k, out, total):
        for q in range(G):
            @pl.when(inner_left)
            def _():
                pad2[q, 0, 8:8 + H, :] = lh[p, 1, q].astype(F32)

            @pl.when(inner_right)
            def _():
                pad2[q, J + 1, 8:8 + H, :] = rh[p, 1, q].astype(F32)
        for q in range(G):
            top = ap[p, 1, q]
            low = bm[p, 1, q]
            for j in range(J):
                r = q * J + j
                m = r * H
                for a, line, at, lines in ((0, 0, 2, top), (2, H - 1, 3, low)):
                    e = j - a + 2
                    outer = e == 0 or e == J + 1
                    for b in range(3):
                        n = 3 * a + b
                        add = lines[j + 2 - b:j + 3 - b]
                        if outer:
                            out[n, m:m + H, :] = pad2[q, e, 9 - b:9 - b + H, :]
                        else:
                            lm[at, r:r + 1, b * W:b * W + C] = add
                        out[n, m + line:m + line + 1, :] += add
                        span = slice(m, m + H) if outer else slice(m, m + 16) if a == 0 else slice(m + H - 16, m + H)
                        xc[span, n * W:n * W + C] = out[n, span, :].astype(BF16)
                    if outer:
                        wide = slice(3 * a * W, 3 * (a + 1) * W)
                        total[m:m + H, :] += product(xc[m:m + H, wide], k[wide], 1, 0)
        add_lines(2, k[0:3 * W], k[6 * W:9 * W], total)

    def lay_out(k, w):
        for n in range(9):
            tap = k[n // 3, n % 3]
            kf[w, n * W:n * W + C] = tap
            kb[w, n * W:n * W + C] = tap.astype(F32).T.astype(BF16)
            if W > C:
                kf[w, n * W + C:n * W + W] = jnp.zeros((W - C, C), BF16)
                kb[w, n * W + C:n * W + W] = jnp.zeros((W - C, C), BF16)

    def apply(taps, k):
        return product(taps[...], k[...], 1, 0)

    def unflat(value, dst):
        for q in range(G):
            for j in range(J):
                m = (q * J + j) * H
                dst[q, j] = value[m:m + H]

    def channel_major(value, dst):
        for q in range(G):
            sides = [value[(q * J + j) * H:(q * J + j + 1) * H].T.astype(BF16) for j in range(J)]
            dst[:, q, :, :] = jnp.stack(sides, axis=1)

    per = C // 16
    tiles = -(-9 * C // LANES)
    blocks = acc.shape[1]

    def pack(terms, w):
        spare = tiles * LANES - 9 * C
        wide = jnp.concatenate(terms + ([jnp.zeros((C, spare), F32)] if spare else []), axis=1)
        for n in range(tiles):
            acc[w, n * per:(n + 1) * per] = wide[:, n * LANES:(n + 1) * LANES].reshape(per, 16, LANES)

    def unpack(w, out):
        parts = [obuf[w, n * per:(n + 1) * per].astype(F32).reshape(C, LANES) for n in range(tiles)]
        wide = jnp.concatenate(parts, axis=1)
        for n in range(9):
            out[n // 3, n % 3] = wide[:, n * C:(n + 1) * C]

    class Sum:
        def __init__(self, w, out):
            self.out, self.at, self.over = out, 0, False
            self.w, self.lo, self.length, self.done = w, 0, blocks, []
            self.used = [0, 0]
            self.sem = 0

        def members(self, bits):
            mine = []
            for axis, s in bits:
                mine.append(lax.rem((t if axis == "tile" else f) // s, 2))
            found = []
            for k in reversed(range(1, 2 ** len(bits))):
                tile, face, digit = t, f, 0
                for pos, (axis, s) in enumerate(bits):
                    bit = mine[pos]
                    if (k >> pos) & 1:
                        if axis == "tile":
                            tile = tile + (1 - 2 * bit) * s
                        else:
                            face = face + (1 - 2 * bit) * s
                        bit = 1 - bit
                    digit = digit + bit * (1 << pos)
                found.append((digit, where_to(tile, face)))
            own = 0
            for pos, bit in enumerate(mine):
                own = own + bit * (1 << pos)
            return own, found

        def begin(self, n):
            bits, full, whole = groups[n]
            own, found = self.members(bits)
            w = self.w
            inbox = rfull if full else rlow
            at = self.used[full]
            part = self.length if whole else self.length // (len(found) + 1)
            self.flying = (inbox, at, part, len(found), whole)
            if whole:
                piece = pl.ds(self.lo, part)
                mine = pl.ds(at + own * part, part)
                sbuf[w, piece] = acc[w, piece].astype(BF16)
                for digit, dev in found:
                    remote(sbuf.at[w, piece], inbox.at[w, mine], w_s.at[w], w_r.at[w, self.sem], dev).start()
                inbox[w, mine] = sbuf[w, piece]
                self.used[full] += part * (len(found) + 1)
                return
            for digit, dev in found:
                give = self.lo + digit * part
                if full:
                    out = acc.at[w, pl.ds(give, part)]
                else:
                    sbuf[w, pl.ds(give, part)] = acc[w, pl.ds(give, part)].astype(BF16)
                    out = sbuf.at[w, pl.ds(give, part)]
                at = self.used[full]
                self.used[full] += part
                remote(out, inbox.at[w, at:at + part], w_s.at[w], w_r.at[w, self.sem], dev).start()
            keep = self.lo + own * part
            self.done.append((keep, part, found))
            self.lo, self.length = keep, part

        def end(self):
            inbox, at, part, count, whole = self.flying
            sent = inbox.at[self.w, at:at + count * part]
            settle(sent, w_s.at[self.w])
            settle(sent, w_r.at[self.w, self.sem])
            self.sem += 1
            terms = [inbox[self.w, at + n * part:at + (n + 1) * part].astype(F32) for n in range(count + whole)]
            total = terms.pop(0) if whole else acc[self.w, pl.ds(self.lo, self.length)]
            for term in terms:
                total = total + term
            acc[self.w, pl.ds(self.lo, self.length)] = total

        def round(self):
            obuf[self.w, pl.ds(self.lo, self.length)] = acc[self.w, pl.ds(self.lo, self.length)].astype(BF16)

        def give(self):
            keep, part, found = self.done.pop()
            self.flying = (part, len(found))
            for digit, dev in found:
                remote(obuf.at[self.w, pl.ds(keep, part)], obuf.at[self.w, pl.ds(keep, part)],
                       w_s.at[self.w], w_r.at[self.w, self.sem], dev).start()

        def given(self):
            part, count = self.flying
            whole = obuf.at[self.w, 0:count * part]
            settle(whole, w_s.at[self.w])
            settle(whole, w_r.at[self.w, self.sem])
            self.sem += 1

        def advance(self):
            at, count = self.at, len(groups)
            self.at += 1
            if self.over:
                return
            if at < count:
                if at > 0:
                    self.end()
                self.begin(at)
                return
            if at == count:
                self.end()
                self.round()
            else:
                self.given()
            if self.done:
                self.give()
            else:
                unpack(self.w, self.out)
                self.over = True

    barrier = pltpu.get_barrier_semaphore()
    loads = [pltpu.make_async_copy(src, dst, sem) for src, dst, sem in (
        (fields_h, raw.at[0], w_s.at[0]), (upstream_h, raw.at[1], w_s.at[1]),
        (k1_h, k1, line_s.at[0]), (k2_h, k2, line_s.at[1]))]
    for load in loads:
        load.start()

    @pl.loop(0, n_f)
    def _(df):
        @pl.loop(0, n_t)
        def _(dt):
            @pl.when(jnp.logical_or(df != f, dt != t))
            def _():
                pl.semaphore_signal(barrier, inc=1, device_id=where_to(dt, df), device_id_type=MESH)
    hidden, pre_grad = y.at[0], y.at[1]
    al[...] = jnp.zeros_like(al)
    tl[...] = jnp.zeros_like(tl)
    dl[...] = jnp.zeros_like(dl)
    for kind in range(2):
        loads[kind].wait()
        for q in range(G):
            for j in range(J):
                x[kind, q, j] = raw[kind, :, q, j, :].astype(F32).T.astype(BF16)
        stage(0, kind, x)
    if blocks > tiles * per:
        for w in range(2):
            acc[w, tiles * per:blocks] = jnp.zeros((blocks - tiles * per, 16, LANES), F32)
    pl.semaphore_wait(barrier, n_t * n_f - 1)

    loads[2].wait()
    loads[3].wait()
    start_far(0, x)
    start_near(0, x)
    lay_out(k1, 0)
    lay_out(k2, 1)
    for a in range(3):
        for side in range(2):
            n = 3 * a + 2 * side
            kl[side, a * W:(a + 1) * W] = kf[0, n * W:(n + 1) * W]
    lm[...] = jnp.zeros_like(lm)
    for taps in (xf1, xf2, xc):
        taps[...] = jnp.zeros_like(taps)
    own_forward(x.at[0], kf.at[0], xf1, pre)
    own_backward(x.at[1], kb.at[1], xb, back)
    await_arrivals(0, x)
    more_forward(0, kf.at[0], xf1, pre)
    more_backward(0, kb.at[1], xb, back)
    await_seam(0)
    forward_late(0, xf1, kf.at[0], pre)
    backward_late(0, xb, kb.at[1], back)
    value, slope = gelu_parts(pre[...])
    cells = value.astype(BF16)
    unflat(cells, hidden)
    one, two = Sum(0, w1_o), Sum(1, w2_o)
    wide = product(cells, xc[...], 0, 0)
    pack([wide[:, n * W:n * W + C] * scale for n in range(9)], 1)
    two.advance()
    cot = (back[...] * slope).astype(BF16)
    unflat(cot, pre_grad)
    pack([product(xf1[:, n * W:n * W + C], cot, 0, 0) * scale for n in range(9)], 0)
    one.advance()
    two.advance()
    one.advance()
    await_sends(0, x)
    stage(1, 0, y)
    stage(1, 1, y)
    two.advance()
    start_far(1, y)
    one.advance()
    start_near(1, y)
    two.advance()
    one.advance()
    await_arrivals(1, y)
    await_seam(1)
    forward_taps(1, hidden, xf2, False)
    channel_major(apply(xf2, kf.at[1]), res_o)
    backward_taps(1, pre_grad, xb, False)
    channel_major(apply(xc, kb.at[0]), fg_o)
    while not (one.over and two.over):
        two.advance()
        one.advance()
    await_sends(1, y)


def deliver(*refs):
    sources, targets, sems = refs[0:4], refs[4:8], refs[8]
    moves = [pltpu.make_async_copy(a, b, sems.at[n]) for n, (a, b) in enumerate(zip(sources, targets))]
    for move in moves:
        move.start()
    for move in moves:
        move.wait()


def plan(n_t, n_f):
    tile_bits = [("tile", 1 << i) for i in range(n_t.bit_length() - 1)]
    face_bits = [("face", 1 << i) for i in range(n_f.bit_length() - 1)]
    groups = [(tile_bits[:1], 0, 0)]
    middle, rest = face_bits + tile_bits[1:3], tile_bits[3:]
    while middle:
        groups.append((middle[:3], 0, 0))
        middle = middle[3:]
    while len(rest) > 2:
        groups.append((rest[:2], 0, 0))
        rest = rest[2:]
    if rest:
        groups.append((rest, 0, 1))
    return groups


def run(fields, upstream, k1, k2, n_t, n_f):
    C, G, J, H = fields.shape
    S = H // 3
    E = J + 2
    M = G * J * H
    W = -(-C // LANES) * LANES
    scale = 1.0 / (S * 12.0 ** 0.5)
    groups = plan(n_t, n_f)
    cuts, stages = 1, 0
    for bits, full, whole in groups:
        cuts *= 1 if whole else 2 ** len(bits)
        stages += 1 if whole else 2
    blocks = -(-9 * C // LANES) * (C // 16)
    blocks = -(-blocks // cuts) * cuts
    length, room = blocks, [1, 1]
    for bits, full, whole in groups:
        members = 2 ** len(bits)
        if whole:
            room[full] += length * members
        else:
            length //= members
            room[full] += length * (members - 1)
    dma = pltpu.SemaphoreType.DMA
    vmem = pl.BlockSpec(memory_space=pltpu.VMEM)
    hbm = pl.BlockSpec(memory_space=pltpu.HBM)
    held = [pltpu.with_memory_space_constraint(a, pltpu.HBM) for a in (fields, upstream, k1, k2)]
    return pl.pallas_call(
        functools.partial(body, n_t, n_f, scale, groups),
        out_shape=(
            jax.ShapeDtypeStruct((C, G, J, H), BF16),
            jax.ShapeDtypeStruct((C, G, J, H), BF16),
            jax.ShapeDtypeStruct((3, 3, C, C), F32),
            jax.ShapeDtypeStruct((3, 3, C, C), F32),
        ),
        in_specs=[hbm] * 4,
        out_specs=[vmem] * 4,
        scratch_shapes=[
            pltpu.VMEM((2, C, G, J, H), BF16),
            pltpu.VMEM((2, G, J, H, C), BF16),
            pltpu.VMEM(k1.shape, BF16),
            pltpu.VMEM(k2.shape, BF16),
            pltpu.VMEM((2, G, J, H, C), BF16),
            pltpu.VMEM((2, 2, 2, G, J, C), F32),
            pltpu.VMEM((2, 2, G, H, C), BF16),
            pltpu.VMEM((2, 2, G, H, C), BF16),
            pltpu.VMEM((2, 2, G, E, C), F32),
            pltpu.VMEM((2, 2, G, E, C), F32),
            pltpu.VMEM((2, n_t, 2, G, E, C), F32),
            pltpu.VMEM((2, n_t, 2, G, J, C), F32),
            pltpu.VMEM((2, n_t, 2, G, J, C), F32),
            pltpu.VMEM((2, G, S + 16, C), F32),
            pltpu.VMEM((2, G, S + 16, C), F32),
            pltpu.VMEM((2, G, S + 32, C), F32),
            pltpu.VMEM((G, J + 2, H + 16, C), F32),
            pltpu.VMEM((9, M, C), F32),
            pltpu.VMEM((M, 9 * W), BF16),
            pltpu.VMEM((M, 9 * W), BF16),
            pltpu.VMEM((M, 9 * W), BF16),
            pltpu.VMEM((2, 9 * W, C), BF16),
            pltpu.VMEM((2, 9 * W, C), BF16),
            pltpu.VMEM((2, 3 * W, C), BF16),
            pltpu.VMEM((4, -(-G * J // 16) * 16, 3 * W), F32),
            pltpu.VMEM((G, J + 2, H + 16, C), F32),
            pltpu.VMEM((M, C), F32),
            pltpu.VMEM((M, C), F32),
            pltpu.VMEM((2, blocks, 16, LANES), F32),
            pltpu.VMEM((2, blocks, 16, LANES), BF16),
            pltpu.VMEM((2, room[0], 16, LANES), BF16),
            pltpu.VMEM((2, room[1], 16, LANES), F32),
            pltpu.VMEM((2, blocks, 16, LANES), BF16),
            dma((2,)), dma((2, 2)),
            dma((2,)), dma((2,)), dma((2,)),
            dma((1,)), dma((1,)), dma((2, 2)),
            dma((2,)), dma((2, stages)),
        ],
        compiler_params=pltpu.CompilerParams(
            collective_id=0, has_side_effects=True, vmem_limit_bytes=24 * 1024 * 1024),
    )(*held)


def send_out(made):
    vmem = pl.BlockSpec(memory_space=pltpu.VMEM)
    hbm = pl.BlockSpec(memory_space=pltpu.HBM)
    return pl.pallas_call(
        deliver,
        out_shape=[jax.ShapeDtypeStruct(a.shape, a.dtype) for a in made],
        in_specs=[vmem] * 4,
        out_specs=[hbm] * 4,
        scratch_shapes=[pltpu.SemaphoreType.DMA((4,))],
    )(*[pltpu.with_memory_space_constraint(a, pltpu.VMEM) for a in made])


def on_device(n_sub, n_t, n_f, fields, upstream, k1, k2):
    own = fields.shape[0]
    if n_sub > 1:
        fields = lax.all_gather(fields, "sub", axis=0, tiled=True)
        upstream = lax.all_gather(upstream, "sub", axis=0, tiled=True)
    made = run(fields, upstream, k1, k2, n_t, n_f)
    if n_sub > 1:
        at = lax.axis_index("sub") * own
        res, fgrad, w1, w2 = made
        return (
            lax.dynamic_slice_in_dim(res, at, own, 0),
            lax.dynamic_slice_in_dim(fgrad, at, own, 0),
            lax.dynamic_slice_in_dim(w1, at, own, 3),
            lax.dynamic_slice_in_dim(w2, at, own, 3),
        )
    return tuple(send_out(made))


def solution(mesh):
    placed = (P("sub", "face", "tile", "parts"), P("sub", "face", "tile", "parts"), P(), P())
    sizes = mesh.shape
    return jax.shard_map(
        functools.partial(on_device, sizes["sub"], sizes["tile"], sizes["face"]),
        mesh=mesh,
        in_specs=placed,
        out_specs=(
            P("sub", "face", "tile", "parts"),
            P("sub", "face", "tile", "parts"),
            P("parts", None, None, "sub"),
            P("parts", None, None, "sub"),
        ),
        check_vma=False,
    )
```
